32 devices in a mesh: gy: 4 (over x, core), gx: 8 (over z, y).
Axes of the slice: x: 2, y: 2, z: 4, core: 2. Of those that a mesh axis runs over, the one named last changes fastest.
Arguments:
- sky: bfloat16 [48, 256, 1024], P(None, 'gy', 'gx'), may hold values from -6 to 6
- lens_phi: bfloat16 [256, 1024], P('gy', 'gx'), may hold values from -6 to 6
- cotangent: bfloat16 [48, 256, 1024], P(None, 'gy', 'gx'), may hold values from -6 to 6
- tile_mask: int32 [32, 128], P('gy', 'gx'), may hold values 0 or 1
- weight_one: bfloat16 [3, 3, 48, 48], replicated, may hold values from -0.3125 to 0.3125
- weight_two: bfloat16 [3, 3, 48, 48], replicated, may hold values from -0.3125 to 0.3125
- cond_one: float32 [48], replicated, may hold values from -3 to 3
- bias_one: float32 [48], replicated, may hold values from -3 to 3
- cond_two: float32 [48], replicated, may hold values from -3 to 3
Outputs:
- delensed: bfloat16 [48, 256, 1024], P(None, 'gy', 'gx')
- grad_input: bfloat16 [48, 256, 1024], P(None, 'gy', 'gx')
- grad_w1: float32 [3, 3, 48, 48], replicated
- grad_w2: float32 [3, 3, 48, 48], replicated
- grad_cond: float32 [3, 48], replicated
The draws below stay inside these ranges and needn't reach their ends.
All inputs are finite; a program needn't handle non-finite values. No bound on the sum of `tile_mask` on one device may be relied on, other than what follows from the above.
Results may differ from the reference program's by a relative error of at most 0.0035.
Values may be sent and summed in bfloat16 or wider, within the bound.
No kernel may reach another device: no remote copies, remote signals or barrier semaphores. Data moves between devices by JAX's collectives and lax.ppermute only.
A program may use at most 64 MiB of HBM per device.

```python
import jax
import jax.numpy as jnp
from jax import lax

C = 48
TILE = 8
TY = 32
TX = 128
NY = 256
NX = 1024


def plant(values, rng, low, top_value):
    place = [jax.random.randint(jax.random.fold_in(rng, axis), (), 0, length) for axis, length in enumerate(values.shape)]
    main_axis = values.shape.index(max(values.shape))
    beside = place[:main_axis] + [(place[main_axis] + 1) % values.shape[main_axis]] + place[main_axis + 1:]
    return values.at[tuple(place)].set(low).at[tuple(beside)].set(top_value)


def steps_of(key, dims, shards, smallest, top_value):
    gain = 1.0
    for axis_at, blocks in shards:
        steps = jax.random.uniform(jax.random.fold_in(jax.random.fold_in(key, 6), axis_at), (blocks,), jnp.float32, smallest / len(shards), top_value / len(shards))
        gain = gain * jnp.repeat(jnp.exp(steps), dims[axis_at] // blocks).reshape((-1,) + (1,) * (len(dims) - 1 - axis_at))
    return gain


def scatter_about(own_key, dims, width, reach, cuts=(), held_as=jnp.bfloat16):
    result = width * jax.random.normal(own_key, dims, jnp.float32)
    if cuts:
        result = result * steps_of(own_key, dims, cuts, -0.22, 0.18)
    return jnp.clip(result, -reach, reach).astype(held_as)


def setup_inputs(seed: int = 0) -> dict:
    key_of = jax.random.split(jax.random.key(seed), 10)
    sky = scatter_about(key_of[0], (C, NY, NX), 1.0, 6.0, ((1, 4), (2, 8)))
    lens_phi = scatter_about(key_of[1], (NY, NX), 1.0, 6.0, ((0, 4), (1, 8)))
    cotangent = scatter_about(key_of[2], (C, NY, NX), 1.0, 6.0, ((1, 4), (2, 8)))
    tile_mask = plant((jax.random.randint(key_of[3], (TY, TX), 0, 5) < 2).astype(jnp.int32), jax.random.fold_in(key_of[3], 1), 0, 1)
    weight_one = scatter_about(key_of[4], (3, 3, C, C), (9 * C) ** -0.5, 0.3125)
    weight_two = scatter_about(key_of[5], (3, 3, C, C), (9 * C) ** -0.5, 0.3125)
    cond_one = scatter_about(key_of[6], (C,), 0.5, 3.0, (), jnp.float32)
    bias_one = scatter_about(key_of[7], (C,), 0.5, 3.0, (), jnp.float32)
    cond_two = scatter_about(key_of[8], (C,), 0.5, 3.0, (), jnp.float32)
    return {"sky": sky, "lens_phi": lens_phi, "cotangent": cotangent, "tile_mask": tile_mask, "weight_one": weight_one, "weight_two": weight_two, "cond_one": cond_one, "bias_one": bias_one, "cond_two": cond_two}


def pad_field(field):
    return jnp.pad(field, ((0, 0), (1, 1), (1, 1)))

def tap_forward(weight_tap, piece):
    chans, rows, cols = piece.shape
    flat = piece.astype(jnp.float32).reshape(chans, rows * cols)
    return jnp.dot(weight_tap.astype(jnp.float32), flat, precision=lax.Precision.HIGHEST).reshape(weight_tap.shape[0], rows, cols)

def forward_conv(weight, padded):
    rows = padded.shape[1] - 2
    cols = padded.shape[2] - 2
    total = jnp.zeros((weight.shape[2], rows, cols), jnp.float32)
    for ky in range(3):
        for kx in range(3):
            total = total + tap_forward(weight[ky, kx], padded[:, ky:ky + rows, kx:kx + cols])
    return total

def back_conv(weight, padded):
    rows = padded.shape[1] - 2
    cols = padded.shape[2] - 2
    total = jnp.zeros((weight.shape[3], rows, cols), jnp.float32)
    for ky in range(3):
        for kx in range(3):
            total = total + tap_forward(weight[ky, kx].T, padded[:, 2 - ky:2 - ky + rows, 2 - kx:2 - kx + cols])
    return total

def weight_grad(grad, padded):
    rows = grad.shape[1]
    cols = grad.shape[2]
    left = grad.astype(jnp.float32).reshape(grad.shape[0], rows * cols)
    taps = []
    for ky in range(3):
        for kx in range(3):
            right = padded[:, ky:ky + rows, kx:kx + cols].astype(jnp.float32).reshape(padded.shape[0], rows * cols)
            taps.append(lax.dot_general(left, right, (((1,), (1,)), ((), ())), precision=lax.Precision.HIGHEST))
    return jnp.stack(taps).reshape(3, 3, grad.shape[0], padded.shape[0])

def reference(sky, lens_phi, cotangent, tile_mask, weight_one, weight_two, cond_one, bias_one, cond_two):
    cell_mask = jnp.repeat(jnp.repeat(tile_mask, TILE, axis=0), TILE, axis=1)
    mask_low = cell_mask.astype(jnp.bfloat16)
    mask_full = cell_mask.astype(jnp.float32)
    phi_full = lens_phi.astype(jnp.float32)
    masked_in = sky * mask_low
    padded_in = pad_field(masked_in)
    pre_one = forward_conv(weight_one, padded_in) + cond_one[:, None, None] * phi_full + bias_one[:, None, None]
    hidden = (jax.nn.silu(pre_one) * mask_full).astype(jnp.bfloat16)
    padded_hidden = pad_field(hidden)
    delensed = ((masked_in.astype(jnp.float32) + forward_conv(weight_two, padded_hidden) + cond_two[:, None, None] * phi_full) * mask_full).astype(jnp.bfloat16)
    grad_out = cotangent * mask_low
    grad_hidden = back_conv(weight_two, pad_field(grad_out)) * mask_full
    sigma = jax.nn.sigmoid(pre_one)
    grad_pre = (grad_hidden * sigma * (1.0 + pre_one * (1.0 - sigma))).astype(jnp.bfloat16)
    grad_input = ((grad_out.astype(jnp.float32) + back_conv(weight_one, pad_field(grad_pre))) * mask_full).astype(jnp.bfloat16)
    factor = 1.0 / jnp.sqrt(jnp.float32(NY * NX))
    grad_w1 = weight_grad(grad_pre, padded_in) * factor
    grad_w2 = weight_grad(grad_out, padded_hidden) * factor
    pre_full = grad_pre.astype(jnp.float32)
    out_full = grad_out.astype(jnp.float32)
    grad_cond = jnp.stack([lax.optimization_barrier(jnp.sum(pre_full * phi_full, axis=(1, 2))), lax.optimization_barrier(jnp.sum(pre_full, axis=(1, 2))), lax.optimization_barrier(jnp.sum(out_full * phi_full, axis=(1, 2)))]) * factor
    return (delensed, grad_input, grad_w1, grad_w2, grad_cond)
```

```python
import jax
import jax.numpy as jnp
from jax import lax
from jax.experimental import pallas as pl
from jax.experimental.pallas import tpu as pltpu
from jax.sharding import PartitionSpec as P

TILE = 8
BF = jnp.bfloat16
F32 = jnp.float32
NT = (((1,), (1,)), ((), ()))
NN = (((1,), (0,)), ((), ()))
R1 = 3
R2 = 4


def lane_iota(rows):
    return lax.broadcasted_iota(jnp.int32, (rows, 128), 1)


def tile_rows(mask_ref):
    tcols = mask_ref.shape[1]
    lane = lax.broadcasted_iota(jnp.int32, (tcols, 128), 1)
    row = lax.broadcasted_iota(jnp.int32, (tcols, 128), 0)
    spread = (lane // TILE == row).astype(F32).astype(BF)
    return lax.dot_general(
        mask_ref[...].astype(F32).astype(BF), spread, NN, preferred_element_type=F32
    )


def row_kernel(sky_top, sky_bot, cot_top, cot_bot, phi_ref, mask_ref, up_ref, down_ref):
    chans = sky_top.shape[0]
    cells = tile_rows(mask_ref)
    for out, sky, cot, first, mrow, prow in (
        (up_ref, sky_top, cot_top, 0, 0, 0),
        (down_ref, sky_bot, cot_bot, 14, mask_ref.shape[0] - 1, phi_ref.shape[0] - 1),
    ):
        keep = cells[mrow : mrow + 1]
        low = jnp.broadcast_to(keep, (chans, 128)).astype(BF)
        for base, src in ((0, sky), (2 * chans, cot)):
            block = jnp.transpose(src[...], (1, 0, 2))
            for k in range(2):
                out[base + k * chans : base + (k + 1) * chans] = block[first + k] * low
        row = lax.broadcasted_iota(jnp.int32, (16, 128), 0)
        prow_v = jnp.broadcast_to(phi_ref[prow : prow + 1].astype(F32), (16, 128))
        extra = jnp.where(row == 0, prow_v, jnp.where(row == 1, keep, 0.0))
        out[4 * chans : 4 * chans + 16] = extra.astype(BF)


def col_kernel(sky_ref, cot_ref, phi_ref, mask_ref, top_ref, bot_ref, left_ref, right_ref, strip):
    chans, rows, width = sky_ref.shape
    half = chans // 2
    lane8 = lane_iota(8)
    row8 = lax.broadcasted_iota(jnp.int32, (8, 128), 0)
    pick = ((row8 < 2) & (lane8 == row8)) | (
        (row8 >= 2) & (row8 < 4) & (lane8 == row8 + (width - 4))
    )
    pick = pick.astype(F32).astype(BF)
    trows, tcols = mask_ref.shape
    prow = lax.broadcasted_iota(jnp.int32, (8, tcols), 0)
    pcol = lax.broadcasted_iota(jnp.int32, (8, tcols), 1)
    pick_t = ((prow < 2) & (pcol == 0)) | ((prow >= 2) & (prow < 4) & (pcol == tcols - 1))
    edge = lax.dot_general(
        pick_t.astype(F32).astype(BF),
        mask_ref[...].astype(F32).astype(BF),
        NT,
        preferred_element_type=F32,
    )
    lane_t = lax.broadcasted_iota(jnp.int32, (trows, 128), 1)
    row_t = lax.broadcasted_iota(jnp.int32, (trows, 128), 0)
    spread = (lane_t // TILE == row_t).astype(F32).astype(BF)
    keep = lax.dot_general(edge.astype(BF), spread, NN, preferred_element_type=F32)
    phis = lax.dot_general(pick, phi_ref[...], NT, preferred_element_type=F32)
    phis = jnp.concatenate([phis, jnp.zeros((8, 128 - rows), F32)], axis=1)
    lane = lane_iota(chans)
    for which, src in ((0, sky_ref), (1, cot_ref)):
        both = jnp.concatenate([src[:half], src[half:]], axis=1).reshape(half * 128, width)
        flat = lax.dot_general(pick, both, NT, preferred_element_type=F32)
        for j in range(half):
            strip[8 * j : 8 * j + 8] = flat[:, 128 * j : 128 * j + 128]
        for k in range(4):
            part = strip[pl.ds(k, half, stride=8), :]
            col = jnp.concatenate([part, pltpu.roll(part, 64, 1)], axis=0)
            col = (col * keep[k : k + 1]).astype(BF)
            at = (0, 1, width - 2, width - 1)[k]
            for ref, where in ((top_ref, (126, 127)), (bot_ref, (rows, rows + 1))):
                for n in range(2):
                    base = (2 * which + n) * chans
                    cell = ref[base : base + chans][:, at : at + 1]
                    col = jnp.where(lane == where[n], jnp.broadcast_to(cell, col.shape), col)
            out = (left_ref, right_ref)[k // 2]
            base = (2 * which + k % 2) * chans
            out[base : base + chans] = col
    row = lax.broadcasted_iota(jnp.int32, (16, 128), 0)
    lane16 = lane_iota(16)
    tops = top_ref[4 * chans : 4 * chans + 16].astype(F32)
    bots = bot_ref[4 * chans : 4 * chans + 16].astype(F32)
    for out, k, at in ((left_ref, 0, 0), (right_ref, 3, width - 1)):
        extra = jnp.where(
            row == 0,
            jnp.broadcast_to(phis[k : k + 1], (16, 128)),
            jnp.where(row == 1, jnp.broadcast_to(keep[k : k + 1], (16, 128)), 0.0),
        )
        extra = jnp.where(lane16 == 127, jnp.broadcast_to(tops[:, at : at + 1], (16, 128)), extra)
        extra = jnp.where(lane16 == rows, jnp.broadcast_to(bots[:, at : at + 1], (16, 128)), extra)
        out[4 * chans : 4 * chans + 16] = extra.astype(BF)


def silu_parts(pre):
    sigma = 1.0 / (1.0 + jnp.exp(-pre))
    return pre * sigma, sigma * (1.0 + pre * (1.0 - sigma))


def fill_sides(dst, y, base, step, chans, left_col, right_col, lane):
    at = y % 128
    centre = dst[base + chans : base + 2 * chans]
    left = jnp.where(
        lane == 0,
        jnp.broadcast_to(left_col[:, at : at + 1], centre.shape),
        pltpu.roll(centre, 1, 1),
    )
    right = jnp.where(
        lane == 127,
        jnp.broadcast_to(right_col[:, at : at + 1], centre.shape),
        pltpu.roll(centre, 127, 1),
    )
    dst[base : base + chans] = left
    dst[base + 2 * chans : base + 3 * chans] = right


def main_kernel(
    sky_ref, cot_ref, phi_ref, mask_ref, top_ref, bot_ref, lft_ref, rgt_ref, mylft_ref, myrgt_ref,
    w1c_ref, w2tc_ref, w1s_ref, w2ts_ref, w2s_ref, w1ts_ref, cond_ref,
    delens_ref, gin_ref, wire_ref,
    a3x, a3g, a3h, a3d, dz, gz, phix, maskx, outd, outg, acc1, acc2, cacc,
):
    chans, rows, width = sky_ref.shape
    step = 3 * chans
    lane = lane_iota(chans)
    trows = mask_ref.shape[0]
    zero = jnp.zeros((chans, 128), BF)

    cells = tile_rows(mask_ref)
    phix[0:1] = top_ref[4 * chans : 4 * chans + 16].astype(F32)[0:1]
    phix[rows + 1 : rows + 2] = bot_ref[4 * chans : 4 * chans + 16].astype(F32)[0:1]
    phix[1 : rows + 1] = phi_ref[...].astype(F32)
    maskx[0:1] = top_ref[4 * chans : 4 * chans + 16].astype(F32)[1:2]
    maskx[rows + 1 : rows + 2] = bot_ref[4 * chans : 4 * chans + 16].astype(F32)[1:2]
    for t in range(trows):
        maskx[1 + TILE * t : 1 + TILE * (t + 1)] = jnp.broadcast_to(cells[t : t + 1], (TILE, 128))

    gphi = jnp.zeros((chans, 128), F32)
    for which, src, dst in ((0, sky_ref, a3x), (1, cot_ref, a3g)):
        for j in range(rows // 16):
            block = jnp.transpose(src[:, 16 * j : 16 * j + 16, :], (1, 0, 2))
            for t in range(2):
                low = jnp.broadcast_to(cells[2 * j + t : 2 * j + t + 1], (chans, 128)).astype(BF)
                for n in range(TILE):
                    y = 16 * j + TILE * t + n
                    value = block[TILE * t + n] * low
                    dst[(y + 2) * step + chans : (y + 2) * step + 2 * chans] = value
                    if which:
                        gz[(y + 2) * chans : (y + 3) * chans] = value
                        gphi = gphi + value.astype(F32) * phix[y + 1 : y + 2]
        for ref, first in ((top_ref, -2), (bot_ref, rows)):
            for n in range(2):
                base = (first + n + 2) * step + chans
                dst[base : base + chans] = ref[(2 * which + n) * chans : (2 * which + n + 1) * chans]
        left_col = lft_ref[(2 * which + 1) * chans : (2 * which + 2) * chans]
        right_col = rgt_ref[2 * which * chans : (2 * which + 1) * chans]
        for y in range(-2, rows + 2):
            fill_sides(dst, y, (y + 2) * step, step, chans, left_col, right_col, lane)
    for z in (dz, gz):
        for y in (-2, -1, rows, rows + 1):
            z[(y + 2) * chans : (y + 3) * chans] = zero
    cacc[2] = gphi

    gain = cond_ref[:, 0:1]
    bias = cond_ref[:, 1:2]
    gain_two = cond_ref[:, 2:3]

    def ring(weights, which):
        base = 2 * which * chans
        pieces = []
        cols = (
            (lft_ref[base : base + chans], lft_ref[base + chans : base + 2 * chans],
             mylft_ref[base : base + chans]),
            (myrgt_ref[base + chans : base + 2 * chans], rgt_ref[base : base + chans],
             rgt_ref[base + chans : base + 2 * chans]),
        )
        for ky in range(3):
            for kx in range(3):
                pair = [
                    side[kx] if ky == 1 else pltpu.roll(side[kx], (1, 0, 127)[ky], 1)
                    for side in cols
                ]
                pieces.append(jnp.concatenate(pair, axis=1))
        return lax.dot_general(
            weights, jnp.concatenate(pieces, axis=0), NN, preferred_element_type=F32
        )

    extra_l = lft_ref[4 * chans : 4 * chans + 16].astype(F32)
    extra_r = rgt_ref[4 * chans : 4 * chans + 16].astype(F32)
    phi_c = jnp.concatenate([extra_l[0:1], extra_r[0:1]], axis=1)
    mask_c = jnp.concatenate([extra_l[1:2], extra_r[1:2]], axis=1)
    pre_c = ring(w1c_ref[...], 0) + gain * phi_c + bias
    act_c, slope_c = silu_parts(pre_c)
    hid_c = (act_c * mask_c).astype(BF)
    dpre_c = (ring(w2tc_ref[...], 1) * mask_c * slope_c).astype(BF)

    split = (rows + 2) // 2
    sums = (jnp.zeros((chans, 128), F32), jnp.zeros((chans, 128), F32))

    def first_pass(it, carry):
        y0 = R1 * it - 1
        win = (R1 + 2) * step

        def both(src):
            a = pl.multiple_of((y0 + 1) * step, 16)
            b = pl.multiple_of((y0 + split + 1) * step, 16)
            return jnp.concatenate([src[pl.ds(a, win), :], src[pl.ds(b, win), :]], axis=1)

        pre = lax.dot_general(w1s_ref[...], both(a3x), NN, preferred_element_type=F32)
        back = lax.dot_general(w2ts_ref[...], both(a3g), NN, preferred_element_type=F32)
        for h in range(2):
            for r in range(R1):
                row = y0 + h * split + r + 1
                here = (slice(r * chans, (r + 1) * chans), slice(h * 128, h * 128 + 128))
                keep = maskx[pl.ds(row, 1), :]
                act, slope = silu_parts(pre[here] + gain * phix[pl.ds(row, 1), :] + bias)
                base = pl.multiple_of(row * step + chans, 16)
                a3h[pl.ds(base, chans), :] = (act * keep).astype(BF)
                a3d[pl.ds(base, chans), :] = (back[here] * keep * slope).astype(BF)
        return carry

    lax.fori_loop(0, split // R1, first_pass, 0)

    for dst, col in ((a3h, hid_c), (a3d, dpre_c)):
        for y in range(-1, rows + 1):
            fill_sides(dst, y, (y + 1) * step, step, chans, col[:, :128], col[:, 128:], lane)
    dphi, dsum = sums
    for y in range(rows):
        value = a3d[(y + 1) * step + chans : (y + 1) * step + 2 * chans]
        dz[(y + 2) * chans : (y + 3) * chans] = value
        wide = value.astype(F32)
        dphi = dphi + wide * phix[y + 1 : y + 2]
        dsum = dsum + wide
    cacc[0] = dphi
    cacc[1] = dsum

    acc1[...] = jnp.zeros_like(acc1)
    acc2[...] = jnp.zeros_like(acc2)
    group = 6

    def grads(it, carry):
        for z, field, off, acc in ((dz, a3x, 2, acc1), (gz, a3h, 1, acc2)):
            lhs, rhs = [], []
            for n in range(group):
                r = group * it + n - 1
                lhs.append(z[pl.ds(pl.multiple_of((r + 1) * chans, 16), step), :])
                rhs.append(field[pl.ds(pl.multiple_of((r + off) * step, 16), step), :])
            acc[...] += lax.dot_general(
                jnp.concatenate(lhs, axis=1), jnp.concatenate(rhs, axis=1), NT,
                preferred_element_type=F32,
            )
        return carry

    lax.fori_loop(0, (rows + 2) // group, grads, 0)

    def second_pass(it, carry):
        y0 = R2 * it
        win = (R2 + 2) * step

        def both(src):
            a = pl.multiple_of(y0 * step, 16)
            b = pl.multiple_of((y0 + rows // 2) * step, 16)
            return jnp.concatenate([src[pl.ds(a, win), :], src[pl.ds(b, win), :]], axis=1)

        fwd = lax.dot_general(w2s_ref[...], both(a3h), NN, preferred_element_type=F32)
        bwd = lax.dot_general(w1ts_ref[...], both(a3d), NN, preferred_element_type=F32)
        for h in range(2):
            for r in range(R2):
                y = y0 + h * (rows // 2) + r
                here = (slice(r * chans, (r + 1) * chans), slice(h * 128, h * 128 + 128))
                keep = maskx[pl.ds(y + 1, 1), :]
                base = pl.multiple_of((y + 2) * step + chans, 16)
                x0 = a3x[pl.ds(base, chans), :].astype(F32)
                g0 = a3g[pl.ds(base, chans), :].astype(F32)
                out = (x0 + fwd[here] + gain_two * phix[pl.ds(y + 1, 1), :]) * keep
                outd[y] = out.astype(BF)
                outg[y] = ((g0 + bwd[here]) * keep).astype(BF)
        return carry

    lax.fori_loop(0, rows // (2 * R2), second_pass, 0)
    for j in range(rows // 16):
        delens_ref[:, 16 * j : 16 * j + 16, :] = jnp.transpose(outd[16 * j : 16 * j + 16], (1, 0, 2))
        gin_ref[:, 16 * j : 16 * j + 16, :] = jnp.transpose(outg[16 * j : 16 * j + 16], (1, 0, 2))

    wide = jnp.concatenate([acc1[...], acc2[...]], axis=1)
    wire_ref[0:step] = wide[:, :128]
    wire_ref[step : 2 * step] = wide[:, 128:256]
    rest = wide[:, 256 : 2 * step]
    cond = jnp.concatenate(
        [jnp.sum(cacc[k], axis=1, keepdims=True) for k in range(3)]
        + [jnp.zeros((chans, 128 - 3 * rest.shape[1] - 3), F32)],
        axis=1,
    )
    wire_ref[2 * step : 2 * step + chans] = jnp.concatenate(
        [rest[k * chans : (k + 1) * chans] for k in range(3)] + [cond], axis=1
    )


def unpack_kernel(factor, wire_ref, w1_ref, w2_ref, cond_ref):
    chans = w1_ref.shape[2]
    step = 3 * chans
    tail = wire_ref[2 * step : 2 * step + chans]
    rest_w = 2 * step - 256
    rest = jnp.concatenate([tail[:, k * rest_w : (k + 1) * rest_w] for k in range(3)], axis=0)
    wide = jnp.concatenate([wire_ref[0:step], wire_ref[step : 2 * step], rest], axis=1) * factor
    for ref, base in ((w1_ref, 0), (w2_ref, step)):
        for ky in range(3):
            for kx in range(3):
                ref[ky, kx] = wide[
                    (2 - ky) * chans : (3 - ky) * chans,
                    base + kx * chans : base + (kx + 1) * chans,
                ]
    cond_ref[...] = jnp.transpose(tail * factor)[3 * rest_w : 3 * rest_w + 3, :chans]


def stacked(block, count, chans):
    step = 3 * chans
    return jnp.concatenate(
        [jnp.pad(block, ((0, 0), (r * step, (count - 1 - r) * step))) for r in range(count)], axis=0
    )


def build(mesh):
    ny, nx = mesh.shape["gy"], mesh.shape["gx"]
    axes = ("gy", "gx")

    def links(move):
        pairs = []
        for a in range(ny):
            for b in range(nx):
                to = move(a, b)
                if 0 <= to[0] < ny and 0 <= to[1] < nx:
                    pairs.append((a * nx + b, to[0] * nx + to[1]))
        return pairs

    def send(value, move):
        return lax.ppermute(value, axes, links(move))

    def local(
        sky, lens_phi, cotangent, tile_mask, weight_one, weight_two, cond_one, bias_one, cond_two
    ):
        chans, rows, width = sky.shape
        step = 3 * chans
        edge = jax.ShapeDtypeStruct((4 * chans + 16, 128), BF)
        vmem = pl.BlockSpec(memory_space=pltpu.VMEM)
        first = pl.BlockSpec((chans, 16, width), lambda i: (0, 0, 0))
        last = pl.BlockSpec((chans, 16, width), lambda i: (0, rows // 16 - 1, 0))
        up, down = pl.pallas_call(
            row_kernel,
            grid=(1,),
            out_shape=(edge, edge),
            in_specs=[first, last, first, last, vmem, vmem],
            out_specs=(vmem, vmem),
            name="edge_rows",
        )(sky, sky, cotangent, cotangent, lens_phi, tile_mask)
        bot = send(up, lambda a, b: (a - 1, b))
        top = send(down, lambda a, b: (a + 1, b))

        def taps(weight, back):
            if back:
                return weight[::-1, ::-1].transpose(3, 0, 1, 2).reshape(chans, 3 * step)
            return weight.transpose(2, 0, 1, 3).reshape(chans, 3 * step)

        w1f, w1b = taps(weight_one, False), taps(weight_one, True)
        w2f, w2b = taps(weight_two, False), taps(weight_two, True)
        conds = jnp.stack([cond_one, bias_one, cond_two], axis=1)
        conds = jnp.pad(conds, ((0, 0), (0, 125)))

        to_left, to_right = pl.pallas_call(
            col_kernel,
            out_shape=(edge, edge),
            scratch_shapes=[pltpu.VMEM((8 * chans // 2, 128), F32)],
            name="edge_cols",
        )(sky, cotangent, lens_phi, tile_mask, top, bot)
        rgt = send(to_left, lambda a, b: (a, b - 1))
        lft = send(to_right, lambda a, b: (a, b + 1))

        field = pltpu.VMEM(((rows + 4) * step, 128), BF)
        inner = pltpu.VMEM(((rows + 2) * step, 128), BF)
        centre = pltpu.VMEM(((rows + 4) * chans, 128), BF)
        rowwise = pltpu.VMEM((rows + 8, 128), F32)
        outrow = pltpu.VMEM((rows, chans, 128), BF)
        acc = pltpu.VMEM((step, step), F32)
        maps = jax.ShapeDtypeStruct(sky.shape, BF)
        delensed, grad_input, wire = pl.pallas_call(
            main_kernel,
            out_shape=(maps, maps, jax.ShapeDtypeStruct((2 * step + chans, 128), F32)),
            scratch_shapes=[
                field, field, inner, inner, centre, centre, rowwise, rowwise, outrow, outrow,
                acc, acc, pltpu.VMEM((3, chans, 128), F32),
            ],
            compiler_params=pltpu.CompilerParams(vmem_limit_bytes=40 << 20),
            name="convolutions",
        )(
            sky, cotangent, lens_phi, tile_mask, top, bot, lft, rgt, to_left, to_right,
            w1f, w2b, stacked(w1f, R1, chans), stacked(w2b, R1, chans),
            stacked(w2f, R2, chans), stacked(w1b, R2, chans), conds,
        )

        bit = 1
        while bit < ny:
            wire = wire + send(wire, lambda a, b: (a ^ bit, b))
            bit *= 2
        bit = 1
        while bit < nx:
            wire = wire + send(wire, lambda a, b: (a, b ^ bit))
            bit *= 2

        factor = float(1.0 / (rows * ny * width * nx) ** 0.5)
        grads = jax.ShapeDtypeStruct((3, 3, chans, chans), F32)
        grad_w1, grad_w2, grad_cond = pl.pallas_call(
            lambda *refs: unpack_kernel(factor, *refs),
            out_shape=(grads, grads, jax.ShapeDtypeStruct((3, chans), F32)),
            name="unpack",
        )(wire)
        return delensed, grad_input, grad_w1, grad_w2, grad_cond

    return local


def solution(mesh):
    return jax.shard_map(
        build(mesh),
        mesh=mesh,
        in_specs=(
            P(None, "gy", "gx"),
            P("gy", "gx"),
            P(None, "gy", "gx"),
            P("gy", "gx"),
            P(),
            P(),
            P(),
            P(),
            P(),
        ),
        out_specs=(P(None, "gy", "gx"), P(None, "gy", "gx"), P(), P(), P()),
        check_vma=False,
    )
```

```python
import jax
import jax.numpy as jnp
from jax import lax
from jax.experimental import pallas as pl
from jax.experimental.pallas import tpu as pltpu
from jax.sharding import PartitionSpec as P

TILE = 8
BF = jnp.bfloat16
F32 = jnp.float32
NT = (((1,), (1,)), ((), ()))
NN = (((1,), (0,)), ((), ()))
R1 = 3
R2 = 4
GROUP1 = 6
GROUP2 = 8


def lane_iota(rows):
    return lax.broadcasted_iota(jnp.int32, (rows, 128), 1)


def tile_rows(mask_ref):
    tcols = mask_ref.shape[1]
    lane = lax.broadcasted_iota(jnp.int32, (tcols, 128), 1)
    row = lax.broadcasted_iota(jnp.int32, (tcols, 128), 0)
    spread = (lane // TILE == row).astype(F32).astype(BF)
    return lax.dot_general(
        mask_ref[...].astype(F32).astype(BF), spread, NN, preferred_element_type=F32
    )


def is_odd(axis):
    return lax.rem(lax.axis_index(axis), 2) == 1


def row_kernel(sky_top, sky_bot, cot_top, cot_bot, phi_ref, mask_ref, a_ref, b_ref):
    chans = sky_top.shape[0]
    cells = tile_rows(mask_ref)
    odd = is_odd("gy")
    parts = []
    for sky, cot, first, mrow, prow in (
        (sky_top, cot_top, 0, 0, 0),
        (sky_bot, cot_bot, 14, mask_ref.shape[0] - 1, phi_ref.shape[0] - 1),
    ):
        keep = cells[mrow : mrow + 1]
        low = jnp.broadcast_to(keep, (chans, 128)).astype(BF)
        part = []
        for src in (sky, cot):
            block = jnp.transpose(src[...], (1, 0, 2))
            part += [block[first] * low, block[first + 1] * low]
        row = lax.broadcasted_iota(jnp.int32, (16, 128), 0)
        prow_v = jnp.broadcast_to(phi_ref[prow : prow + 1].astype(F32), (16, 128))
        part.append(jnp.where(row == 0, prow_v, jnp.where(row == 1, keep, 0.0)).astype(BF))
        parts.append(jnp.concatenate(part, axis=0))
    up, down = parts
    a_ref[...] = jnp.where(odd, up, down)
    b_ref[...] = jnp.where(odd, down, up)


def col_kernel(
    sky_ref, cot_ref, phi_ref, mask_ref, a_ref, b_ref,
    sa_ref, sb_ref, own_ref, halo_ref, strip,
):
    chans, rows, width = sky_ref.shape
    size = a_ref.shape[0]
    odd = is_odd("gy")
    ra, rb = a_ref[...], b_ref[...]
    tops_all = jnp.where(odd, ra, rb)
    bots_all = jnp.where(odd, rb, ra)
    halo_ref[0] = tops_all
    halo_ref[1] = bots_all
    half = chans // 2
    lane8 = lane_iota(8)
    row8 = lax.broadcasted_iota(jnp.int32, (8, 128), 0)
    pick = ((row8 < 2) & (lane8 == row8)) | (
        (row8 >= 2) & (row8 < 4) & (lane8 == row8 + (width - 4))
    )
    pick = pick.astype(F32).astype(BF)
    trows, tcols = mask_ref.shape
    prow = lax.broadcasted_iota(jnp.int32, (8, tcols), 0)
    pcol = lax.broadcasted_iota(jnp.int32, (8, tcols), 1)
    pick_t = ((prow < 2) & (pcol == 0)) | ((prow >= 2) & (prow < 4) & (pcol == tcols - 1))
    edge = lax.dot_general(
        pick_t.astype(F32).astype(BF),
        mask_ref[...].astype(F32).astype(BF),
        NT,
        preferred_element_type=F32,
    )
    lane_t = lax.broadcasted_iota(jnp.int32, (trows, 128), 1)
    row_t = lax.broadcasted_iota(jnp.int32, (trows, 128), 0)
    spread = (lane_t // TILE == row_t).astype(F32).astype(BF)
    keep = lax.dot_general(edge.astype(BF), spread, NN, preferred_element_type=F32)
    phis = lax.dot_general(pick, phi_ref[...], NT, preferred_element_type=F32)
    phis = jnp.concatenate([phis, jnp.zeros((8, 128 - rows), F32)], axis=1)
    lane = lane_iota(chans)
    for which, src in ((0, sky_ref), (1, cot_ref)):
        both = jnp.concatenate([src[:half], src[half:]], axis=1).reshape(half * 128, width)
        flat = lax.dot_general(pick, both, NT, preferred_element_type=F32)
        for j in range(half):
            strip[8 * j : 8 * j + 8] = flat[:, 128 * j : 128 * j + 128]
        for k in range(4):
            part = strip[pl.ds(k, half, stride=8), :]
            col = jnp.concatenate([part, pltpu.roll(part, 64, 1)], axis=0)
            col = (col * keep[k : k + 1]).astype(BF)
            at = (0, 1, width - 2, width - 1)[k]
            for value, where in ((tops_all, (126, 127)), (bots_all, (rows, rows + 1))):
                for n in range(2):
                    base = (2 * which + n) * chans
                    cell = value[base : base + chans, at : at + 1]
                    col = jnp.where(lane == where[n], jnp.broadcast_to(cell, col.shape), col)
            base = (2 * which + k % 2) * chans
            own_ref[k // 2, base : base + chans] = col
    row = lax.broadcasted_iota(jnp.int32, (16, 128), 0)
    lane16 = lane_iota(16)
    tops = tops_all[4 * chans : size].astype(F32)
    bots = bots_all[4 * chans : size].astype(F32)
    for side, k, at in ((0, 0, 0), (1, 3, width - 1)):
        extra = jnp.where(
            row == 0,
            jnp.broadcast_to(phis[k : k + 1], (16, 128)),
            jnp.where(row == 1, jnp.broadcast_to(keep[k : k + 1], (16, 128)), 0.0),
        )
        extra = jnp.where(lane16 == 127, jnp.broadcast_to(tops[:, at : at + 1], (16, 128)), extra)
        extra = jnp.where(lane16 == rows, jnp.broadcast_to(bots[:, at : at + 1], (16, 128)), extra)
        own_ref[side, 4 * chans : size] = extra.astype(BF)
    odd_x = is_odd("gx")
    sa_ref[...] = jnp.where(odd_x, own_ref[0], own_ref[1])
    sb_ref[...] = jnp.where(odd_x, own_ref[1], own_ref[0])


def silu_parts(pre):
    sigma = 1.0 / (1.0 + jnp.exp(-pre))
    return pre * sigma, sigma * (1.0 + pre * (1.0 - sigma))


def two_windows(src, first, second, size):
    a = pl.multiple_of(first, 16)
    b = pl.multiple_of(second, 16)
    return jnp.concatenate([src[pl.ds(a, size), :], src[pl.ds(b, size), :]], axis=1)


def hidden_kernel(
    sky_ref, cot_ref, phi_ref, mask_ref, halo_ref, w1s_ref, w2ts_ref, cond_ref,
    hid_ref, dpre_ref, acc1, acc2, cacc,
    a3x, a3g, dz, phix, maskx,
):
    chans, rows, width = sky_ref.shape
    size = halo_ref.shape[1]
    step = 3 * chans
    trows = mask_ref.shape[0]
    cells = tile_rows(mask_ref)
    lane1 = lane_iota(1)
    inside = jnp.where((lane1 == 0) | (lane1 == 127), 0.0, 1.0)
    for k, at in ((0, 0), (1, rows + 1)):
        extra = halo_ref[k, 4 * chans : size].astype(F32)
        phix[at : at + 1] = extra[0:1]
        maskx[at : at + 1] = extra[1:2] * inside
    phix[1 : rows + 1] = phi_ref[...].astype(F32)
    for t in range(trows):
        maskx[1 + TILE * t : 1 + TILE * (t + 1)] = jnp.broadcast_to(
            cells[t : t + 1] * inside, (TILE, 128)
        )

    gphi = jnp.zeros((chans, 128), F32)

    def put(dst, y, value):
        base = (y + 2) * step
        dst[base : base + chans] = pltpu.roll(value, 1, 1)
        dst[base + chans : base + 2 * chans] = value
        dst[base + 2 * chans : base + 3 * chans] = pltpu.roll(value, 127, 1)

    for which, src, dst in ((0, sky_ref, a3x), (1, cot_ref, a3g)):
        for j in range(rows // 16):
            block = jnp.transpose(src[:, 16 * j : 16 * j + 16, :], (1, 0, 2))
            for t in range(2):
                low = jnp.broadcast_to(cells[2 * j + t : 2 * j + t + 1], (chans, 128)).astype(BF)
                for n in range(TILE):
                    y = 16 * j + TILE * t + n
                    value = block[TILE * t + n] * low
                    put(dst, y, value)
                    if which:
                        gphi = gphi + value.astype(F32) * phix[y + 1 : y + 2]
        for k, first in ((0, -2), (1, rows)):
            for n in range(2):
                base = (2 * which + n) * chans
                put(dst, first + n, halo_ref[k, base : base + chans])
    cacc[2] = gphi

    gain = cond_ref[:, 0:1]
    bias = cond_ref[:, 1:2]
    split = (rows + 2) // 2
    zero = jnp.zeros((chans, 128), BF)
    for y in (-2, -1, rows, rows + 1):
        dz[(y + 2) * chans : (y + 3) * chans] = zero

    def first_pass(it, carry):
        y0 = R1 * it - 1
        win = (R1 + 2) * step
        at = ((y0 + 1) * step, (y0 + split + 1) * step)
        pre = lax.dot_general(
            w1s_ref[...], two_windows(a3x, *at, win), NN, preferred_element_type=F32
        )
        back = lax.dot_general(
            w2ts_ref[...], two_windows(a3g, *at, win), NN, preferred_element_type=F32
        )
        for h in range(2):
            for r in range(R1):
                row = y0 + h * split + r + 1
                here = (slice(r * chans, (r + 1) * chans), slice(h * 128, h * 128 + 128))
                keep = maskx[pl.ds(row, 1), :]
                act, slope = silu_parts(pre[here] + gain * phix[pl.ds(row, 1), :] + bias)
                base = pl.multiple_of(row * chans, 16)
                hid_ref[pl.ds(base, chans), :] = (act * keep).astype(BF)
                dpre_ref[pl.ds(base, chans), :] = (back[here] * keep * slope).astype(BF)
        return carry

    lax.fori_loop(0, split // R1, first_pass, 0)

    dphi = jnp.zeros((chans, 128), F32)
    dsum = jnp.zeros((chans, 128), F32)
    for y in range(rows):
        value = dpre_ref[(y + 1) * chans : (y + 2) * chans]
        dz[(y + 2) * chans : (y + 3) * chans] = value
        wide = value.astype(F32)
        dphi = dphi + wide * phix[y + 1 : y + 2]
        dsum = dsum + wide
    cacc[0] = dphi
    cacc[1] = dsum

    acc1[...] = jnp.zeros_like(acc1)
    acc2[...] = jnp.zeros_like(acc2)

    def rows_of(src, start, size):
        return src[pl.ds(pl.multiple_of(start, 16), size), :]

    def grads_one(it, carry):
        ys = [GROUP1 * it + n - 1 for n in range(GROUP1)]
        acc1[...] += lax.dot_general(
            jnp.concatenate([rows_of(dz, (y + 1) * chans, step) for y in ys], axis=1),
            jnp.concatenate([rows_of(a3x, (y + 2) * step, step) for y in ys], axis=1),
            NT, preferred_element_type=F32,
        )
        return carry

    def grads_two(it, carry):
        ys = [GROUP2 * it + n for n in range(GROUP2)]
        acc2[...] += lax.dot_general(
            jnp.concatenate([rows_of(a3g, (y + 2) * step, step) for y in ys], axis=1),
            jnp.concatenate([rows_of(hid_ref, y * chans, step) for y in ys], axis=1),
            NT, preferred_element_type=F32,
        )
        return carry

    lax.fori_loop(0, (rows + 2) // GROUP1, grads_one, 0)
    lax.fori_loop(0, rows // GROUP2, grads_two, 0)


def edge_kernel(
    rows, a_ref, b_ref, own_ref, w1c_ref, w2tc_ref, cond_ref, acc1, acc2, cacc,
    hcol_ref, dcol_ref, keep_ref, give_ref, wire,
):
    size = a_ref.shape[0]
    chans = (size - 16) // 4
    step = 3 * chans
    odd = is_odd("gx")
    ra, rb = a_ref[...], b_ref[...]
    lft = jnp.where(odd, ra, rb)
    rgt = jnp.where(odd, rb, ra)
    own_l, own_r = own_ref[0], own_ref[1]

    def at(value, which, n):
        base = (2 * which + n) * chans
        return value[base : base + chans]

    def columns(which):
        return [at(v, which, n) for v in (lft, own_l, own_r, rgt) for n in range(2)]

    centres = (1, 2, 5, 6)

    def taps_of(cols):
        pieces = []
        for ky in range(3):
            moved = [c if ky == 1 else pltpu.roll(c, (1, 0, 127)[ky], 1) for c in cols]
            for kx in range(3):
                pieces.append(jnp.concatenate([moved[c + kx - 1] for c in centres], axis=1))
        return jnp.concatenate(pieces, axis=0)

    x_taps = taps_of(columns(0))
    g_cols = columns(1)
    extra = [v[4 * chans : size].astype(F32) for v in (lft, own_l, own_r, rgt)]
    phi_c = jnp.concatenate([e[0:1] for e in extra], axis=1)
    mask_c = jnp.concatenate([e[1:2] for e in extra], axis=1)
    pre = lax.dot_general(w1c_ref[...], x_taps, NN, preferred_element_type=F32)
    back = lax.dot_general(w2tc_ref[...], taps_of(g_cols), NN, preferred_element_type=F32)
    act, slope = silu_parts(pre + cond_ref[:, 0:1] * phi_c + cond_ref[:, 1:2])
    hcol = (act * mask_c).astype(BF)
    dcol = (back * mask_c * slope).astype(BF)
    hcol_ref[...] = hcol
    dcol_ref[...] = dcol

    mine = jnp.broadcast_to((lane_iota(1) < rows).astype(F32), (chans, 128)).astype(BF)
    d_own = [dcol[:, 128:256] * mine, dcol[:, 256:384] * mine]
    part1 = lax.dot_general(
        jnp.concatenate(d_own, axis=1), x_taps[:, 128:384], NT, preferred_element_type=F32
    )
    h_cols = [hcol[:, 128 * k : 128 * k + 128] for k in range(4)]
    g_own = {k: g_cols[n] * mine for k, n in ((0, 2), (1, 3), (2, 4), (3, 5))}
    for kx, pairs in (
        (0, ((0, 0), (1, 1))),
        (1, ((0, 1), (3, 2))),
        (2, ((2, 2), (3, 3))),
    ):
        lhs = jnp.concatenate([g_own[g] for g, _ in pairs], axis=1)
        rhs = []
        for ky in range(3):
            moved = [
                h_cols[h] if ky == 1 else pltpu.roll(h_cols[h], (1, 0, 127)[ky], 1)
                for _, h in pairs
            ]
            rhs.append(jnp.concatenate(moved, axis=1))
        part2 = lax.dot_general(
            lhs, jnp.concatenate(rhs, axis=0), NT, preferred_element_type=F32
        )
        low = (2 - kx) * chans
        wide = jnp.concatenate(
            [
                acc1[low : low + chans] + part1[:, kx * step : (kx + 1) * step],
                acc2[low : low + chans] + part2,
            ],
            axis=1,
        )
        wire[low : low + chans] = wide[:, :128]
        wire[step + low : step + low + chans] = wide[:, 128:256]
        if kx == 0:
            tails = []
        tails.insert(0, wide[:, 256 : 2 * step])
    dphi, dsum = cacc[0], cacc[1]
    for d, k in ((d_own[0], 1), (d_own[1], 2)):
        dphi = dphi + d.astype(F32) * extra[k][0:1]
        dsum = dsum + d.astype(F32)
    sums = [jnp.sum(v, axis=1, keepdims=True) for v in (dphi, dsum, cacc[2])]
    fill = jnp.zeros((chans, 128 - 3 * tails[0].shape[1] - 3), F32)
    wire[2 * step : 2 * step + chans] = jnp.concatenate(tails + sums + [fill], axis=1)
    count = wire.shape[0] // 2
    core = lax.rem(lax.axis_index("gy"), 2)
    keep_ref[...] = wire[pl.ds(pl.multiple_of(core * count, 8), count), :]
    give_ref[...] = wire[pl.ds(pl.multiple_of((1 - core) * count, 8), count), :]


def output_kernel(
    with_phi, src_ref, phi_ref, mask_ref, mid_ref, col_ref, weights_ref, cond_ref,
    out_ref, a3, rowbuf, phix,
):
    chans, rows, width = src_ref.shape
    step = 3 * chans
    lane = lane_iota(chans)
    cells = tile_rows(mask_ref)
    cols = [col_ref[:, 128 * k : 128 * k + 128] for k in range(4)]
    if with_phi:
        phix[...] = phi_ref[...].astype(F32)
        gain = cond_ref[:, 2:3]

    def cell(col, y):
        at = y % 128
        return jnp.broadcast_to(col[:, at : at + 1], (chans, 128))

    for y in range(-1, rows + 1):
        centre = mid_ref[(y + 1) * chans : (y + 2) * chans]
        centre = jnp.where(lane == 0, cell(cols[1], y), centre)
        centre = jnp.where(lane == 127, cell(cols[2], y), centre)
        base = (y + 1) * step
        a3[base : base + chans] = jnp.where(
            lane == 0, cell(cols[0], y), pltpu.roll(centre, 1, 1)
        )
        a3[base + chans : base + 2 * chans] = centre
        a3[base + 2 * chans : base + 3 * chans] = jnp.where(
            lane == 127, cell(cols[3], y), pltpu.roll(centre, 127, 1)
        )

    def second_pass(it, carry):
        y0 = R2 * it
        got = lax.dot_general(
            weights_ref[...],
            two_windows(a3, y0 * step, (y0 + rows // 2) * step, (R2 + 2) * step),
            NN, preferred_element_type=F32,
        )
        for h in range(2):
            for r in range(R2):
                y = y0 + h * (rows // 2) + r
                part = got[r * chans : (r + 1) * chans, h * 128 : h * 128 + 128]
                if with_phi:
                    part = part + gain * phix[pl.ds(y, 1), :]
                rowbuf[y] = part
        return carry

    lax.fori_loop(0, rows // (2 * R2), second_pass, 0)
    for j in range(rows // 16):
        block = jnp.transpose(src_ref[:, 16 * j : 16 * j + 16, :], (1, 0, 2))
        done = []
        for n in range(16):
            keep = cells[(16 * j + n) // TILE : (16 * j + n) // TILE + 1]
            done.append(((rowbuf[16 * j + n] + block[n].astype(F32)) * keep).astype(BF))
        out_ref[:, 16 * j : 16 * j + 16, :] = jnp.transpose(jnp.stack(done), (1, 0, 2))


def unpack_kernel(factor, keep_ref, other_ref, w1_ref, w2_ref, cond_ref, wire):
    chans = w1_ref.shape[2]
    step = 3 * chans
    count = keep_ref.shape[0]
    core = lax.rem(lax.axis_index("gy"), 2)
    wire[pl.ds(pl.multiple_of(core * count, 8), count), :] = keep_ref[...]
    wire[pl.ds(pl.multiple_of((1 - core) * count, 8), count), :] = other_ref[...]
    tail = wire[2 * step : 2 * step + chans] * factor
    rest_w = 2 * step - 256
    for n in range(3):
        low = n * chans
        wide = jnp.concatenate(
            [
                wire[low : low + chans] * factor,
                wire[step + low : step + low + chans] * factor,
                tail[:, n * rest_w : (n + 1) * rest_w],
            ],
            axis=1,
        )
        for k in range(3):
            w1_ref[2 - n, k] = wide[:, k * chans : (k + 1) * chans]
            w2_ref[k, 2 - n] = wide[:, step + k * chans : step + (k + 1) * chans]
    cond_ref[...] = jnp.transpose(tail)[3 * rest_w : 3 * rest_w + 3, :chans]


def stacked(block, count, chans):
    step = 3 * chans
    return jnp.concatenate(
        [jnp.pad(block, ((0, 0), (r * step, (count - 1 - r) * step))) for r in range(count)], axis=0
    )


def build(mesh):
    ny, nx = mesh.shape["gy"], mesh.shape["gx"]
    axes = ("gy", "gx")

    def send(value, move):
        pairs = []
        for a in range(ny):
            for b in range(nx):
                to = move(a, b)
                if 0 <= to[0] < ny and 0 <= to[1] < nx:
                    pairs.append((a * nx + b, to[0] * nx + to[1]))
        return lax.ppermute(value, axes, pairs)

    def swap(first, second, axis):
        def partner(offset):
            def move(a, b):
                v = [a, b]
                v[axis] += 1 if (v[axis] + offset) % 2 == 0 else -1
                return v

            return move

        return send(first, partner(0)), send(second, partner(1))

    def local(
        sky, lens_phi, cotangent, tile_mask, weight_one, weight_two, cond_one, bias_one, cond_two
    ):
        chans, rows, width = sky.shape
        step = 3 * chans
        size = 4 * chans + 16
        edge = jax.ShapeDtypeStruct((size, 128), BF)
        edges = jax.ShapeDtypeStruct((2, size, 128), BF)
        vmem = pl.BlockSpec(memory_space=pltpu.VMEM)
        first = pl.BlockSpec((chans, 16, width), lambda i: (0, 0, 0))
        last = pl.BlockSpec((chans, 16, width), lambda i: (0, rows // 16 - 1, 0))
        ra, rb = pl.pallas_call(
            row_kernel,
            grid=(1,),
            out_shape=(edge, edge),
            in_specs=[first, last, first, last, vmem, vmem],
            out_specs=(vmem, vmem),
            name="edge_rows",
        )(sky, sky, cotangent, cotangent, lens_phi, tile_mask)
        ra, rb = swap(ra, rb, 0)

        def taps(weight, back):
            if back:
                return weight[::-1, ::-1].transpose(3, 0, 1, 2).reshape(chans, 3 * step)
            return weight.transpose(2, 0, 1, 3).reshape(chans, 3 * step)

        w1f, w1b = taps(weight_one, False), taps(weight_one, True)
        w2f, w2b = taps(weight_two, False), taps(weight_two, True)
        conds = jnp.stack([cond_one, bias_one, cond_two], axis=1)
        conds = jnp.pad(conds, ((0, 0), (0, 125)))

        ca, cb, own, halo = pl.pallas_call(
            col_kernel,
            out_shape=(edge, edge, edges, edges),
            scratch_shapes=[pltpu.VMEM((8 * chans // 2, 128), F32)],
            name="edge_cols",
        )(sky, cotangent, lens_phi, tile_mask, ra, rb)
        ca, cb = swap(ca, cb, 1)

        flops = 2 * 9 * chans * chans * rows * width
        field = pltpu.VMEM(((rows + 4) * step, 128), BF)
        rowwise = pltpu.VMEM((rows + 8, 128), F32)
        inner = jax.ShapeDtypeStruct(((rows + 2) * chans, 128), BF)
        acc = jax.ShapeDtypeStruct((step, step), F32)
        hid, dpre, acc1, acc2, cacc = pl.pallas_call(
            hidden_kernel,
            out_shape=(inner, inner, acc, acc, jax.ShapeDtypeStruct((3, chans, 128), F32)),
            scratch_shapes=[
                field, field, pltpu.VMEM(((rows + 4) * chans, 128), BF), rowwise, rowwise,
            ],
            compiler_params=pltpu.CompilerParams(vmem_limit_bytes=32 << 20),
            cost_estimate=pl.CostEstimate(
                flops=8 * flops, bytes_accessed=8 << 20, transcendentals=0
            ),
            name="hidden",
        )(
            sky, cotangent, lens_phi, tile_mask, halo,
            stacked(w1f, R1, chans), stacked(w2b, R1, chans), conds,
        )

        cols = jax.ShapeDtypeStruct((chans, 512), BF)
        count = (2 * step + chans) // 2
        wires = jax.ShapeDtypeStruct((count, 128), F32)
        hcol, dcol, keep, give = pl.pallas_call(
            lambda *refs: edge_kernel(rows, *refs),
            out_shape=(cols, cols, wires, wires),
            scratch_shapes=[pltpu.VMEM((2 * count, 128), F32)],
            name="edge_parts",
        )(ca, cb, own, w1f, w2b, conds, acc1, acc2, cacc)

        def output(with_phi, src, mid, col, weights, name):
            return pl.pallas_call(
                lambda *refs: output_kernel(with_phi, *refs),
                out_shape=jax.ShapeDtypeStruct(src.shape, BF),
                scratch_shapes=[
                    pltpu.VMEM(((rows + 2) * step, 128), BF),
                    pltpu.VMEM((rows, chans, 128), F32),
                    pltpu.VMEM((rows, 128), F32),
                ],
                compiler_params=pltpu.CompilerParams(vmem_limit_bytes=16 << 20),
                cost_estimate=pl.CostEstimate(
                    flops=2 * flops, bytes_accessed=4 << 20, transcendentals=0
                ),
                name=name,
            )(src, lens_phi, tile_mask, mid, col, weights, conds)

        delensed = output(True, sky, hid, hcol, stacked(w2f, R2, chans), "delensed")
        grad_input = output(False, cotangent, dpre, dcol, stacked(w1b, R2, chans), "grad_input")

        keep = keep + send(give, lambda a, b: (a ^ 1, b))
        for bit in [1 << k for k in range(1, ny.bit_length() - 1)]:
            keep = keep + send(keep, lambda a, b: (a ^ bit, b))
        for bit in [1 << k for k in range(nx.bit_length() - 1)]:
            keep = keep + send(keep, lambda a, b: (a, b ^ bit))
        other = send(keep, lambda a, b: (a ^ 1, b))

        factor = float(1.0 / (rows * ny * width * nx) ** 0.5)
        grads = jax.ShapeDtypeStruct((3, 3, chans, chans), F32)
        grad_w1, grad_w2, grad_cond = pl.pallas_call(
            lambda *refs: unpack_kernel(factor, *refs),
            out_shape=(grads, grads, jax.ShapeDtypeStruct((3, chans), F32)),
            scratch_shapes=[pltpu.VMEM((2 * count, 128), F32)],
            name="unpack",
        )(keep, other)
        return delensed, grad_input, grad_w1, grad_w2, grad_cond

    return local


def solution(mesh):
    return jax.shard_map(
        build(mesh),
        mesh=mesh,
        in_specs=(
            P(None, "gy", "gx"),
            P("gy", "gx"),
            P(None, "gy", "gx"),
            P("gy", "gx"),
            P(),
            P(),
            P(),
            P(),
            P(),
        ),
        out_specs=(P(None, "gy", "gx"), P(None, "gy", "gx"), P(), P(), P()),
        check_vma=False,
    )
```

```python
import jax
import jax.numpy as jnp
from jax import lax
from jax.experimental import pallas as pl
from jax.experimental.pallas import tpu as pltpu
from jax.sharding import PartitionSpec as P

TILE = 8
BF = jnp.bfloat16
F32 = jnp.float32
NT = (((1,), (1,)), ((), ()))
NN = (((1,), (0,)), ((), ()))
TN = (((0,), (0,)), ((), ()))
R1 = 3
R2 = 4
GROUP1 = 6
GROUP2 = 8


def lane_iota(rows):
    return lax.broadcasted_iota(jnp.int32, (rows, 128), 1)


def tile_rows(mask_ref):
    tcols = mask_ref.shape[1]
    lane = lax.broadcasted_iota(jnp.int32, (tcols, 128), 1)
    row = lax.broadcasted_iota(jnp.int32, (tcols, 128), 0)
    spread = (lane // TILE == row).astype(F32).astype(BF)
    return lax.dot_general(
        mask_ref[...].astype(F32).astype(BF), spread, NN, preferred_element_type=F32
    )


def is_odd(axis):
    return lax.rem(lax.axis_index(axis), 2) == 1


def row_kernel(sky_top, sky_bot, cot_top, cot_bot, phi_ref, mask_ref, a_ref, b_ref):
    chans = sky_top.shape[0]
    cells = tile_rows(mask_ref)
    odd = is_odd("gy")
    parts = []
    for sky, cot, first, mrow, prow in (
        (sky_top, cot_top, 0, 0, 0),
        (sky_bot, cot_bot, 14, mask_ref.shape[0] - 1, phi_ref.shape[0] - 1),
    ):
        keep = cells[mrow : mrow + 1]
        low = jnp.broadcast_to(keep, (chans, 128)).astype(BF)
        part = []
        for src in (sky, cot):
            block = jnp.transpose(src[...], (1, 0, 2))
            part += [block[first] * low, block[first + 1] * low]
        row = lax.broadcasted_iota(jnp.int32, (16, 128), 0)
        prow_v = jnp.broadcast_to(phi_ref[prow : prow + 1].astype(F32), (16, 128))
        part.append(jnp.where(row == 0, prow_v, jnp.where(row == 1, keep, 0.0)).astype(BF))
        parts.append(jnp.concatenate(part, axis=0))
    up, down = parts
    a_ref[...] = jnp.where(odd, up, down)
    b_ref[...] = jnp.where(odd, down, up)


def col_kernel(
    sky_ref, cot_ref, phi_ref, mask_ref, a_ref, b_ref,
    sa_ref, sb_ref, own_ref, halo_ref, strip,
):
    chans, rows, width = sky_ref.shape
    size = a_ref.shape[0]
    odd = is_odd("gy")
    ra, rb = a_ref[...], b_ref[...]
    tops_all = jnp.where(odd, ra, rb)
    bots_all = jnp.where(odd, rb, ra)
    halo_ref[0] = tops_all
    halo_ref[1] = bots_all
    half = chans // 2
    lane8 = lane_iota(8)
    row8 = lax.broadcasted_iota(jnp.int32, (8, 128), 0)
    pick = ((row8 < 2) & (lane8 == row8)) | (
        (row8 >= 2) & (row8 < 4) & (lane8 == row8 + (width - 4))
    )
    pick = pick.astype(F32).astype(BF)
    trows, tcols = mask_ref.shape
    prow = lax.broadcasted_iota(jnp.int32, (8, tcols), 0)
    pcol = lax.broadcasted_iota(jnp.int32, (8, tcols), 1)
    pick_t = ((prow < 2) & (pcol == 0)) | ((prow >= 2) & (prow < 4) & (pcol == tcols - 1))
    edge = lax.dot_general(
        pick_t.astype(F32).astype(BF),
        mask_ref[...].astype(F32).astype(BF),
        NT,
        preferred_element_type=F32,
    )
    lane_t = lax.broadcasted_iota(jnp.int32, (trows, 128), 1)
    row_t = lax.broadcasted_iota(jnp.int32, (trows, 128), 0)
    spread = (lane_t // TILE == row_t).astype(F32).astype(BF)
    keep = lax.dot_general(edge.astype(BF), spread, NN, preferred_element_type=F32)
    phis = lax.dot_general(pick, phi_ref[...], NT, preferred_element_type=F32)
    phis = jnp.concatenate([phis, jnp.zeros((8, 128 - rows), F32)], axis=1)
    lane = lane_iota(chans)
    for which, src in ((0, sky_ref), (1, cot_ref)):
        both = jnp.concatenate([src[:half], src[half:]], axis=1).reshape(half * 128, width)
        flat = lax.dot_general(pick, both, NT, preferred_element_type=F32)
        for j in range(half):
            strip[8 * j : 8 * j + 8] = flat[:, 128 * j : 128 * j + 128]
        for k in range(4):
            part = strip[pl.ds(k, half, stride=8), :]
            col = jnp.concatenate([part, pltpu.roll(part, 64, 1)], axis=0)
            col = (col * keep[k : k + 1]).astype(BF)
            at = (0, 1, width - 2, width - 1)[k]
            for value, where in ((tops_all, (126, 127)), (bots_all, (rows, rows + 1))):
                for n in range(2):
                    base = (2 * which + n) * chans
                    cell = value[base : base + chans, at : at + 1]
                    col = jnp.where(lane == where[n], jnp.broadcast_to(cell, col.shape), col)
            base = (2 * which + k % 2) * chans
            own_ref[k // 2, base : base + chans] = col
    row = lax.broadcasted_iota(jnp.int32, (16, 128), 0)
    lane16 = lane_iota(16)
    tops = tops_all[4 * chans : size].astype(F32)
    bots = bots_all[4 * chans : size].astype(F32)
    for side, k, at in ((0, 0, 0), (1, 3, width - 1)):
        extra = jnp.where(
            row == 0,
            jnp.broadcast_to(phis[k : k + 1], (16, 128)),
            jnp.where(row == 1, jnp.broadcast_to(keep[k : k + 1], (16, 128)), 0.0),
        )
        extra = jnp.where(lane16 == 127, jnp.broadcast_to(tops[:, at : at + 1], (16, 128)), extra)
        extra = jnp.where(lane16 == rows, jnp.broadcast_to(bots[:, at : at + 1], (16, 128)), extra)
        own_ref[side, 4 * chans : size] = extra.astype(BF)
    odd_x = is_odd("gx")
    sa_ref[...] = jnp.where(odd_x, own_ref[0], own_ref[1])
    sb_ref[...] = jnp.where(odd_x, own_ref[1], own_ref[0])


def silu_parts(pre):
    sigma = 1.0 / (1.0 + jnp.exp(-pre))
    return pre * sigma, sigma * (1.0 + pre * (1.0 - sigma))


def two_windows(src, first, second, size):
    return jnp.concatenate([src[first : first + size], src[second : second + size]], axis=1)


def hidden_kernel(
    sky_ref, cot_ref, phi_ref, mask_ref, halo_ref, w1s_ref, w2ts_ref, cond_ref,
    hid_ref, dpre_ref, acc1, acc2, cacc,
    a3x, a3g, dz, phix, maskx,
):
    chans, rows, width = sky_ref.shape
    size = halo_ref.shape[1]
    step = 3 * chans
    trows = mask_ref.shape[0]
    cells = tile_rows(mask_ref)
    lane1 = lane_iota(1)
    inside = jnp.where((lane1 == 0) | (lane1 == 127), 0.0, 1.0)
    for k, at in ((0, 0), (1, rows + 1)):
        extra = halo_ref[k, 4 * chans : size].astype(F32)
        phix[at : at + 1] = extra[0:1]
        maskx[at : at + 1] = extra[1:2] * inside
    phix[1 : rows + 1] = phi_ref[...].astype(F32)
    for t in range(trows):
        maskx[1 + TILE * t : 1 + TILE * (t + 1)] = jnp.broadcast_to(
            cells[t : t + 1] * inside, (TILE, 128)
        )

    gphi = jnp.zeros((chans, 128), F32)

    def put(dst, y, value):
        base = (y + 2) * step
        dst[base : base + chans] = pltpu.roll(value, 1, 1)
        dst[base + chans : base + 2 * chans] = value
        dst[base + 2 * chans : base + 3 * chans] = pltpu.roll(value, 127, 1)

    for which, src, dst in ((0, sky_ref, a3x), (1, cot_ref, a3g)):
        for j in range(rows // 16):
            block = jnp.transpose(src[:, 16 * j : 16 * j + 16, :], (1, 0, 2))
            for t in range(2):
                low = jnp.broadcast_to(cells[2 * j + t : 2 * j + t + 1], (chans, 128)).astype(BF)
                for n in range(TILE):
                    y = 16 * j + TILE * t + n
                    value = block[TILE * t + n] * low
                    put(dst, y, value)
                    if which:
                        gphi = gphi + value.astype(F32) * phix[y + 1 : y + 2]
        for k, first in ((0, -2), (1, rows)):
            for n in range(2):
                base = (2 * which + n) * chans
                put(dst, first + n, halo_ref[k, base : base + chans])
    cacc[2] = gphi

    gain = cond_ref[:, 0:1]
    bias = cond_ref[:, 1:2]
    split = (rows + 2) // 2
    zero = jnp.zeros((chans, 128), BF)
    for y in (-2, -1, rows, rows + 1):
        dz[(y + 2) * chans : (y + 3) * chans] = zero

    def first_pass(it, dphi, dsum):
        y0 = R1 * it - 1
        win = (R1 + 2) * step
        at = ((y0 + 1) * step, (y0 + split + 1) * step)
        pre = lax.dot_general(
            w1s_ref[...], two_windows(a3x, *at, win), NN, preferred_element_type=F32
        )
        back = lax.dot_general(
            w2ts_ref[...], two_windows(a3g, *at, win), NN, preferred_element_type=F32
        )
        for h in range(2):
            for r in range(R1):
                row = y0 + h * split + r + 1
                here = (slice(r * chans, (r + 1) * chans), slice(h * 128, h * 128 + 128))
                keep = maskx[row : row + 1]
                act, slope = silu_parts(pre[here] + gain * phix[row : row + 1] + bias)
                base = row * chans
                hid_ref[base : base + chans] = (act * keep).astype(BF)
                value = (back[here] * keep * slope).astype(BF)
                dpre_ref[base : base + chans] = value
                if 1 <= row <= rows:
                    dz[base + chans : base + 2 * chans] = value
                    wide = value.astype(F32)
                    dphi = dphi + wide * phix[row : row + 1]
                    dsum = dsum + wide
        return dphi, dsum

    dphi = jnp.zeros((chans, 128), F32)
    dsum = jnp.zeros((chans, 128), F32)
    for it in range(split // R1):
        dphi, dsum = first_pass(it, dphi, dsum)
    cacc[0] = dphi
    cacc[1] = dsum

    acc1[...] = jnp.zeros_like(acc1)
    acc2[...] = jnp.zeros_like(acc2)

    def rows_of(src, start, size):
        return src[start : start + size]

    def grads_one(it):
        ys = [GROUP1 * it + n - 1 for n in range(GROUP1)]
        acc1[...] += lax.dot_general(
            jnp.concatenate([rows_of(dz, (y + 1) * chans, step) for y in ys], axis=1),
            jnp.concatenate([rows_of(a3x, (y + 2) * step, step) for y in ys], axis=1),
            NT, preferred_element_type=F32,
        )

    def grads_two(it):
        ys = [GROUP2 * it + n for n in range(GROUP2)]
        acc2[...] += lax.dot_general(
            jnp.concatenate([rows_of(a3g, (y + 2) * step, step) for y in ys], axis=1),
            jnp.concatenate([rows_of(hid_ref, y * chans, step) for y in ys], axis=1),
            NT, preferred_element_type=F32,
        )

    for it in range((rows + 2) // GROUP1):
        grads_one(it)
    for it in range(rows // GROUP2):
        grads_two(it)


def edge_kernel(
    rows, a_ref, b_ref, own_ref, w1c_ref, w2tc_ref, w2c_ref, w1tc_ref, cond_ref,
    acc1, acc2, cacc,
    hfix_ref, dfix_ref, keep_ref, give_ref, wire,
):
    size = a_ref.shape[0]
    chans = (size - 16) // 4
    step = 3 * chans
    odd = is_odd("gx")
    ra, rb = a_ref[...], b_ref[...]
    lft = jnp.where(odd, ra, rb)
    rgt = jnp.where(odd, rb, ra)
    own_l, own_r = own_ref[0], own_ref[1]

    def at(value, which, n):
        base = (2 * which + n) * chans
        return value[base : base + chans]

    def columns(which):
        return [at(v, which, n) for v in (lft, own_l, own_r, rgt) for n in range(2)]

    centres = (1, 2, 5, 6)

    def taps_of(cols):
        pieces = []
        for ky in range(3):
            moved = [c if ky == 1 else pltpu.roll(c, (1, 0, 127)[ky], 1) for c in cols]
            for kx in range(3):
                pieces.append(jnp.concatenate([moved[c + kx - 1] for c in centres], axis=1))
        return jnp.concatenate(pieces, axis=0)

    x_taps = taps_of(columns(0))
    g_cols = columns(1)
    extra = [v[4 * chans : size].astype(F32) for v in (lft, own_l, own_r, rgt)]
    phi_c = jnp.concatenate([e[0:1] for e in extra], axis=1)
    mask_c = jnp.concatenate([e[1:2] for e in extra], axis=1)
    pre = lax.dot_general(w1c_ref[...], x_taps, NN, preferred_element_type=F32)
    back = lax.dot_general(w2tc_ref[...], taps_of(g_cols), NN, preferred_element_type=F32)
    act, slope = silu_parts(pre + cond_ref[:, 0:1] * phi_c + cond_ref[:, 1:2])
    hcol = (act * mask_c).astype(BF)
    dcol = (back * mask_c * slope).astype(BF)

    mine = jnp.broadcast_to((lane_iota(1) < rows).astype(F32), (chans, 128)).astype(BF)
    d_own = [dcol[:, 128:256] * mine, dcol[:, 256:384] * mine]
    part1 = lax.dot_general(
        jnp.concatenate(d_own, axis=1), x_taps[:, 128:384], NT, preferred_element_type=F32
    )
    h_cols = [hcol[:, 128 * k : 128 * k + 128] for k in range(4)]
    g_own = {k: g_cols[n] * mine for k, n in ((0, 2), (1, 3), (2, 4), (3, 5))}
    for kx, pairs in (
        (0, ((0, 0), (1, 1))),
        (1, ((0, 1), (3, 2))),
        (2, ((2, 2), (3, 3))),
    ):
        lhs = jnp.concatenate([g_own[g] for g, _ in pairs], axis=1)
        rhs = []
        for ky in range(3):
            moved = [
                h_cols[h] if ky == 1 else pltpu.roll(h_cols[h], (1, 0, 127)[ky], 1)
                for _, h in pairs
            ]
            rhs.append(jnp.concatenate(moved, axis=1))
        part2 = lax.dot_general(
            lhs, jnp.concatenate(rhs, axis=0), NT, preferred_element_type=F32
        )
        low = (2 - kx) * chans
        wide = jnp.concatenate(
            [
                acc1[low : low + chans] + part1[:, kx * step : (kx + 1) * step],
                acc2[low : low + chans] + part2,
            ],
            axis=1,
        )
        wire[low : low + chans] = wide[:, :128]
        wire[step + low : step + low + chans] = wide[:, 128:256]
        if kx == 0:
            tails = []
        tails.insert(0, wide[:, 256 : 2 * step])
    dphi, dsum = cacc[0], cacc[1]
    for d, k in ((d_own[0], 1), (d_own[1], 2)):
        dphi = dphi + d.astype(F32) * extra[k][0:1]
        dsum = dsum + d.astype(F32)
    sums = [jnp.sum(v, axis=1, keepdims=True) for v in (dphi, dsum, cacc[2])]
    fill = jnp.zeros((chans, 128 - 3 * tails[0].shape[1] - 3), F32)
    wire[2 * step : 2 * step + chans] = jnp.concatenate(tails + sums + [fill], axis=1)
    none = jnp.zeros((chans, 128), BF)
    half = chans // 2
    lane = lane_iota(half)
    for weights, field, fix in ((w2c_ref, hcol, hfix_ref), (w1tc_ref, dcol, dfix_ref)):
        f = [field[:, 128 * k : 128 * k + 128] for k in range(4)]
        pieces = []
        for ky in range(3):
            m = [c if ky == 1 else pltpu.roll(c, (1, 0, 127)[ky], 1) for c in f]
            pieces.append(jnp.concatenate([m[0], m[1], none, none], axis=1))
            pieces.append(jnp.concatenate([m[1], none, none, m[2]], axis=1))
            pieces.append(jnp.concatenate([none, none, m[2], m[3]], axis=1))
        fixes = lax.dot_general(
            weights[...], jnp.concatenate(pieces, axis=0), NN, preferred_element_type=F32
        )
        for k in range(4):
            col = fixes[:, 128 * k : 128 * k + 128]
            part = jnp.where(lane < rows, col[:half], pltpu.roll(col[half:], rows, 1))
            high = part.astype(BF).astype(F32)
            fix[pl.ds(k, half, stride=8), :] = high
            fix[pl.ds(4 + k, half, stride=8), :] = part - high

    count = wire.shape[0] // 2
    core = lax.rem(lax.axis_index("gy"), 2)
    keep_ref[...] = wire[pl.ds(pl.multiple_of(core * count, 8), count), :]
    give_ref[...] = wire[pl.ds(pl.multiple_of((1 - core) * count, 8), count), :]


def output_kernel(
    with_phi, src_ref, phi_ref, mask_ref, mid_ref, fix_ref, weights_ref, cond_ref,
    out_ref, a3, rowbuf, fixbuf,
):
    chans, rows, width = src_ref.shape
    step = 3 * chans
    half = chans // 2
    cells = tile_rows(mask_ref)
    if with_phi:
        phi = phi_ref[...].astype(F32)
        gain = cond_ref[:, 2:3]
    lane8 = lane_iota(8)
    row8 = lax.rem(lax.broadcasted_iota(jnp.int32, (8, 128), 0), 4)
    place = (lane8 == jnp.where(row8 < 2, row8, row8 + (width - 4))).astype(F32).astype(BF)
    for j in range(half):
        got = lax.dot_general(
            fix_ref[8 * j : 8 * j + 8].astype(BF), place, TN, preferred_element_type=F32
        )
        fixbuf[j] = got[:rows]
        fixbuf[j + half] = got[rows:]

    for y in range(rows + 2):
        centre = mid_ref[y * chans : (y + 1) * chans]
        base = y * step
        a3[base : base + chans] = pltpu.roll(centre, 1, 1)
        a3[base + chans : base + 2 * chans] = centre
        a3[base + 2 * chans : base + 3 * chans] = pltpu.roll(centre, 127, 1)

    for it in range(rows // (2 * R2)):
        y0 = R2 * it
        got = lax.dot_general(
            weights_ref[...],
            two_windows(a3, y0 * step, (y0 + rows // 2) * step, (R2 + 2) * step),
            NN, preferred_element_type=F32,
        )
        for h in range(2):
            for r in range(R2):
                y = y0 + h * (rows // 2) + r
                part = got[r * chans : (r + 1) * chans, h * 128 : h * 128 + 128]
                if with_phi:
                    part = part + gain * phi[y : y + 1]
                rowbuf[y] = part

    for j in range(rows // 16):
        here = slice(16 * j, 16 * j + 16)
        keep = jnp.concatenate(
            [jnp.broadcast_to(cells[2 * j + t : 2 * j + t + 1], (TILE, 128)) for t in range(2)],
            axis=0,
        )
        total = jnp.transpose(rowbuf[here], (1, 0, 2)) + fixbuf[:, here, :]
        out_ref[:, here, :] = ((total + src_ref[:, here, :].astype(F32)) * keep[None]).astype(BF)


def unpack_kernel(factor, keep_ref, other_ref, w1_ref, w2_ref, cond_ref, wire):
    chans = w1_ref.shape[2]
    step = 3 * chans
    count = keep_ref.shape[0]
    core = lax.rem(lax.axis_index("gy"), 2)
    wire[pl.ds(pl.multiple_of(core * count, 8), count), :] = keep_ref[...]
    wire[pl.ds(pl.multiple_of((1 - core) * count, 8), count), :] = other_ref[...]
    tail = wire[2 * step : 2 * step + chans] * factor
    rest_w = 2 * step - 256
    for n in range(3):
        low = n * chans
        wide = jnp.concatenate(
            [
                wire[low : low + chans] * factor,
                wire[step + low : step + low + chans] * factor,
                tail[:, n * rest_w : (n + 1) * rest_w],
            ],
            axis=1,
        )
        for k in range(3):
            w1_ref[2 - n, k] = wide[:, k * chans : (k + 1) * chans]
            w2_ref[k, 2 - n] = wide[:, step + k * chans : step + (k + 1) * chans]
    cond_ref[...] = jnp.transpose(tail)[3 * rest_w : 3 * rest_w + 3, :chans]


def limit(mib):
    return pltpu.CompilerParams(vmem_limit_bytes=mib << 20)


def stacked(block, count, chans):
    step = 3 * chans
    return jnp.concatenate(
        [jnp.pad(block, ((0, 0), (r * step, (count - 1 - r) * step))) for r in range(count)], axis=0
    )


def build(mesh):
    ny, nx = mesh.shape["gy"], mesh.shape["gx"]
    axes = ("gy", "gx")

    def send(value, move):
        pairs = []
        for a in range(ny):
            for b in range(nx):
                to = move(a, b)
                if 0 <= to[0] < ny and 0 <= to[1] < nx:
                    pairs.append((a * nx + b, to[0] * nx + to[1]))
        return lax.ppermute(value, axes, pairs)

    def swap(first, second, axis):
        def partner(offset):
            def move(a, b):
                v = [a, b]
                v[axis] += 1 if (v[axis] + offset) % 2 == 0 else -1
                return v

            return move

        return send(first, partner(0)), send(second, partner(1))

    def local(
        sky, lens_phi, cotangent, tile_mask, weight_one, weight_two, cond_one, bias_one, cond_two
    ):
        chans, rows, width = sky.shape
        step = 3 * chans
        size = 4 * chans + 16
        assert 2 * rows == 128 and width == 128
        edge = jax.ShapeDtypeStruct((size, 128), BF)
        edges = jax.ShapeDtypeStruct((2, size, 128), BF)
        vmem = pl.BlockSpec(memory_space=pltpu.VMEM)
        first = pl.BlockSpec((chans, 16, width), lambda i: (0, 0, 0))
        last = pl.BlockSpec((chans, 16, width), lambda i: (0, rows // 16 - 1, 0))
        ra, rb = pl.pallas_call(
            row_kernel,
            grid=(1,),
            out_shape=(edge, edge),
            in_specs=[first, last, first, last, vmem, vmem],
            out_specs=(vmem, vmem),
            compiler_params=limit(8),
            name="edge_rows",
        )(sky, sky, cotangent, cotangent, lens_phi, tile_mask)
        ra, rb = swap(ra, rb, 0)

        def taps(weight, back):
            if back:
                return weight[::-1, ::-1].transpose(3, 0, 1, 2).reshape(chans, 3 * step)
            return weight.transpose(2, 0, 1, 3).reshape(chans, 3 * step)

        w1f, w1b = taps(weight_one, False), taps(weight_one, True)
        w2f, w2b = taps(weight_two, False), taps(weight_two, True)
        conds = jnp.stack([cond_one, bias_one, cond_two], axis=1)
        conds = jnp.pad(conds, ((0, 0), (0, 125)))

        ca, cb, own, halo = pl.pallas_call(
            col_kernel,
            out_shape=(edge, edge, edges, edges),
            scratch_shapes=[pltpu.VMEM((8 * chans // 2, 128), F32)],
            compiler_params=limit(8),
            name="edge_cols",
        )(sky, cotangent, lens_phi, tile_mask, ra, rb)
        ca, cb = swap(ca, cb, 1)

        flops = 2 * 9 * chans * chans * rows * width
        field = pltpu.VMEM(((rows + 4) * step, 128), BF)
        rowwise = pltpu.VMEM((rows + 8, 128), F32)
        inner = jax.ShapeDtypeStruct(((rows + 2) * chans, 128), BF)
        acc = jax.ShapeDtypeStruct((step, step), F32)
        hid, dpre, acc1, acc2, cacc = pl.pallas_call(
            hidden_kernel,
            out_shape=(inner, inner, acc, acc, jax.ShapeDtypeStruct((3, chans, 128), F32)),
            scratch_shapes=[
                field, field, pltpu.VMEM(((rows + 4) * chans, 128), BF), rowwise, rowwise,
            ],
            compiler_params=limit(16),
            cost_estimate=pl.CostEstimate(
                flops=8 * flops, bytes_accessed=8 << 20, transcendentals=0
            ),
            name="hidden",
        )(
            sky, cotangent, lens_phi, tile_mask, halo,
            stacked(w1f, R1, chans), stacked(w2b, R1, chans), conds,
        )

        fix = jax.ShapeDtypeStruct((4 * chans, 128), F32)
        count = (2 * step + chans) // 2
        wires = jax.ShapeDtypeStruct((count, 128), F32)
        hfix, dfix, keep, give = pl.pallas_call(
            lambda *refs: edge_kernel(rows, *refs),
            out_shape=(fix, fix, wires, wires),
            scratch_shapes=[pltpu.VMEM((2 * count, 128), F32)],
            compiler_params=limit(8),
            name="edge_parts",
        )(ca, cb, own, w1f, w2b, w2f, w1b, conds, acc1, acc2, cacc)

        def output(with_phi, src, mid, fix, weights, name):
            return pl.pallas_call(
                lambda *refs: output_kernel(with_phi, *refs),
                out_shape=jax.ShapeDtypeStruct(src.shape, BF),
                scratch_shapes=[
                    pltpu.VMEM(((rows + 2) * step, 128), BF),
                    pltpu.VMEM((rows, chans, 128), F32),
                    pltpu.VMEM((chans, rows, 128), F32),
                ],
                compiler_params=limit(16),
                cost_estimate=pl.CostEstimate(
                    flops=2 * flops, bytes_accessed=4 << 20, transcendentals=0
                ),
                name=name,
            )(src, lens_phi, tile_mask, mid, fix, weights, conds)

        w2s, w1s = stacked(w2f, R2, chans), stacked(w1b, R2, chans)
        moves = [lambda a, b, bit=1 << k: (a ^ bit, b) for k in range(1, ny.bit_length() - 1)]
        moves += [lambda a, b, bit=1 << k: (a, b ^ bit) for k in range(nx.bit_length() - 1)]
        keep = keep + send(give, lambda a, b: (a ^ 1, b))
        outs = []
        for n, move in enumerate(moves):
            if n == 0:
                keep, hfix = lax.optimization_barrier((keep, hfix))
                outs.append(output(True, sky, hid, hfix, w2s, "delensed"))
            if n == 1:
                keep, dfix = lax.optimization_barrier((keep, dfix))
                outs.append(output(False, cotangent, dpre, dfix, w1s, "grad_input"))
            keep = keep + send(keep, move)
            if n < 2:
                keep, outs[n] = lax.optimization_barrier((keep, outs[n]))
        delensed, grad_input = outs
        other = send(keep, lambda a, b: (a ^ 1, b))

        factor = float(1.0 / (rows * ny * width * nx) ** 0.5)
        grads = jax.ShapeDtypeStruct((3, 3, chans, chans), F32)
        grad_w1, grad_w2, grad_cond = pl.pallas_call(
            lambda *refs: unpack_kernel(factor, *refs),
            out_shape=(grads, grads, jax.ShapeDtypeStruct((3, chans), F32)),
            scratch_shapes=[pltpu.VMEM((2 * count, 128), F32)],
            compiler_params=limit(8),
            name="unpack",
        )(keep, other)
        return delensed, grad_input, grad_w1, grad_w2, grad_cond

    return local


def solution(mesh):
    return jax.shard_map(
        build(mesh),
        mesh=mesh,
        in_specs=(
            P(None, "gy", "gx"),
            P("gy", "gx"),
            P(None, "gy", "gx"),
            P("gy", "gx"),
            P(),
            P(),
            P(),
            P(),
            P(),
        ),
        out_specs=(P(None, "gy", "gx"), P(None, "gy", "gx"), P(), P(), P()),
        check_vma=False,
    )
```

```python
import jax
import jax.numpy as jnp
from jax import lax
from jax.experimental import pallas as pl
from jax.experimental.pallas import tpu as pltpu
from jax.sharding import PartitionSpec as P

TILE = 8
BF = jnp.bfloat16
F32 = jnp.float32
NT = (((1,), (1,)), ((), ()))
NN = (((1,), (0,)), ((), ()))
TN = (((0,), (0,)), ((), ()))
R1 = 3
R2 = 4
GROUP1 = 6
GROUP2 = 8


def lane_iota(rows):
    return lax.broadcasted_iota(jnp.int32, (rows, 128), 1)


def tile_rows(mask_ref):
    tcols = mask_ref.shape[1]
    lane = lax.broadcasted_iota(jnp.int32, (tcols, 128), 1)
    row = lax.broadcasted_iota(jnp.int32, (tcols, 128), 0)
    spread = (lane // TILE == row).astype(F32).astype(BF)
    return lax.dot_general(
        mask_ref[...].astype(F32).astype(BF), spread, NN, preferred_element_type=F32
    )


def is_odd(axis):
    return lax.rem(lax.axis_index(axis), 2) == 1


def row_kernel(sky_ref, cot_ref, phi_ref, mask_ref, a_ref, b_ref, blocks, phis, tiles, sems):
    chans, rows, _ = sky_ref.shape
    copies = []
    for n, (src, dst) in enumerate(
        [
            (ref.at[:, pl.ds(first, 16), :], blocks.at[k])
            for k, (ref, first) in enumerate(
                ((sky_ref, 0), (cot_ref, 0), (sky_ref, rows - 16), (cot_ref, rows - 16))
            )
        ]
        + [(phi_ref.at[pl.ds(0, 16), :], phis.at[0]), (phi_ref.at[pl.ds(rows - 16, 16), :], phis.at[1])]
        + [(mask_ref, tiles)]
    ):
        copies.append(pltpu.make_async_copy(src, dst, sems.at[n]))
        copies[-1].start()
    for copy in copies:
        copy.wait()
    cells = tile_rows(tiles)
    odd = is_odd("gy")
    parts = []
    for side, (first, mrow) in enumerate(((0, 0), (14, tiles.shape[0] - 1))):
        keep = cells[mrow : mrow + 1]
        low = jnp.broadcast_to(keep, (chans, 128)).astype(BF)
        part = []
        for k in range(2):
            block = jnp.transpose(blocks[2 * side + k], (1, 0, 2))
            part += [block[first] * low, block[first + 1] * low]
        row = lax.broadcasted_iota(jnp.int32, (16, 128), 0)
        prow = phis[side].astype(F32)[15 * side : 15 * side + 1]
        prow = jnp.broadcast_to(prow, (16, 128))
        part.append(jnp.where(row == 0, prow, jnp.where(row == 1, keep, 0.0)).astype(BF))
        parts.append(jnp.concatenate(part, axis=0))
    up, down = parts
    a_ref[...] = jnp.where(odd, up, down)
    b_ref[...] = jnp.where(odd, down, up)


def prep_kernel(
    sky_hbm, cot_hbm, phi_hbm, mask_hbm, a3, own_ref, gphi_ref, phix, maskx,
    strip, sky_ref, cot_ref, phi_ref, mask_ref, sems,
):
    chans, rows, width = sky_ref.shape
    size = own_ref.shape[1]
    step = 3 * chans
    half = chans // 2
    copies = [
        pltpu.make_async_copy(src, dst, sems.at[n])
        for n, (src, dst) in enumerate(
            ((mask_hbm, mask_ref), (phi_hbm, phi_ref), (sky_hbm, sky_ref), (cot_hbm, cot_ref))
        )
    ]
    for copy in copies:
        copy.start()
    copies[0].wait()
    copies[1].wait()
    cells = tile_rows(mask_ref)
    phi = phi_ref[...].astype(F32)
    phix[...] = phi
    for t in range(mask_ref.shape[0]):
        maskx[TILE * t : TILE * (t + 1)] = jnp.broadcast_to(cells[t : t + 1], (TILE, 128))
    lane8 = lane_iota(8)
    row8 = lax.broadcasted_iota(jnp.int32, (8, 128), 0)
    pick = ((row8 < 2) & (lane8 == row8)) | (
        (row8 >= 2) & (row8 < 4) & (lane8 == row8 + (width - 4))
    )
    pick = pick.astype(F32).astype(BF)
    trows, tcols = mask_ref.shape
    prow = lax.broadcasted_iota(jnp.int32, (8, tcols), 0)
    pcol = lax.broadcasted_iota(jnp.int32, (8, tcols), 1)
    pick_t = ((prow < 2) & (pcol == 0)) | ((prow >= 2) & (prow < 4) & (pcol == tcols - 1))
    edge = lax.dot_general(
        pick_t.astype(F32).astype(BF),
        mask_ref[...].astype(F32).astype(BF),
        NT,
        preferred_element_type=F32,
    )
    lane_t = lax.broadcasted_iota(jnp.int32, (trows, 128), 1)
    row_t = lax.broadcasted_iota(jnp.int32, (trows, 128), 0)
    spread = (lane_t // TILE == row_t).astype(F32).astype(BF)
    keep = lax.dot_general(edge.astype(BF), spread, NN, preferred_element_type=F32)
    phis = lax.dot_general(pick, phi_ref[...], NT, preferred_element_type=F32)
    phis = jnp.concatenate([phis, jnp.zeros((8, 128 - rows), F32)], axis=1)
    gphi = jnp.zeros((chans, 128), F32)
    for which, src in ((0, sky_ref), (1, cot_ref)):
        copies[2 + which].wait()
        both = jnp.concatenate([src[:half], src[half:]], axis=1).reshape(half * 128, width)
        flat = lax.dot_general(pick, both, NT, preferred_element_type=F32)
        for j in range(half):
            strip[which, 8 * j : 8 * j + 8] = flat[:, 128 * j : 128 * j + 128]
        for k in range(4):
            part = strip[which, pl.ds(k, half, stride=8), :]
            col = jnp.concatenate([part, pltpu.roll(part, 64, 1)], axis=0)
            base = (2 * which + k % 2) * chans
            own_ref[k // 2, base : base + chans] = (col * keep[k : k + 1]).astype(BF)
        for j in range(rows // 16):
            block = jnp.transpose(src[:, 16 * j : 16 * j + 16, :], (1, 0, 2))
            for t in range(2):
                low = jnp.broadcast_to(cells[2 * j + t : 2 * j + t + 1], (chans, 128)).astype(BF)
                for n in range(TILE):
                    y = 16 * j + TILE * t + n
                    value = block[TILE * t + n] * low
                    a3[which, y * step : (y + 1) * step] = three_copies(value)
                    if which:
                        gphi = gphi + value.astype(F32) * phi[y : y + 1]
    gphi_ref[...] = gphi
    row = lax.broadcasted_iota(jnp.int32, (16, 128), 0)
    for side, k in ((0, 0), (1, 3)):
        extra = jnp.where(
            row == 0,
            jnp.broadcast_to(phis[k : k + 1], (16, 128)),
            jnp.where(row == 1, jnp.broadcast_to(keep[k : k + 1], (16, 128)), 0.0),
        )
        own_ref[side, 4 * chans : size] = extra.astype(BF)


def three_copies(value):
    return jnp.concatenate([pltpu.roll(value, 1, 1), value, pltpu.roll(value, 127, 1)], axis=0)


def col_kernel(rows, width, mine_ref, a_ref, b_ref, sa_ref, sb_ref, own_ref, halo_ref):
    size = a_ref.shape[0]
    odd = is_odd("gy")
    ra, rb = a_ref[...], b_ref[...]
    tops = jnp.where(odd, ra, rb)
    bots = jnp.where(odd, rb, ra)
    halo_ref[0] = tops
    halo_ref[1] = bots
    chans = (size - 16) // 4
    lane = lane_iota(chans)
    lane16 = lane_iota(16)
    sides = []
    for side in range(2):
        parts = []
        for m in range(4):
            which, k = divmod(m, 2)
            at = k + (width - 2) * side
            col = mine_ref[side, m * chans : (m + 1) * chans]
            for value, where in ((tops, (126, 127)), (bots, (rows, rows + 1))):
                for n in range(2):
                    base = (2 * which + n) * chans
                    cell = value[base : base + chans, at : at + 1]
                    col = jnp.where(lane == where[n], jnp.broadcast_to(cell, col.shape), col)
            parts.append(col)
        at = (width - 1) * side
        extra = mine_ref[side, 4 * chans : size].astype(F32)
        for value, where in ((tops, 127), (bots, rows)):
            cell = value[4 * chans : size].astype(F32)[:, at : at + 1]
            extra = jnp.where(lane16 == where, jnp.broadcast_to(cell, (16, 128)), extra)
        parts.append(extra.astype(BF))
        sides.append(jnp.concatenate(parts, axis=0))
        own_ref[side] = sides[side]
    odd_x = is_odd("gx")
    sa_ref[...] = jnp.where(odd_x, sides[0], sides[1])
    sb_ref[...] = jnp.where(odd_x, sides[1], sides[0])


def silu_parts(pre):
    sigma = 1.0 / (1.0 + jnp.exp(-pre))
    return pre * sigma, sigma * (1.0 + pre * (1.0 - sigma))


def hidden_kernel(
    a3, phi_own, mask_own, halo_ref, w1s_ref, w2ts_ref, cond_ref,
    hid_ref, dpre_ref, acc1, acc2, cacc,
    dz, phix, maskx, ringx, ringg,
):
    rows, width = phi_own.shape
    a3x, a3g = a3.at[0], a3.at[1]
    size = halo_ref.shape[1]
    chans = (size - 16) // 4
    step = 3 * chans
    lane1 = lane_iota(1)
    inside = jnp.where((lane1 == 0) | (lane1 == 127), 0.0, 1.0)
    for k, at in ((0, 0), (1, rows + 1)):
        extra = halo_ref[k, 4 * chans : size].astype(F32)
        phix[at : at + 1] = extra[0:1]
        maskx[at : at + 1] = extra[1:2] * inside
    phix[1 : rows + 1] = phi_own[...]
    maskx[1 : rows + 1] = mask_own[...] * inside
    for which, ring in ((0, ringx), (1, ringg)):
        for k in range(2):
            for n in range(2):
                base = (2 * which + n) * chans
                ring[(2 * k + n) * step : (2 * k + n + 1) * step] = three_copies(
                    halo_ref[k, base : base + chans]
                )

    def window(own, ring, y, count):
        parts = []
        if y < 0:
            parts.append(ring[(y + 2) * step : min(2, y + 2 + count) * step])
        low, high = max(y, 0), min(y + count, rows)
        if low < high:
            parts.append(own[low * step : high * step])
        if y + count > rows:
            low = max(y, rows) - rows
            parts.append(ring[(2 + low) * step : (2 + y + count - rows) * step])
        return parts[0] if len(parts) == 1 else jnp.concatenate(parts, axis=0)

    gain = cond_ref[:, 0:1]
    bias = cond_ref[:, 1:2]
    split = (rows + 2) // 2
    zero = jnp.zeros((chans, 128), BF)
    for y in (-2, -1, rows, rows + 1):
        dz[(y + 2) * chans : (y + 3) * chans] = zero

    def first_pass(it, dphi, dsum):
        y0 = R1 * it - 1

        def both(own, ring):
            pair = [window(own, ring, y0 - 1 + h * split, R1 + 2) for h in range(2)]
            return jnp.concatenate(pair, axis=1)

        pre = lax.dot_general(w1s_ref[...], both(a3x, ringx), NN, preferred_element_type=F32)
        back = lax.dot_general(w2ts_ref[...], both(a3g, ringg), NN, preferred_element_type=F32)
        for h in range(2):
            for r in range(R1):
                row = y0 + h * split + r + 1
                here = (slice(r * chans, (r + 1) * chans), slice(h * 128, h * 128 + 128))
                keep = maskx[row : row + 1]
                act, slope = silu_parts(pre[here] + gain * phix[row : row + 1] + bias)
                base = row * chans
                hid_ref[base : base + chans] = (act * keep).astype(BF)
                value = (back[here] * keep * slope).astype(BF)
                dpre_ref[base : base + chans] = value
                if 1 <= row <= rows:
                    dz[base + chans : base + 2 * chans] = value
                    wide = value.astype(F32)
                    dphi = dphi + wide * phix[row : row + 1]
                    dsum = dsum + wide
        return dphi, dsum

    dphi = jnp.zeros((chans, 128), F32)
    dsum = jnp.zeros((chans, 128), F32)
    for it in range(split // R1):
        dphi, dsum = first_pass(it, dphi, dsum)
    cacc[0] = dphi
    cacc[1] = dsum

    acc1[...] = jnp.zeros_like(acc1)
    acc2[...] = jnp.zeros_like(acc2)

    def rows_of(src, start, size):
        return src[start : start + size]

    def grads_one(it):
        ys = [GROUP1 * it + n - 1 for n in range(GROUP1)]
        acc1[...] += lax.dot_general(
            jnp.concatenate([rows_of(dz, (y + 1) * chans, step) for y in ys], axis=1),
            jnp.concatenate([window(a3x, ringx, y, 1) for y in ys], axis=1),
            NT, preferred_element_type=F32,
        )

    def grads_two(it):
        ys = [GROUP2 * it + n for n in range(GROUP2)]
        acc2[...] += lax.dot_general(
            jnp.concatenate([window(a3g, ringg, y, 1) for y in ys], axis=1),
            jnp.concatenate([rows_of(hid_ref, y * chans, step) for y in ys], axis=1),
            NT, preferred_element_type=F32,
        )

    for it in range((rows + 2) // GROUP1):
        grads_one(it)
    for it in range(rows // GROUP2):
        grads_two(it)


def edge_kernel(
    rows, a_ref, b_ref, own_ref, w1c_ref, w2tc_ref, w2c_ref, w1tc_ref, cond_ref,
    acc1, acc2, cacc, gphi_ref,
    hfix_ref, dfix_ref, keep_ref, give_ref, wire,
):
    size = a_ref.shape[0]
    chans = (size - 16) // 4
    step = 3 * chans
    odd = is_odd("gx")
    ra, rb = a_ref[...], b_ref[...]
    lft = jnp.where(odd, ra, rb)
    rgt = jnp.where(odd, rb, ra)
    own_l, own_r = own_ref[0], own_ref[1]

    def at(value, which, n):
        base = (2 * which + n) * chans
        return value[base : base + chans]

    def columns(which):
        return [at(v, which, n) for v in (lft, own_l, own_r, rgt) for n in range(2)]

    centres = (1, 2, 5, 6)

    def taps_of(cols):
        pieces = []
        for ky in range(3):
            moved = [c if ky == 1 else pltpu.roll(c, (1, 0, 127)[ky], 1) for c in cols]
            for kx in range(3):
                pieces.append(jnp.concatenate([moved[c + kx - 1] for c in centres], axis=1))
        return jnp.concatenate(pieces, axis=0)

    x_taps = taps_of(columns(0))
    g_cols = columns(1)
    extra = [v[4 * chans : size].astype(F32) for v in (lft, own_l, own_r, rgt)]
    phi_c = jnp.concatenate([e[0:1] for e in extra], axis=1)
    mask_c = jnp.concatenate([e[1:2] for e in extra], axis=1)
    pre = lax.dot_general(w1c_ref[...], x_taps, NN, preferred_element_type=F32)
    back = lax.dot_general(w2tc_ref[...], taps_of(g_cols), NN, preferred_element_type=F32)
    act, slope = silu_parts(pre + cond_ref[:, 0:1] * phi_c + cond_ref[:, 1:2])
    hcol = (act * mask_c).astype(BF)
    dcol = (back * mask_c * slope).astype(BF)

    mine = jnp.broadcast_to((lane_iota(1) < rows).astype(F32), (chans, 128)).astype(BF)
    d_own = [dcol[:, 128:256] * mine, dcol[:, 256:384] * mine]
    part1 = lax.dot_general(
        jnp.concatenate(d_own, axis=1), x_taps[:, 128:384], NT, preferred_element_type=F32
    )
    h_cols = [hcol[:, 128 * k : 128 * k + 128] for k in range(4)]
    g_own = {k: g_cols[n] * mine for k, n in ((0, 2), (1, 3), (2, 4), (3, 5))}
    for kx, pairs in (
        (0, ((0, 0), (1, 1))),
        (1, ((0, 1), (3, 2))),
        (2, ((2, 2), (3, 3))),
    ):
        lhs = jnp.concatenate([g_own[g] for g, _ in pairs], axis=1)
        rhs = []
        for ky in range(3):
            moved = [
                h_cols[h] if ky == 1 else pltpu.roll(h_cols[h], (1, 0, 127)[ky], 1)
                for _, h in pairs
            ]
            rhs.append(jnp.concatenate(moved, axis=1))
        part2 = lax.dot_general(
            lhs, jnp.concatenate(rhs, axis=0), NT, preferred_element_type=F32
        )
        low = (2 - kx) * chans
        wide = jnp.concatenate(
            [
                acc1[low : low + chans] + part1[:, kx * step : (kx + 1) * step],
                acc2[low : low + chans] + part2,
            ],
            axis=1,
        )
        wire[low : low + chans] = wide[:, :128]
        wire[step + low : step + low + chans] = wide[:, 128:256]
        if kx == 0:
            tails = []
        tails.insert(0, wide[:, 256 : 2 * step])
    dphi, dsum = cacc[0], cacc[1]
    for d, k in ((d_own[0], 1), (d_own[1], 2)):
        dphi = dphi + d.astype(F32) * extra[k][0:1]
        dsum = dsum + d.astype(F32)
    sums = [jnp.sum(v, axis=1, keepdims=True) for v in (dphi, dsum, gphi_ref[...])]
    fill = jnp.zeros((chans, 128 - 3 * tails[0].shape[1] - 3), F32)
    wire[2 * step : 2 * step + chans] = jnp.concatenate(tails + sums + [fill], axis=1)
    none = jnp.zeros((chans, 128), BF)
    half = chans // 2
    lane = lane_iota(half)
    for weights, field, fix in ((w2c_ref, hcol, hfix_ref), (w1tc_ref, dcol, dfix_ref)):
        f = [field[:, 128 * k : 128 * k + 128] for k in range(4)]
        pieces = []
        for ky in range(3):
            m = [c if ky == 1 else pltpu.roll(c, (1, 0, 127)[ky], 1) for c in f]
            pieces.append(jnp.concatenate([m[0], m[1], none, none], axis=1))
            pieces.append(jnp.concatenate([m[1], none, none, m[2]], axis=1))
            pieces.append(jnp.concatenate([none, none, m[2], m[3]], axis=1))
        fixes = lax.dot_general(
            weights[...], jnp.concatenate(pieces, axis=0), NN, preferred_element_type=F32
        )
        for k in range(4):
            col = fixes[:, 128 * k : 128 * k + 128]
            part = jnp.where(lane < rows, col[:half], pltpu.roll(col[half:], rows, 1))
            high = part.astype(BF).astype(F32)
            fix[pl.ds(k, half, stride=8), :] = high
            fix[pl.ds(4 + k, half, stride=8), :] = part - high

    count = wire.shape[0] // 2
    core = lax.rem(lax.axis_index("gy"), 2)
    keep_ref[...] = wire[pl.ds(pl.multiple_of(core * count, 8), count), :]
    give_ref[...] = wire[pl.ds(pl.multiple_of((1 - core) * count, 8), count), :]


def output_kernel(
    with_phi, src_hbm, phi_ref, mask_ref, mid_ref, fix_ref, weights_ref, cond_ref,
    out_ref, a3, rowbuf, fixbuf, src_ref, sem,
):
    chans, rows, width = src_ref.shape
    step = 3 * chans
    half = chans // 2
    fetch = pltpu.make_async_copy(src_hbm, src_ref, sem)
    fetch.start()
    if with_phi:
        gain = cond_ref[:, 2:3]
    lane8 = lane_iota(8)
    row8 = lax.rem(lax.broadcasted_iota(jnp.int32, (8, 128), 0), 4)
    place = (lane8 == jnp.where(row8 < 2, row8, row8 + (width - 4))).astype(F32).astype(BF)
    for j in range(half):
        got = lax.dot_general(
            fix_ref[8 * j : 8 * j + 8].astype(BF), place, TN, preferred_element_type=F32
        )
        fixbuf[j] = got[:rows]
        fixbuf[j + half] = got[rows:]

    for y in range(rows + 2):
        centre = mid_ref[y * chans : (y + 1) * chans]
        base = y * step
        a3[base : base + chans] = pltpu.roll(centre, 1, 1)
        a3[base + chans : base + 2 * chans] = centre
        a3[base + 2 * chans : base + 3 * chans] = pltpu.roll(centre, 127, 1)

    for it in range(rows // (2 * R2)):
        y0 = R2 * it
        got = lax.dot_general(
            weights_ref[...],
            jnp.concatenate(
                [a3[(y0 + h) * step : (y0 + h + R2 + 2) * step] for h in (0, rows // 2)], axis=1
            ),
            NN, preferred_element_type=F32,
        )
        for h in range(2):
            for r in range(R2):
                y = y0 + h * (rows // 2) + r
                part = got[r * chans : (r + 1) * chans, h * 128 : h * 128 + 128]
                if with_phi:
                    part = part + gain * phi_ref[y : y + 1]
                rowbuf[y] = part

    fetch.wait()
    for j in range(rows // 16):
        here = slice(16 * j, 16 * j + 16)
        keep = mask_ref[here]
        total = jnp.transpose(rowbuf[here], (1, 0, 2)) + fixbuf[:, here, :]
        out_ref[:, here, :] = ((total + src_ref[:, here, :].astype(F32)) * keep[None]).astype(BF)


def unpack_kernel(factor, keep_ref, other_ref, w1_ref, w2_ref, cond_ref, wire):
    chans = w1_ref.shape[2]
    step = 3 * chans
    count = keep_ref.shape[0]
    core = lax.rem(lax.axis_index("gy"), 2)
    wire[pl.ds(pl.multiple_of(core * count, 8), count), :] = keep_ref[...]
    wire[pl.ds(pl.multiple_of((1 - core) * count, 8), count), :] = other_ref[...]
    tail = wire[2 * step : 2 * step + chans] * factor
    rest_w = 2 * step - 256
    for n in range(3):
        low = n * chans
        wide = jnp.concatenate(
            [
                wire[low : low + chans] * factor,
                wire[step + low : step + low + chans] * factor,
                tail[:, n * rest_w : (n + 1) * rest_w],
            ],
            axis=1,
        )
        for k in range(3):
            w1_ref[2 - n, k] = wide[:, k * chans : (k + 1) * chans]
            w2_ref[k, 2 - n] = wide[:, step + k * chans : step + (k + 1) * chans]
    cond_ref[...] = jnp.transpose(tail)[3 * rest_w : 3 * rest_w + 3, :chans]


def limit(mib):
    return pltpu.CompilerParams(vmem_limit_bytes=mib << 20)


def keep_near(value):
    return pltpu.with_memory_space_constraint(value, pltpu.VMEM)


def stacked(block, count):
    chans, taps = block.shape
    step = taps // 3
    rows = []
    for r in range(count):
        parts = [block]
        if r:
            parts.insert(0, jnp.zeros((chans, r * step), BF))
        if r < count - 1:
            parts.append(jnp.zeros((chans, (count - 1 - r) * step), BF))
        rows.append(jnp.concatenate(parts, axis=1))
    return jnp.concatenate(rows, axis=0)


def weight_kernel(
    one_hbm, two_hbm, c1_hbm, b1_hbm, c2_hbm,
    w1f_ref, w2b_ref, w2f_ref, w1b_ref, w1s_ref, w2bs_ref, w2s_ref, w1bs_ref, cond_ref,
    one, two, vec0, vec1, vec2, sems,
):
    copies = [
        pltpu.make_async_copy(src, dst, sems.at[n])
        for n, (src, dst) in enumerate(
            ((one_hbm, one), (two_hbm, two), (c1_hbm, vec0), (b1_hbm, vec1), (c2_hbm, vec2))
        )
    ]
    for copy in copies:
        copy.start()
    for copy in copies:
        copy.wait()
    chans = one.shape[2]
    for src, fwd, fwd_s, count, bwd, bwd_s, back in (
        (one, w1f_ref, w1s_ref, R1, w1b_ref, w1bs_ref, R2),
        (two, w2f_ref, w2s_ref, R2, w2b_ref, w2bs_ref, R1),
    ):
        taps = [src[k // 3, k % 3] for k in range(9)]
        plain = jnp.concatenate(taps, axis=1)
        turned = jnp.concatenate(
            [jnp.transpose(t.astype(F32)).astype(BF) for t in taps[::-1]], axis=1
        )
        fwd[...] = plain
        bwd[...] = turned
        fwd_s[...] = stacked(plain, count)
        bwd_s[...] = stacked(turned, back)
    row = lax.broadcasted_iota(jnp.int32, (8, chans), 0)
    table = jnp.zeros((8, chans), F32)
    for k, ref in enumerate((vec0, vec1, vec2)):
        table = jnp.where(row == k, jnp.broadcast_to(ref[...].reshape(1, chans), (8, chans)), table)
    table = jnp.concatenate([table, jnp.zeros((8, 128 - chans), F32)], axis=1)
    table = jnp.concatenate([table, jnp.zeros((120, 128), F32)], axis=0)
    cond_ref[...] = jnp.transpose(table)[:chans]


def build(mesh):
    ny, nx = mesh.shape["gy"], mesh.shape["gx"]
    axes = ("gy", "gx")

    def send(value, move):
        pairs = []
        for a in range(ny):
            for b in range(nx):
                to = move(a, b)
                if 0 <= to[0] < ny and 0 <= to[1] < nx:
                    pairs.append((a * nx + b, to[0] * nx + to[1]))
        return lax.ppermute(value, axes, pairs)

    def swap(first, second, axis):
        def partner(offset):
            def move(a, b):
                v = [a, b]
                v[axis] += 1 if (v[axis] + offset) % 2 == 0 else -1
                return v

            return move

        return send(first, partner(0)), send(second, partner(1))

    def exchange(value, moves):
        got = [send(value, lambda a, b: (a ^ m[0], b ^ m[1])) for m in moves]
        if len(moves) == 1:
            return value + got[0]
        both = (moves[0][0] ^ moves[1][0], moves[0][1] ^ moves[1][1])
        far = send(value, lambda a, b: (a ^ both[0], b ^ both[1]))
        return (value + got[0]) + (got[1] + far)

    def local(
        sky, lens_phi, cotangent, tile_mask, weight_one, weight_two, cond_one, bias_one, cond_two
    ):
        chans, rows, width = sky.shape
        step = 3 * chans
        size = 4 * chans + 16
        assert 2 * rows == 128 and width == 128
        edge = jax.ShapeDtypeStruct((size, 128), BF)
        edges = jax.ShapeDtypeStruct((2, size, 128), BF)
        hbm = pl.BlockSpec(memory_space=pltpu.HBM)
        near = pl.BlockSpec(memory_space=pltpu.VMEM)
        far = [
            pltpu.with_memory_space_constraint(v, pltpu.HBM)
            for v in (sky, cotangent, lens_phi, tile_mask)
        ]
        ra, rb = pl.pallas_call(
            row_kernel,
            out_shape=(edge, edge),
            in_specs=[hbm] * 4,
            scratch_shapes=[
                pltpu.VMEM((4, chans, 16, width), BF),
                pltpu.VMEM((2, 16, width), BF),
                pltpu.VMEM(tile_mask.shape, jnp.int32),
                pltpu.SemaphoreType.DMA((7,)),
            ],
            compiler_params=limit(8),
            name="edge_rows",
        )(*far)
        ra, rb, weight_one, weight_two = lax.optimization_barrier((ra, rb, weight_one, weight_two))
        ra, rb = swap(ra, rb, 0)

        flat_w = jax.ShapeDtypeStruct((chans, 3 * step), BF)
        first_w = jax.ShapeDtypeStruct((R1 * chans, (R1 + 2) * step), BF)
        second_w = jax.ShapeDtypeStruct((R2 * chans, (R2 + 2) * step), BF)
        w1f, w2b, w2f, w1b, w1s, w2bs, w2s, w1bs, conds = pl.pallas_call(
            weight_kernel,
            out_shape=(
                flat_w, flat_w, flat_w, flat_w, first_w, first_w, second_w, second_w,
                jax.ShapeDtypeStruct((chans, 128), F32),
            ),
            in_specs=[hbm] * 5,
            scratch_shapes=[
                pltpu.VMEM(weight_one.shape, BF),
                pltpu.VMEM(weight_two.shape, BF),
                pltpu.VMEM((chans,), F32),
                pltpu.VMEM((chans,), F32),
                pltpu.VMEM((chans,), F32),
                pltpu.SemaphoreType.DMA((5,)),
            ],
            compiler_params=limit(8),
            name="weights",
        )(*[
            pltpu.with_memory_space_constraint(v, pltpu.HBM)
            for v in (weight_one, weight_two, cond_one, bias_one, cond_two)
        ])

        flops = 2 * 9 * chans * chans * rows * width
        field = jax.ShapeDtypeStruct((2, rows * step, 128), BF)
        flat = jax.ShapeDtypeStruct(lens_phi.shape, F32)
        a3, mine, gphi, phi_own, mask_own = pl.pallas_call(
            prep_kernel,
            out_shape=(field, edges, jax.ShapeDtypeStruct((chans, 128), F32), flat, flat),
            in_specs=[hbm] * 4,
            scratch_shapes=[
                pltpu.VMEM((2, 8 * chans // 2, 128), F32),
                pltpu.VMEM(sky.shape, BF),
                pltpu.VMEM(sky.shape, BF),
                pltpu.VMEM(lens_phi.shape, BF),
                pltpu.VMEM(tile_mask.shape, jnp.int32),
                pltpu.SemaphoreType.DMA((4,)),
            ],
            compiler_params=limit(8),
            cost_estimate=pl.CostEstimate(
                flops=4 * flops, bytes_accessed=8 << 20, transcendentals=0
            ),
            name="prep",
        )(*far)
        ca, cb, own, halo = pl.pallas_call(
            lambda *refs: col_kernel(rows, width, *refs),
            out_shape=(edge, edge, edges, edges),
            compiler_params=limit(8),
            name="edge_cols",
        )(mine, ra, rb)
        ca, cb = swap(ca, cb, 1)

        ring = pltpu.VMEM((4 * step, 128), BF)
        rowwise = pltpu.VMEM((rows + 8, 128), F32)
        inner = jax.ShapeDtypeStruct(((rows + 2) * chans, 128), BF)
        acc = jax.ShapeDtypeStruct((step, step), F32)
        hid, dpre, acc1, acc2, cacc = pl.pallas_call(
            hidden_kernel,
            out_shape=(inner, inner, acc, acc, jax.ShapeDtypeStruct((2, chans, 128), F32)),
            scratch_shapes=[
                pltpu.VMEM(((rows + 4) * chans, 128), BF), rowwise, rowwise, ring, ring,
            ],
            compiler_params=limit(16),
            cost_estimate=pl.CostEstimate(
                flops=8 * flops, bytes_accessed=8 << 20, transcendentals=0
            ),
            name="hidden",
        )(
            keep_near(a3), phi_own, mask_own, halo,
            w1s, w2bs, conds,
        )

        fix = jax.ShapeDtypeStruct((4 * chans, 128), F32)
        count = (2 * step + chans) // 2
        wires = jax.ShapeDtypeStruct((count, 128), F32)
        hfix, dfix, keep, give = pl.pallas_call(
            lambda *refs: edge_kernel(rows, *refs),
            out_shape=(fix, fix, wires, wires),
            scratch_shapes=[pltpu.VMEM((2 * count, 128), F32)],
            compiler_params=limit(8),
            name="edge_parts",
        )(ca, cb, own, w1f, w2b, w2f, w1b, conds, acc1, acc2, cacc, gphi)

        def output(with_phi, src, mid, fix, weights, name):
            return pl.pallas_call(
                lambda *refs: output_kernel(with_phi, *refs),
                out_shape=jax.ShapeDtypeStruct(src.shape, BF),
                scratch_shapes=[
                    pltpu.VMEM(((rows + 2) * step, 128), BF),
                    pltpu.VMEM((rows, chans, 128), F32),
                    pltpu.VMEM((chans, rows, 128), F32),
                    pltpu.VMEM(src.shape, BF),
                    pltpu.SemaphoreType.DMA(()),
                ],
                in_specs=[hbm] + [near] * 6,
                compiler_params=limit(16),
                cost_estimate=pl.CostEstimate(
                    flops=2 * flops, bytes_accessed=4 << 20, transcendentals=0
                ),
                name=name,
            )(src, phi_own, mask_own, mid, fix, weights, conds)

        moves = [(1 << k, 0) for k in range(1, ny.bit_length() - 1)]
        moves += [(0, 1 << k) for k in range(nx.bit_length() - 1)]
        rounds = [moves[:2]] + [[move] for move in moves[2:]]
        keep = keep + send(give, lambda a, b: (a ^ 1, b))
        outs = []
        for n, move in enumerate(rounds):
            if n == 0:
                keep, hfix = lax.optimization_barrier((keep, hfix))
                outs.append(output(True, far[0], hid, hfix, w2s, "delensed"))
            if n == 1:
                keep, dfix = lax.optimization_barrier((keep, dfix))
                outs.append(output(False, far[1], dpre, dfix, w1bs, "grad_input"))
            keep = exchange(keep, move)
            if n < 2:
                keep, outs[n] = lax.optimization_barrier((keep, outs[n]))
        delensed, grad_input = outs
        other = send(keep, lambda a, b: (a ^ 1, b))

        factor = float(1.0 / (rows * ny * width * nx) ** 0.5)
        grads = jax.ShapeDtypeStruct((3, 3, chans, chans), F32)
        grad_w1, grad_w2, grad_cond = pl.pallas_call(
            lambda *refs: unpack_kernel(factor, *refs),
            out_shape=(grads, grads, jax.ShapeDtypeStruct((3, chans), F32)),
            scratch_shapes=[pltpu.VMEM((2 * count, 128), F32)],
            compiler_params=limit(8),
            name="unpack",
        )(keep, other)
        return delensed, grad_input, grad_w1, grad_w2, grad_cond

    return local


def solution(mesh):
    return jax.shard_map(
        build(mesh),
        mesh=mesh,
        in_specs=(
            P(None, "gy", "gx"),
            P("gy", "gx"),
            P(None, "gy", "gx"),
            P("gy", "gx"),
            P(),
            P(),
            P(),
            P(),
            P(),
        ),
        out_specs=(P(None, "gy", "gx"), P(None, "gy", "gx"), P(), P(), P()),
        check_vma=False,
    )
```

```python
import jax
import jax.numpy as jnp
from jax import lax
from jax.experimental import pallas as pl
from jax.experimental.pallas import tpu as pltpu
from jax.sharding import PartitionSpec as P

TILE = 8
BF = jnp.bfloat16
F32 = jnp.float32
NT = (((1,), (1,)), ((), ()))
NN = (((1,), (0,)), ((), ()))
TN = (((0,), (0,)), ((), ()))
R1 = 3
R2 = 4
GROUP1 = 6
GROUP2 = 8


def lane_iota(rows):
    return lax.broadcasted_iota(jnp.int32, (rows, 128), 1)


def tile_rows(mask_ref):
    tcols = mask_ref.shape[1]
    lane = lax.broadcasted_iota(jnp.int32, (tcols, 128), 1)
    row = lax.broadcasted_iota(jnp.int32, (tcols, 128), 0)
    spread = (lane // TILE == row).astype(F32).astype(BF)
    return lax.dot_general(
        mask_ref[...].astype(F32).astype(BF), spread, NN, preferred_element_type=F32
    )


def is_odd(axis):
    return lax.rem(lax.axis_index(axis), 2) == 1


def received(axis, count, a_ref, b_ref):
    ends = (lax.axis_index(axis) == 0) | (lax.axis_index(axis) == count - 1)
    ra = a_ref[...]
    rb = jnp.where(ends, jnp.zeros_like(ra), b_ref[...])
    odd = is_odd(axis)
    return jnp.where(odd, ra, rb), jnp.where(odd, rb, ra)


def row_kernel(sky_ref, cot_ref, phi_ref, mask_ref, a_ref, b_ref, blocks, phis, tiles, sems):
    chans, rows, _ = sky_ref.shape
    copies = []
    for n, (src, dst) in enumerate(
        [
            (ref.at[:, pl.ds(first, 16), :], blocks.at[k])
            for k, (ref, first) in enumerate(
                ((sky_ref, 0), (cot_ref, 0), (sky_ref, rows - 16), (cot_ref, rows - 16))
            )
        ]
        + [(phi_ref.at[pl.ds(0, 16), :], phis.at[0]), (phi_ref.at[pl.ds(rows - 16, 16), :], phis.at[1])]
        + [(mask_ref, tiles)]
    ):
        copies.append(pltpu.make_async_copy(src, dst, sems.at[n]))
        copies[-1].start()
    for copy in copies:
        copy.wait()
    cells = tile_rows(tiles)
    odd = is_odd("gy")
    parts = []
    for side, (first, mrow) in enumerate(((0, 0), (14, tiles.shape[0] - 1))):
        keep = cells[mrow : mrow + 1]
        low = jnp.broadcast_to(keep, (chans, 128)).astype(BF)
        part = []
        for k in range(2):
            block = jnp.transpose(blocks[2 * side + k], (1, 0, 2))
            part += [block[first] * low, block[first + 1] * low]
        row = lax.broadcasted_iota(jnp.int32, (16, 128), 0)
        prow = phis[side].astype(F32)[15 * side : 15 * side + 1]
        prow = jnp.broadcast_to(prow, (16, 128))
        part.append(jnp.where(row == 0, prow, jnp.where(row == 1, keep, 0.0)).astype(BF))
        parts.append(jnp.concatenate(part, axis=0))
    up, down = parts
    a_ref[...] = jnp.where(odd, up, down)
    b_ref[...] = jnp.where(odd, down, up)


def prep_kernel(*refs):
    far, (a3, own_ref, gphi_ref, phix, maskx), mats = refs[:9], refs[9:14], refs[14:23]
    strip, near, sems = refs[23], refs[24:33], refs[33]
    copies = {
        n: pltpu.make_async_copy(far[n], near[n], sems.at[n])
        for n in (3, 2, 4, 5, 6, 7, 8, 0, 1)
    }
    for copy in copies.values():
        copy.start()
    for n in (3, 2, 4, 5, 6, 7, 8):
        copies[n].wait()
    weight_matrices(*near[4:], *mats)
    copies[0].wait()
    copies[1].wait()
    own_fields(*near[:4], a3, own_ref, gphi_ref, phix, maskx, strip)


def own_fields(
    sky_ref, cot_ref, phi_ref, mask_ref, a3, own_ref, gphi_ref, phix, maskx, strip
):
    chans, rows, width = sky_ref.shape
    size = own_ref.shape[1]
    step = 3 * chans
    half = chans // 2
    cells = tile_rows(mask_ref)
    phi = phi_ref[...].astype(F32)
    phix[...] = phi
    for t in range(mask_ref.shape[0]):
        maskx[TILE * t : TILE * (t + 1)] = jnp.broadcast_to(cells[t : t + 1], (TILE, 128))
    lane8 = lane_iota(8)
    row8 = lax.broadcasted_iota(jnp.int32, (8, 128), 0)
    pick = ((row8 < 2) & (lane8 == row8)) | (
        (row8 >= 2) & (row8 < 4) & (lane8 == row8 + (width - 4))
    )
    pick = pick.astype(F32).astype(BF)
    trows, tcols = mask_ref.shape
    prow = lax.broadcasted_iota(jnp.int32, (8, tcols), 0)
    pcol = lax.broadcasted_iota(jnp.int32, (8, tcols), 1)
    pick_t = ((prow < 2) & (pcol == 0)) | ((prow >= 2) & (prow < 4) & (pcol == tcols - 1))
    edge = lax.dot_general(
        pick_t.astype(F32).astype(BF),
        mask_ref[...].astype(F32).astype(BF),
        NT,
        preferred_element_type=F32,
    )
    lane_t = lax.broadcasted_iota(jnp.int32, (trows, 128), 1)
    row_t = lax.broadcasted_iota(jnp.int32, (trows, 128), 0)
    spread = (lane_t // TILE == row_t).astype(F32).astype(BF)
    keep = lax.dot_general(edge.astype(BF), spread, NN, preferred_element_type=F32)
    phis = lax.dot_general(pick, phi_ref[...], NT, preferred_element_type=F32)
    phis = jnp.concatenate([phis, jnp.zeros((8, 128 - rows), F32)], axis=1)
    gphi = jnp.zeros((chans, 128), F32)
    for which, src in ((0, sky_ref), (1, cot_ref)):
        both = jnp.concatenate([src[:half], src[half:]], axis=1).reshape(half * 128, width)
        flat = lax.dot_general(pick, both, NT, preferred_element_type=F32)
        for j in range(half):
            strip[which, 8 * j : 8 * j + 8] = flat[:, 128 * j : 128 * j + 128]
        for k in range(4):
            part = strip[which, pl.ds(k, half, stride=8), :]
            col = jnp.concatenate([part, pltpu.roll(part, 64, 1)], axis=0)
            base = (2 * which + k % 2) * chans
            own_ref[k // 2, base : base + chans] = (col * keep[k : k + 1]).astype(BF)
        for j in range(rows // 16):
            block = jnp.transpose(src[:, 16 * j : 16 * j + 16, :], (1, 0, 2))
            for t in range(2):
                low = jnp.broadcast_to(cells[2 * j + t : 2 * j + t + 1], (chans, 128)).astype(BF)
                for n in range(TILE):
                    y = 16 * j + TILE * t + n
                    value = block[TILE * t + n] * low
                    a3[which, y * step : (y + 1) * step] = three_copies(value)
                    if which:
                        gphi = gphi + value.astype(F32) * phi[y : y + 1]
    gphi_ref[...] = gphi
    row = lax.broadcasted_iota(jnp.int32, (16, 128), 0)
    for side, k in ((0, 0), (1, 3)):
        extra = jnp.where(
            row == 0,
            jnp.broadcast_to(phis[k : k + 1], (16, 128)),
            jnp.where(row == 1, jnp.broadcast_to(keep[k : k + 1], (16, 128)), 0.0),
        )
        own_ref[side, 4 * chans : size] = extra.astype(BF)


def three_copies(value):
    return jnp.concatenate([pltpu.roll(value, 1, 1), value, pltpu.roll(value, 127, 1)], axis=0)


def col_kernel(rows, width, count, mine_ref, a_ref, b_ref, sa_ref, sb_ref, own_ref, halo_ref):
    size = a_ref.shape[0]
    tops, bots = received("gy", count, a_ref, b_ref)
    halo_ref[0] = tops
    halo_ref[1] = bots
    chans = (size - 16) // 4
    lane = lane_iota(chans)
    lane16 = lane_iota(16)
    sides = []
    for side in range(2):
        parts = []
        for m in range(4):
            which, k = divmod(m, 2)
            at = k + (width - 2) * side
            col = mine_ref[side, m * chans : (m + 1) * chans]
            for value, where in ((tops, (126, 127)), (bots, (rows, rows + 1))):
                for n in range(2):
                    base = (2 * which + n) * chans
                    cell = value[base : base + chans, at : at + 1]
                    col = jnp.where(lane == where[n], jnp.broadcast_to(cell, col.shape), col)
            parts.append(col)
        at = (width - 1) * side
        extra = mine_ref[side, 4 * chans : size].astype(F32)
        for value, where in ((tops, 127), (bots, rows)):
            cell = value[4 * chans : size].astype(F32)[:, at : at + 1]
            extra = jnp.where(lane16 == where, jnp.broadcast_to(cell, (16, 128)), extra)
        parts.append(extra.astype(BF))
        sides.append(jnp.concatenate(parts, axis=0))
        own_ref[side] = sides[side]
    odd_x = is_odd("gx")
    sa_ref[...] = jnp.where(odd_x, sides[0], sides[1])
    sb_ref[...] = jnp.where(odd_x, sides[1], sides[0])


def silu_parts(pre):
    sigma = 1.0 / (1.0 + jnp.exp(-pre))
    return pre * sigma, sigma * (1.0 + pre * (1.0 - sigma))


def hidden_kernel(
    a3, phi_own, mask_own, halo_ref, w1s_ref, w2ts_ref, cond_ref,
    hid_ref, dpre_ref, acc1, acc2, cacc,
    dz, phix, maskx, ringx, ringg,
):
    rows, width = phi_own.shape
    a3x, a3g = a3.at[0], a3.at[1]
    size = halo_ref.shape[1]
    chans = (size - 16) // 4
    step = 3 * chans
    lane1 = lane_iota(1)
    inside = jnp.where((lane1 == 0) | (lane1 == 127), 0.0, 1.0)
    for k, at in ((0, 0), (1, rows + 1)):
        extra = halo_ref[k, 4 * chans : size].astype(F32)
        phix[at : at + 1] = extra[0:1]
        maskx[at : at + 1] = extra[1:2] * inside
    phix[1 : rows + 1] = phi_own[...]
    maskx[1 : rows + 1] = mask_own[...] * inside
    for which, ring in ((0, ringx), (1, ringg)):
        for k in range(2):
            for n in range(2):
                base = (2 * which + n) * chans
                ring[(2 * k + n) * step : (2 * k + n + 1) * step] = three_copies(
                    halo_ref[k, base : base + chans]
                )

    def window(own, ring, y, count):
        parts = []
        if y < 0:
            parts.append(ring[(y + 2) * step : min(2, y + 2 + count) * step])
        low, high = max(y, 0), min(y + count, rows)
        if low < high:
            parts.append(own[low * step : high * step])
        if y + count > rows:
            low = max(y, rows) - rows
            parts.append(ring[(2 + low) * step : (2 + y + count - rows) * step])
        return parts[0] if len(parts) == 1 else jnp.concatenate(parts, axis=0)

    gain = cond_ref[:, 0:1]
    bias = cond_ref[:, 1:2]
    split = (rows + 2) // 2
    zero = jnp.zeros((chans, 128), BF)
    for y in (-2, -1, rows, rows + 1):
        dz[(y + 2) * chans : (y + 3) * chans] = zero

    def first_pass(it, dphi, dsum):
        y0 = R1 * it - 1

        def both(own, ring):
            pair = [window(own, ring, y0 - 1 + h * split, R1 + 2) for h in range(2)]
            return jnp.concatenate(pair, axis=1)

        pre = lax.dot_general(w1s_ref[...], both(a3x, ringx), NN, preferred_element_type=F32)
        back = lax.dot_general(w2ts_ref[...], both(a3g, ringg), NN, preferred_element_type=F32)
        for h in range(2):
            for r in range(R1):
                row = y0 + h * split + r + 1
                here = (slice(r * chans, (r + 1) * chans), slice(h * 128, h * 128 + 128))
                keep = maskx[row : row + 1]
                act, slope = silu_parts(pre[here] + gain * phix[row : row + 1] + bias)
                base = row * chans
                hid_ref[base : base + chans] = (act * keep).astype(BF)
                value = (back[here] * keep * slope).astype(BF)
                dpre_ref[base : base + chans] = value
                if 1 <= row <= rows:
                    dz[base + chans : base + 2 * chans] = value
                    wide = value.astype(F32)
                    dphi = dphi + wide * phix[row : row + 1]
                    dsum = dsum + wide
        return dphi, dsum

    dphi = jnp.zeros((chans, 128), F32)
    dsum = jnp.zeros((chans, 128), F32)
    for it in range(split // R1):
        dphi, dsum = first_pass(it, dphi, dsum)
    cacc[0] = dphi
    cacc[1] = dsum

    acc1[...] = jnp.zeros_like(acc1)
    acc2[...] = jnp.zeros_like(acc2)

    def rows_of(src, start, size):
        return src[start : start + size]

    def grads_one(it):
        ys = [GROUP1 * it + n - 1 for n in range(GROUP1)]
        acc1[...] += lax.dot_general(
            jnp.concatenate([rows_of(dz, (y + 1) * chans, step) for y in ys], axis=1),
            jnp.concatenate([window(a3x, ringx, y, 1) for y in ys], axis=1),
            NT, preferred_element_type=F32,
        )

    def grads_two(it):
        ys = [GROUP2 * it + n for n in range(GROUP2)]
        acc2[...] += lax.dot_general(
            jnp.concatenate([window(a3g, ringg, y, 1) for y in ys], axis=1),
            jnp.concatenate([rows_of(hid_ref, y * chans, step) for y in ys], axis=1),
            NT, preferred_element_type=F32,
        )

    for it in range((rows + 2) // GROUP1):
        grads_one(it)
    for it in range(rows // GROUP2):
        grads_two(it)


def edge_kernel(
    rows, count, a_ref, b_ref, own_ref, w1c_ref, w2tc_ref, cond_ref,
    acc1, acc2, cacc, gphi_ref,
    hcol_ref, dcol_ref, keep_ref, give_ref, wire,
):
    size = a_ref.shape[0]
    chans = (size - 16) // 4
    step = 3 * chans
    lft, rgt = received("gx", count, a_ref, b_ref)
    own_l, own_r = own_ref[0], own_ref[1]

    def at(value, which, n):
        base = (2 * which + n) * chans
        return value[base : base + chans]

    def columns(which):
        return [at(v, which, n) for v in (lft, own_l, own_r, rgt) for n in range(2)]

    centres = (1, 2, 5, 6)

    def taps_of(cols):
        pieces = []
        for ky in range(3):
            moved = [c if ky == 1 else pltpu.roll(c, (1, 0, 127)[ky], 1) for c in cols]
            for kx in range(3):
                pieces.append(jnp.concatenate([moved[c + kx - 1] for c in centres], axis=1))
        return jnp.concatenate(pieces, axis=0)

    x_taps = taps_of(columns(0))
    g_cols = columns(1)
    extra = [v[4 * chans : size].astype(F32) for v in (lft, own_l, own_r, rgt)]
    phi_c = jnp.concatenate([e[0:1] for e in extra], axis=1)
    mask_c = jnp.concatenate([e[1:2] for e in extra], axis=1)
    pre = lax.dot_general(w1c_ref[...], x_taps, NN, preferred_element_type=F32)
    back = lax.dot_general(w2tc_ref[...], taps_of(g_cols), NN, preferred_element_type=F32)
    act, slope = silu_parts(pre + cond_ref[:, 0:1] * phi_c + cond_ref[:, 1:2])
    hcol = (act * mask_c).astype(BF)
    dcol = (back * mask_c * slope).astype(BF)
    hcol_ref[...] = hcol
    dcol_ref[...] = dcol

    mine = jnp.broadcast_to((lane_iota(1) < rows).astype(F32), (chans, 128)).astype(BF)
    d_own = [dcol[:, 128:256] * mine, dcol[:, 256:384] * mine]
    part1 = lax.dot_general(
        jnp.concatenate(d_own, axis=1), x_taps[:, 128:384], NT, preferred_element_type=F32
    )
    h_cols = [hcol[:, 128 * k : 128 * k + 128] for k in range(4)]
    g_own = {k: g_cols[n] * mine for k, n in ((0, 2), (1, 3), (2, 4), (3, 5))}
    for kx, pairs in (
        (0, ((0, 0), (1, 1))),
        (1, ((0, 1), (3, 2))),
        (2, ((2, 2), (3, 3))),
    ):
        lhs = jnp.concatenate([g_own[g] for g, _ in pairs], axis=1)
        rhs = []
        for ky in range(3):
            moved = [
                h_cols[h] if ky == 1 else pltpu.roll(h_cols[h], (1, 0, 127)[ky], 1)
                for _, h in pairs
            ]
            rhs.append(jnp.concatenate(moved, axis=1))
        part2 = lax.dot_general(
            lhs, jnp.concatenate(rhs, axis=0), NT, preferred_element_type=F32
        )
        low = (2 - kx) * chans
        wide = jnp.concatenate(
            [
                acc1[low : low + chans] + part1[:, kx * step : (kx + 1) * step],
                acc2[low : low + chans] + part2,
            ],
            axis=1,
        )
        wire[low : low + chans] = wide[:, :128]
        wire[step + low : step + low + chans] = wide[:, 128:256]
        if kx == 0:
            tails = []
        tails.insert(0, wide[:, 256 : 2 * step])
    dphi, dsum = cacc[0], cacc[1]
    for d, k in ((d_own[0], 1), (d_own[1], 2)):
        dphi = dphi + d.astype(F32) * extra[k][0:1]
        dsum = dsum + d.astype(F32)
    sums = [jnp.sum(v, axis=1, keepdims=True) for v in (dphi, dsum, gphi_ref[...])]
    fill = jnp.zeros((chans, 128 - 3 * tails[0].shape[1] - 3), F32)
    wire[2 * step : 2 * step + chans] = jnp.concatenate(tails + sums + [fill], axis=1)
    half = wire.shape[0] // 2
    core = lax.rem(lax.axis_index("gy"), 2)
    keep_ref[...] = wire[pl.ds(pl.multiple_of(core * half, 8), half), :]
    give_ref[...] = wire[pl.ds(pl.multiple_of((1 - core) * half, 8), half), :]


def fix_kernel(rows, w2c_ref, w1tc_ref, hcol_ref, dcol_ref, hfix_ref, dfix_ref):
    chans = hcol_ref.shape[0]
    none = jnp.zeros((chans, 128), BF)
    half = chans // 2
    lane = lane_iota(half)
    for weights, field, fix in ((w2c_ref, hcol_ref, hfix_ref), (w1tc_ref, dcol_ref, dfix_ref)):
        f = [field[:, 128 * k : 128 * k + 128] for k in range(4)]
        pieces = []
        for ky in range(3):
            m = [c if ky == 1 else pltpu.roll(c, (1, 0, 127)[ky], 1) for c in f]
            pieces.append(jnp.concatenate([m[0], m[1], none, none], axis=1))
            pieces.append(jnp.concatenate([m[1], none, none, m[2]], axis=1))
            pieces.append(jnp.concatenate([none, none, m[2], m[3]], axis=1))
        fixes = lax.dot_general(
            weights[...], jnp.concatenate(pieces, axis=0), NN, preferred_element_type=F32
        )
        for k in range(4):
            col = fixes[:, 128 * k : 128 * k + 128]
            part = jnp.where(lane < rows, col[:half], pltpu.roll(col[half:], rows, 1))
            high = part.astype(BF).astype(F32)
            fix[pl.ds(k, half, stride=8), :] = high
            fix[pl.ds(4 + k, half, stride=8), :] = part - high


def output_kernel(
    with_phi, src_hbm, phi_ref, mask_ref, mid_ref, fix_ref, weights_ref, cond_ref,
    out_ref, a3, rowbuf, fixbuf, src_ref, sem,
):
    chans, rows, width = src_ref.shape
    step = 3 * chans
    half = chans // 2
    fetch = pltpu.make_async_copy(src_hbm, src_ref, sem)
    fetch.start()
    if with_phi:
        gain = cond_ref[:, 2:3]
    lane8 = lane_iota(8)
    row8 = lax.rem(lax.broadcasted_iota(jnp.int32, (8, 128), 0), 4)
    place = (lane8 == jnp.where(row8 < 2, row8, row8 + (width - 4))).astype(F32).astype(BF)
    for j in range(half):
        got = lax.dot_general(
            fix_ref[8 * j : 8 * j + 8].astype(BF), place, TN, preferred_element_type=F32
        )
        fixbuf[j] = got[:rows]
        fixbuf[j + half] = got[rows:]

    for y in range(rows + 2):
        centre = mid_ref[y * chans : (y + 1) * chans]
        base = y * step
        a3[base : base + chans] = pltpu.roll(centre, 1, 1)
        a3[base + chans : base + 2 * chans] = centre
        a3[base + 2 * chans : base + 3 * chans] = pltpu.roll(centre, 127, 1)

    for it in range(rows // (2 * R2)):
        y0 = R2 * it
        got = lax.dot_general(
            weights_ref[...],
            jnp.concatenate(
                [a3[(y0 + h) * step : (y0 + h + R2 + 2) * step] for h in (0, rows // 2)], axis=1
            ),
            NN, preferred_element_type=F32,
        )
        for h in range(2):
            for r in range(R2):
                y = y0 + h * (rows // 2) + r
                part = got[r * chans : (r + 1) * chans, h * 128 : h * 128 + 128]
                if with_phi:
                    part = part + gain * phi_ref[y : y + 1]
                rowbuf[y] = part

    fetch.wait()
    for j in range(rows // 16):
        here = slice(16 * j, 16 * j + 16)
        keep = mask_ref[here]
        total = jnp.transpose(rowbuf[here], (1, 0, 2)) + fixbuf[:, here, :]
        out_ref[:, here, :] = ((total + src_ref[:, here, :].astype(F32)) * keep[None]).astype(BF)


def unpack_kernel(factor, keep_ref, other_ref, w1_ref, w2_ref, cond_ref, wire):
    chans = w1_ref.shape[2]
    step = 3 * chans
    count = keep_ref.shape[0]
    core = lax.rem(lax.axis_index("gy"), 2)
    wire[pl.ds(pl.multiple_of(core * count, 8), count), :] = keep_ref[...]
    wire[pl.ds(pl.multiple_of((1 - core) * count, 8), count), :] = other_ref[...]
    tail = wire[2 * step : 2 * step + chans] * factor
    rest_w = 2 * step - 256
    for n in range(3):
        low = n * chans
        wide = jnp.concatenate(
            [
                wire[low : low + chans] * factor,
                wire[step + low : step + low + chans] * factor,
                tail[:, n * rest_w : (n + 1) * rest_w],
            ],
            axis=1,
        )
        for k in range(3):
            w1_ref[2 - n, k] = wide[:, k * chans : (k + 1) * chans]
            w2_ref[k, 2 - n] = wide[:, step + k * chans : step + (k + 1) * chans]
    cond_ref[...] = jnp.transpose(tail)[3 * rest_w : 3 * rest_w + 3, :chans]


def limit(mib):
    return pltpu.CompilerParams(vmem_limit_bytes=mib << 20)


def keep_near(value):
    return pltpu.with_memory_space_constraint(value, pltpu.VMEM)


def stacked(block, count):
    chans, taps = block.shape
    step = taps // 3
    rows = []
    for r in range(count):
        parts = [block]
        if r:
            parts.insert(0, jnp.zeros((chans, r * step), BF))
        if r < count - 1:
            parts.append(jnp.zeros((chans, (count - 1 - r) * step), BF))
        rows.append(jnp.concatenate(parts, axis=1))
    return jnp.concatenate(rows, axis=0)


def weight_matrices(
    one, two, vec0, vec1, vec2,
    w1f_ref, w2b_ref, w2f_ref, w1b_ref, w1s_ref, w2bs_ref, w2s_ref, w1bs_ref, cond_ref,
):
    chans = one.shape[2]
    for src, fwd, fwd_s, count, bwd, bwd_s, back in (
        (one, w1f_ref, w1s_ref, R1, w1b_ref, w1bs_ref, R2),
        (two, w2f_ref, w2s_ref, R2, w2b_ref, w2bs_ref, R1),
    ):
        taps = [src[k // 3, k % 3] for k in range(9)]
        plain = jnp.concatenate(taps, axis=1)
        turned = jnp.concatenate(
            [jnp.transpose(t.astype(F32)).astype(BF) for t in taps[::-1]], axis=1
        )
        fwd[...] = plain
        bwd[...] = turned
        fwd_s[...] = stacked(plain, count)
        bwd_s[...] = stacked(turned, back)
    row = lax.broadcasted_iota(jnp.int32, (8, chans), 0)
    table = jnp.zeros((8, chans), F32)
    for k, ref in enumerate((vec0, vec1, vec2)):
        table = jnp.where(row == k, jnp.broadcast_to(ref[...].reshape(1, chans), (8, chans)), table)
    table = jnp.concatenate([table, jnp.zeros((8, 128 - chans), F32)], axis=1)
    table = jnp.concatenate([table, jnp.zeros((120, 128), F32)], axis=0)
    cond_ref[...] = jnp.transpose(table)[:chans]


def build(mesh):
    ny, nx = mesh.shape["gy"], mesh.shape["gx"]
    axes = ("gy", "gx")

    def send(value, move):
        pairs = []
        for a in range(ny):
            for b in range(nx):
                to = move(a, b)
                pairs.append((a * nx + b, to[0] * nx + to[1]))
        return lax.ppermute(value, axes, pairs)

    def swap(first, second, axis):
        def partner(offset):
            def move(a, b):
                v = [a, b]
                v[axis] += 1 if (v[axis] + offset) % 2 == 0 else -1
                if 0 <= v[axis] < (ny, nx)[axis]:
                    return v
                return (a, b ^ 1) if axis == 0 else (a ^ 1, b)

            return move

        return send(first, partner(0)), send(second, partner(1))

    def exchange(value, moves):
        got = [send(value, lambda a, b: (a ^ m[0], b ^ m[1])) for m in moves]
        if len(moves) == 1:
            return value + got[0]
        both = (moves[0][0] ^ moves[1][0], moves[0][1] ^ moves[1][1])
        far = send(value, lambda a, b: (a ^ both[0], b ^ both[1]))
        return (value + got[0]) + (got[1] + far)

    def local(
        sky, lens_phi, cotangent, tile_mask, weight_one, weight_two, cond_one, bias_one, cond_two
    ):
        chans, rows, width = sky.shape
        step = 3 * chans
        size = 4 * chans + 16
        assert 2 * rows == 128 and width == 128
        edge = jax.ShapeDtypeStruct((size, 128), BF)
        edges = jax.ShapeDtypeStruct((2, size, 128), BF)
        hbm = pl.BlockSpec(memory_space=pltpu.HBM)
        far = [
            pltpu.with_memory_space_constraint(v, pltpu.HBM)
            for v in (
                sky, cotangent, lens_phi, tile_mask,
                weight_one, weight_two, cond_one, bias_one, cond_two,
            )
        ]
        vmem = pl.BlockSpec(memory_space=pltpu.VMEM)
        ra, rb = pl.pallas_call(
            row_kernel,
            out_shape=(edge, edge),
            in_specs=[hbm] * 4,
            scratch_shapes=[
                pltpu.VMEM((4, chans, 16, width), BF),
                pltpu.VMEM((2, 16, width), BF),
                pltpu.VMEM(tile_mask.shape, jnp.int32),
                pltpu.SemaphoreType.DMA((7,)),
            ],
            compiler_params=limit(8),
            name="edge_rows",
        )(*far[:4])
        ra, rb = swap(ra, rb, 0)

        flat_w = jax.ShapeDtypeStruct((chans, 3 * step), BF)
        first_w = jax.ShapeDtypeStruct((R1 * chans, (R1 + 2) * step), BF)
        second_w = jax.ShapeDtypeStruct((R2 * chans, (R2 + 2) * step), BF)
        matrices = (
            flat_w, flat_w, flat_w, flat_w, first_w, first_w, second_w, second_w,
            jax.ShapeDtypeStruct((chans, 128), F32),
        )
        flops = 2 * 9 * chans * chans * rows * width
        field = jax.ShapeDtypeStruct((2, rows * step, 128), BF)
        flat = jax.ShapeDtypeStruct(lens_phi.shape, F32)
        a3, mine, gphi, phi_own, mask_own, *matrices = pl.pallas_call(
            prep_kernel,
            out_shape=(field, edges, jax.ShapeDtypeStruct((chans, 128), F32), flat, flat)
            + matrices,
            in_specs=[hbm] * 9,
            scratch_shapes=[pltpu.VMEM((2, 8 * chans // 2, 128), F32)]
            + [pltpu.VMEM(v.shape, v.dtype) for v in far]
            + [pltpu.SemaphoreType.DMA((9,))],
            compiler_params=limit(8),
            cost_estimate=pl.CostEstimate(
                flops=4 * flops, bytes_accessed=8 << 20, transcendentals=0
            ),
            name="prep",
        )(*far)
        w1f, w2b, w2f, w1b, w1s, w2bs, w2s, w1bs, conds = matrices
        ca, cb, own, halo = pl.pallas_call(
            lambda *refs: col_kernel(rows, width, ny, *refs),
            out_shape=(edge, edge, edges, edges),
            compiler_params=limit(8),
            name="edge_cols",
        )(mine, ra, rb)
        ca, cb = swap(ca, cb, 1)

        ring = pltpu.VMEM((4 * step, 128), BF)
        rowwise = pltpu.VMEM((rows + 8, 128), F32)
        inner = jax.ShapeDtypeStruct(((rows + 2) * chans, 128), BF)
        acc = jax.ShapeDtypeStruct((step, step), F32)
        hid, dpre, acc1, acc2, cacc = pl.pallas_call(
            hidden_kernel,
            out_shape=(inner, inner, acc, acc, jax.ShapeDtypeStruct((2, chans, 128), F32)),
            scratch_shapes=[
                pltpu.VMEM(((rows + 4) * chans, 128), BF), rowwise, rowwise, ring, ring,
            ],
            compiler_params=limit(16),
            cost_estimate=pl.CostEstimate(
                flops=8 * flops, bytes_accessed=8 << 20, transcendentals=0
            ),
            name="hidden",
        )(
            keep_near(a3), phi_own, mask_own, halo,
            w1s, w2bs, conds,
        )

        fix = jax.ShapeDtypeStruct((4 * chans, 128), F32)
        count = (2 * step + chans) // 2
        wires = jax.ShapeDtypeStruct((count, 128), F32)
        cols = jax.ShapeDtypeStruct((chans, 512), BF)
        hcol, dcol, keep, give = pl.pallas_call(
            lambda *refs: edge_kernel(rows, nx, *refs),
            out_shape=(cols, cols, wires, wires),
            scratch_shapes=[pltpu.VMEM((2 * count, 128), F32)],
            compiler_params=limit(8),
            name="edge_parts",
        )(ca, cb, own, w1f, w2b, conds, acc1, acc2, cacc, gphi)
        hfix, dfix = pl.pallas_call(
            lambda *refs: fix_kernel(rows, *refs),
            out_shape=(fix, fix),
            compiler_params=limit(8),
            cost_estimate=pl.CostEstimate(
                flops=flops // 2, bytes_accessed=1 << 20, transcendentals=0
            ),
            name="edge_fixes",
        )(w2f, w1b, hcol, dcol)

        def output(with_phi, src, mid, fix, weights, name):
            return pl.pallas_call(
                lambda *refs: output_kernel(with_phi, *refs),
                out_shape=jax.ShapeDtypeStruct(src.shape, BF),
                scratch_shapes=[
                    pltpu.VMEM(((rows + 2) * step, 128), BF),
                    pltpu.VMEM((rows, chans, 128), F32),
                    pltpu.VMEM((chans, rows, 128), F32),
                    pltpu.VMEM(src.shape, BF),
                    pltpu.SemaphoreType.DMA(()),
                ],
                in_specs=[hbm] + [vmem] * 6,
                compiler_params=limit(16),
                cost_estimate=pl.CostEstimate(
                    flops=2 * flops, bytes_accessed=4 << 20, transcendentals=0
                ),
                name=name,
            )(src, phi_own, mask_own, mid, fix, weights, conds)

        moves = [(1 << k, 0) for k in range(1, ny.bit_length() - 1)]
        moves += [(0, 1 << k) for k in range(nx.bit_length() - 1)]
        rounds = [moves[:2]] + [[move] for move in moves[2:]]
        keep = keep + send(give, lambda a, b: (a ^ 1, b))
        outs = []
        for n, move in enumerate(rounds):
            if n == 0:
                keep, hfix = lax.optimization_barrier((keep, hfix))
                outs.append(output(True, far[0], hid, hfix, w2s, "delensed"))
            if n == 1:
                keep, dfix = lax.optimization_barrier((keep, dfix))
                outs.append(output(False, far[1], dpre, dfix, w1bs, "grad_input"))
            keep = exchange(keep, move)
            if n < 2:
                keep, outs[n] = lax.optimization_barrier((keep, outs[n]))
        delensed, grad_input = outs
        other = send(keep, lambda a, b: (a ^ 1, b))

        factor = float(1.0 / (rows * ny * width * nx) ** 0.5)
        grads = jax.ShapeDtypeStruct((3, 3, chans, chans), F32)
        grad_w1, grad_w2, grad_cond = pl.pallas_call(
            lambda *refs: unpack_kernel(factor, *refs),
            out_shape=(grads, grads, jax.ShapeDtypeStruct((3, chans), F32)),
            scratch_shapes=[pltpu.VMEM((2 * count, 128), F32)],
            compiler_params=limit(8),
            name="unpack",
        )(keep, other)
        return delensed, grad_input, grad_w1, grad_w2, grad_cond

    return local


def solution(mesh):
    return jax.shard_map(
        build(mesh),
        mesh=mesh,
        in_specs=(
            P(None, "gy", "gx"),
            P("gy", "gx"),
            P(None, "gy", "gx"),
            P("gy", "gx"),
            P(),
            P(),
            P(),
            P(),
            P(),
        ),
        out_specs=(P(None, "gy", "gx"), P(None, "gy", "gx"), P(), P(), P()),
        check_vma=False,
    )
```

```python
import jax
import jax.numpy as jnp
from jax import lax
from jax.experimental import pallas as pl
from jax.experimental.pallas import tpu as pltpu
from jax.sharding import PartitionSpec as P

TILE = 8
BF = jnp.bfloat16
F32 = jnp.float32
NT = (((1,), (1,)), ((), ()))
NN = (((1,), (0,)), ((), ()))
TN = (((0,), (0,)), ((), ()))
R1 = 3
R2 = 4
GROUP1 = 6
GROUP2 = 8


def lane_iota(rows):
    return lax.broadcasted_iota(jnp.int32, (rows, 128), 1)


def tile_rows(mask_ref):
    tcols = mask_ref.shape[1]
    lane = lax.broadcasted_iota(jnp.int32, (tcols, 128), 1)
    row = lax.broadcasted_iota(jnp.int32, (tcols, 128), 0)
    spread = (lane // TILE == row).astype(F32).astype(BF)
    return lax.dot_general(
        mask_ref[...].astype(F32).astype(BF), spread, NN, preferred_element_type=F32
    )


def is_odd(axis):
    return lax.rem(lax.axis_index(axis), 2) == 1


def received(axis, count, a_ref, b_ref):
    ends = (lax.axis_index(axis) == 0) | (lax.axis_index(axis) == count - 1)
    ra = a_ref[...]
    rb = jnp.where(ends, jnp.zeros_like(ra), b_ref[...])
    odd = is_odd(axis)
    return jnp.where(odd, ra, rb), jnp.where(odd, rb, ra)


def row_kernel(sky_ref, cot_ref, phi_ref, mask_ref, a_ref, b_ref, blocks, phis, tiles, sems):
    chans, rows, _ = sky_ref.shape
    copies = []
    for n, (src, dst) in enumerate(
        [
            (ref.at[:, pl.ds(first, 16), :], blocks.at[k])
            for k, (ref, first) in enumerate(
                ((sky_ref, 0), (cot_ref, 0), (sky_ref, rows - 16), (cot_ref, rows - 16))
            )
        ]
        + [(phi_ref.at[pl.ds(0, 16), :], phis.at[0]), (phi_ref.at[pl.ds(rows - 16, 16), :], phis.at[1])]
        + [(mask_ref, tiles)]
    ):
        copies.append(pltpu.make_async_copy(src, dst, sems.at[n]))
        copies[-1].start()
    for copy in copies:
        copy.wait()
    cells = tile_rows(tiles)
    odd = is_odd("gy")
    parts = []
    for side, (first, mrow) in enumerate(((0, 0), (14, tiles.shape[0] - 1))):
        keep = cells[mrow : mrow + 1]
        low = jnp.broadcast_to(keep, (chans, 128)).astype(BF)
        part = []
        for k in range(2):
            block = jnp.transpose(blocks[2 * side + k], (1, 0, 2))
            part += [block[first] * low, block[first + 1] * low]
        row = lax.broadcasted_iota(jnp.int32, (16, 128), 0)
        prow = phis[side].astype(F32)[15 * side : 15 * side + 1]
        prow = jnp.broadcast_to(prow, (16, 128))
        part.append(jnp.where(row == 0, prow, jnp.where(row == 1, keep, 0.0)).astype(BF))
        parts.append(jnp.concatenate(part, axis=0))
    up, down = parts
    a_ref[...] = jnp.where(odd, up, down)
    b_ref[...] = jnp.where(odd, down, up)


def prep_kernel(*refs):
    far, (a3, own_ref, gphi_ref, phix, maskx), mats = refs[:9], refs[9:14], refs[14:23]
    strip, near, sems = refs[23], refs[24:33], refs[33]
    copies = {
        n: pltpu.make_async_copy(far[n], near[n], sems.at[n])
        for n in (3, 2, 4, 5, 6, 7, 8, 0, 1)
    }
    for copy in copies.values():
        copy.start()
    for n in (3, 2, 4, 5, 6, 7, 8):
        copies[n].wait()
    weight_matrices(*near[4:], *mats)
    copies[0].wait()
    copies[1].wait()
    own_fields(*near[:4], a3, own_ref, gphi_ref, phix, maskx, strip)


def own_fields(
    sky_ref, cot_ref, phi_ref, mask_ref, a3, own_ref, gphi_ref, phix, maskx, strip
):
    chans, rows, width = sky_ref.shape
    size = own_ref.shape[1]
    step = 3 * chans
    half = chans // 2
    cells = tile_rows(mask_ref)
    phi = phi_ref[...].astype(F32)
    phix[...] = phi
    for t in range(mask_ref.shape[0]):
        maskx[TILE * t : TILE * (t + 1)] = jnp.broadcast_to(cells[t : t + 1], (TILE, 128))
    lane8 = lane_iota(8)
    row8 = lax.broadcasted_iota(jnp.int32, (8, 128), 0)
    pick = ((row8 < 2) & (lane8 == row8)) | (
        (row8 >= 2) & (row8 < 4) & (lane8 == row8 + (width - 4))
    )
    pick = pick.astype(F32).astype(BF)
    trows, tcols = mask_ref.shape
    prow = lax.broadcasted_iota(jnp.int32, (8, tcols), 0)
    pcol = lax.broadcasted_iota(jnp.int32, (8, tcols), 1)
    pick_t = ((prow < 2) & (pcol == 0)) | ((prow >= 2) & (prow < 4) & (pcol == tcols - 1))
    edge = lax.dot_general(
        pick_t.astype(F32).astype(BF),
        mask_ref[...].astype(F32).astype(BF),
        NT,
        preferred_element_type=F32,
    )
    lane_t = lax.broadcasted_iota(jnp.int32, (trows, 128), 1)
    row_t = lax.broadcasted_iota(jnp.int32, (trows, 128), 0)
    spread = (lane_t // TILE == row_t).astype(F32).astype(BF)
    keep = lax.dot_general(edge.astype(BF), spread, NN, preferred_element_type=F32)
    phis = lax.dot_general(pick, phi_ref[...], NT, preferred_element_type=F32)
    phis = jnp.concatenate([phis, jnp.zeros((8, 128 - rows), F32)], axis=1)
    gphi = jnp.zeros((chans, 128), F32)
    for which, src in ((0, sky_ref), (1, cot_ref)):
        both = jnp.concatenate([src[:half], src[half:]], axis=1).reshape(half * 128, width)
        flat = lax.dot_general(pick, both, NT, preferred_element_type=F32)
        for j in range(half):
            strip[which, 8 * j : 8 * j + 8] = flat[:, 128 * j : 128 * j + 128]
        for k in range(4):
            part = strip[which, pl.ds(k, half, stride=8), :]
            col = jnp.concatenate([part, pltpu.roll(part, 64, 1)], axis=0)
            base = (2 * which + k % 2) * chans
            own_ref[k // 2, base : base + chans] = (col * keep[k : k + 1]).astype(BF)
        for j in range(rows // 16):
            block = jnp.transpose(src[:, 16 * j : 16 * j + 16, :], (1, 0, 2))
            for t in range(2):
                low = jnp.broadcast_to(cells[2 * j + t : 2 * j + t + 1], (chans, 128)).astype(BF)
                for n in range(TILE):
                    y = 16 * j + TILE * t + n
                    value = block[TILE * t + n] * low
                    a3[which, y * step : (y + 1) * step] = three_copies(value)
                    if which:
                        gphi = gphi + value.astype(F32) * phi[y : y + 1]
    gphi_ref[...] = gphi
    row = lax.broadcasted_iota(jnp.int32, (16, 128), 0)
    for side, k in ((0, 0), (1, 3)):
        extra = jnp.where(
            row == 0,
            jnp.broadcast_to(phis[k : k + 1], (16, 128)),
            jnp.where(row == 1, jnp.broadcast_to(keep[k : k + 1], (16, 128)), 0.0),
        )
        own_ref[side, 4 * chans : size] = extra.astype(BF)


def three_copies(value):
    return jnp.concatenate([pltpu.roll(value, 1, 1), value, pltpu.roll(value, 127, 1)], axis=0)


def col_kernel(rows, width, count, mine_ref, a_ref, b_ref, sa_ref, sb_ref, own_ref, halo_ref):
    size = a_ref.shape[0]
    tops, bots = received("gy", count, a_ref, b_ref)
    halo_ref[0] = tops
    halo_ref[1] = bots
    chans = (size - 16) // 4
    lane = lane_iota(chans)
    lane16 = lane_iota(16)
    sides = []
    for side in range(2):
        parts = []
        for m in range(4):
            which, k = divmod(m, 2)
            at = k + (width - 2) * side
            col = mine_ref[side, m * chans : (m + 1) * chans]
            for value, where in ((tops, (126, 127)), (bots, (rows, rows + 1))):
                for n in range(2):
                    base = (2 * which + n) * chans
                    cell = value[base : base + chans, at : at + 1]
                    col = jnp.where(lane == where[n], jnp.broadcast_to(cell, col.shape), col)
            parts.append(col)
        at = (width - 1) * side
        extra = mine_ref[side, 4 * chans : size].astype(F32)
        for value, where in ((tops, 127), (bots, rows)):
            cell = value[4 * chans : size].astype(F32)[:, at : at + 1]
            extra = jnp.where(lane16 == where, jnp.broadcast_to(cell, (16, 128)), extra)
        parts.append(extra.astype(BF))
        sides.append(jnp.concatenate(parts, axis=0))
        own_ref[side] = sides[side]
    odd_x = is_odd("gx")
    sa_ref[...] = jnp.where(odd_x, sides[0], sides[1])
    sb_ref[...] = jnp.where(odd_x, sides[1], sides[0])


def silu_parts(pre):
    sigma = 1.0 / (1.0 + jnp.exp(-pre))
    return pre * sigma, sigma * (1.0 + pre * (1.0 - sigma))


def hidden_kernel(
    a3, phi_own, mask_own, halo_ref, w1s_ref, w2ts_ref, cond_ref,
    hid_ref, dpre_ref, acc1, acc2, cacc,
    dz, phix, maskx, ringx, ringg,
):
    rows, width = phi_own.shape
    a3x, a3g = a3.at[0], a3.at[1]
    size = halo_ref.shape[1]
    chans = (size - 16) // 4
    step = 3 * chans
    lane1 = lane_iota(1)
    inside = jnp.where((lane1 == 0) | (lane1 == 127), 0.0, 1.0)
    for k, at in ((0, 0), (1, rows + 1)):
        extra = halo_ref[k, 4 * chans : size].astype(F32)
        phix[at : at + 1] = extra[0:1]
        maskx[at : at + 1] = extra[1:2] * inside
    phix[1 : rows + 1] = phi_own[...]
    maskx[1 : rows + 1] = mask_own[...] * inside
    for which, ring in ((0, ringx), (1, ringg)):
        for k in range(2):
            for n in range(2):
                base = (2 * which + n) * chans
                ring[(2 * k + n) * step : (2 * k + n + 1) * step] = three_copies(
                    halo_ref[k, base : base + chans]
                )

    def window(own, ring, y, count):
        parts = []
        if y < 0:
            parts.append(ring[(y + 2) * step : min(2, y + 2 + count) * step])
        low, high = max(y, 0), min(y + count, rows)
        if low < high:
            parts.append(own[low * step : high * step])
        if y + count > rows:
            low = max(y, rows) - rows
            parts.append(ring[(2 + low) * step : (2 + y + count - rows) * step])
        return parts[0] if len(parts) == 1 else jnp.concatenate(parts, axis=0)

    gain = cond_ref[:, 0:1]
    bias = cond_ref[:, 1:2]
    split = (rows + 2) // 2
    zero = jnp.zeros((chans, 128), BF)
    for y in (-2, -1, rows, rows + 1):
        dz[(y + 2) * chans : (y + 3) * chans] = zero

    def first_pass(it, dphi, dsum):
        y0 = R1 * it - 1

        def both(own, ring):
            pair = [window(own, ring, y0 - 1 + h * split, R1 + 2) for h in range(2)]
            return jnp.concatenate(pair, axis=1)

        pre = lax.dot_general(w1s_ref[...], both(a3x, ringx), NN, preferred_element_type=F32)
        back = lax.dot_general(w2ts_ref[...], both(a3g, ringg), NN, preferred_element_type=F32)
        for h in range(2):
            for r in range(R1):
                row = y0 + h * split + r + 1
                here = (slice(r * chans, (r + 1) * chans), slice(h * 128, h * 128 + 128))
                keep = maskx[row : row + 1]
                act, slope = silu_parts(pre[here] + gain * phix[row : row + 1] + bias)
                base = row * chans
                hid_ref[base : base + chans] = (act * keep).astype(BF)
                value = (back[here] * keep * slope).astype(BF)
                dpre_ref[base : base + chans] = value
                if 1 <= row <= rows:
                    dz[base + chans : base + 2 * chans] = value
                    wide = value.astype(F32)
                    dphi = dphi + wide * phix[row : row + 1]
                    dsum = dsum + wide
        return dphi, dsum

    dphi = jnp.zeros((chans, 128), F32)
    dsum = jnp.zeros((chans, 128), F32)
    for it in range(split // R1):
        dphi, dsum = first_pass(it, dphi, dsum)
    cacc[0] = dphi
    cacc[1] = dsum

    acc1[...] = jnp.zeros_like(acc1)
    acc2[...] = jnp.zeros_like(acc2)

    def rows_of(src, start, size):
        return src[start : start + size]

    def grads_one(it):
        ys = [GROUP1 * it + n - 1 for n in range(GROUP1)]
        acc1[...] += lax.dot_general(
            jnp.concatenate([rows_of(dz, (y + 1) * chans, step) for y in ys], axis=1),
            jnp.concatenate([window(a3x, ringx, y, 1) for y in ys], axis=1),
            NT, preferred_element_type=F32,
        )

    def grads_two(it):
        ys = [GROUP2 * it + n for n in range(GROUP2)]
        acc2[...] += lax.dot_general(
            jnp.concatenate([window(a3g, ringg, y, 1) for y in ys], axis=1),
            jnp.concatenate([rows_of(hid_ref, y * chans, step) for y in ys], axis=1),
            NT, preferred_element_type=F32,
        )

    for it in range((rows + 2) // GROUP1):
        grads_one(it)
    for it in range(rows // GROUP2):
        grads_two(it)


def edge_kernel(
    rows, count, a_ref, b_ref, own_ref, w1c_ref, w2tc_ref, cond_ref,
    acc1, acc2, cacc, gphi_ref,
    hcol_ref, dcol_ref, keep_ref, give_ref, wire,
):
    size = a_ref.shape[0]
    chans = (size - 16) // 4
    step = 3 * chans
    lft, rgt = received("gx", count, a_ref, b_ref)
    own_l, own_r = own_ref[0], own_ref[1]

    def at(value, which, n):
        base = (2 * which + n) * chans
        return value[base : base + chans]

    def columns(which):
        return [at(v, which, n) for v in (lft, own_l, own_r, rgt) for n in range(2)]

    centres = (1, 2, 5, 6)

    def taps_of(cols):
        pieces = []
        for ky in range(3):
            moved = [c if ky == 1 else pltpu.roll(c, (1, 0, 127)[ky], 1) for c in cols]
            for kx in range(3):
                pieces.append(jnp.concatenate([moved[c + kx - 1] for c in centres], axis=1))
        return jnp.concatenate(pieces, axis=0)

    x_taps = taps_of(columns(0))
    g_cols = columns(1)
    extra = [v[4 * chans : size].astype(F32) for v in (lft, own_l, own_r, rgt)]
    phi_c = jnp.concatenate([e[0:1] for e in extra], axis=1)
    mask_c = jnp.concatenate([e[1:2] for e in extra], axis=1)
    pre = lax.dot_general(w1c_ref[...], x_taps, NN, preferred_element_type=F32)
    back = lax.dot_general(w2tc_ref[...], taps_of(g_cols), NN, preferred_element_type=F32)
    act, slope = silu_parts(pre + cond_ref[:, 0:1] * phi_c + cond_ref[:, 1:2])
    hcol = (act * mask_c).astype(BF)
    dcol = (back * mask_c * slope).astype(BF)
    hcol_ref[...] = hcol
    dcol_ref[...] = dcol

    mine = jnp.broadcast_to((lane_iota(1) < rows).astype(F32), (chans, 128)).astype(BF)
    d_own = [dcol[:, 128:256] * mine, dcol[:, 256:384] * mine]
    part1 = lax.dot_general(
        jnp.concatenate(d_own, axis=1), x_taps[:, 128:384], NT, preferred_element_type=F32
    )
    h_cols = [hcol[:, 128 * k : 128 * k + 128] for k in range(4)]
    g_own = {k: g_cols[n] * mine for k, n in ((0, 2), (1, 3), (2, 4), (3, 5))}
    for kx, pairs in (
        (0, ((0, 0), (1, 1))),
        (1, ((0, 1), (3, 2))),
        (2, ((2, 2), (3, 3))),
    ):
        lhs = jnp.concatenate([g_own[g] for g, _ in pairs], axis=1)
        rhs = []
        for ky in range(3):
            moved = [
                h_cols[h] if ky == 1 else pltpu.roll(h_cols[h], (1, 0, 127)[ky], 1)
                for _, h in pairs
            ]
            rhs.append(jnp.concatenate(moved, axis=1))
        part2 = lax.dot_general(
            lhs, jnp.concatenate(rhs, axis=0), NT, preferred_element_type=F32
        )
        low = (2 - kx) * chans
        wide = jnp.concatenate(
            [
                acc1[low : low + chans] + part1[:, kx * step : (kx + 1) * step],
                acc2[low : low + chans] + part2,
            ],
            axis=1,
        )
        wire[low : low + chans] = wide[:, :128]
        wire[step + low : step + low + chans] = wide[:, 128:256]
        if kx == 0:
            tails = []
        tails.insert(0, wide[:, 256 : 2 * step])
    dphi, dsum = cacc[0], cacc[1]
    for d, k in ((d_own[0], 1), (d_own[1], 2)):
        dphi = dphi + d.astype(F32) * extra[k][0:1]
        dsum = dsum + d.astype(F32)
    sums = [jnp.sum(v, axis=1, keepdims=True) for v in (dphi, dsum, gphi_ref[...])]
    fill = jnp.zeros((chans, 128 - 3 * tails[0].shape[1] - 3), F32)
    wire[2 * step : 2 * step + chans] = jnp.concatenate(tails + sums + [fill], axis=1)
    half = wire.shape[0] // 2
    core = lax.rem(lax.axis_index("gy"), 2)
    keep_ref[...] = wire[pl.ds(pl.multiple_of(core * half, 8), half), :]
    give_ref[...] = wire[pl.ds(pl.multiple_of((1 - core) * half, 8), half), :]


def fix_kernel(rows, w2c_ref, w1tc_ref, hcol_ref, dcol_ref, hfix_ref, dfix_ref):
    chans = hcol_ref.shape[0]
    none = jnp.zeros((chans, 128), BF)
    half = chans // 2
    lane = lane_iota(half)
    for weights, field, fix in ((w2c_ref, hcol_ref, hfix_ref), (w1tc_ref, dcol_ref, dfix_ref)):
        f = [field[:, 128 * k : 128 * k + 128] for k in range(4)]
        pieces = []
        for ky in range(3):
            m = [c if ky == 1 else pltpu.roll(c, (1, 0, 127)[ky], 1) for c in f]
            pieces.append(jnp.concatenate([m[0], m[1], none, none], axis=1))
            pieces.append(jnp.concatenate([m[1], none, none, m[2]], axis=1))
            pieces.append(jnp.concatenate([none, none, m[2], m[3]], axis=1))
        fixes = lax.dot_general(
            weights[...], jnp.concatenate(pieces, axis=0), NN, preferred_element_type=F32
        )
        for k in range(4):
            col = fixes[:, 128 * k : 128 * k + 128]
            part = jnp.where(lane < rows, col[:half], pltpu.roll(col[half:], rows, 1))
            high = part.astype(BF).astype(F32)
            fix[pl.ds(k, half, stride=8), :] = high
            fix[pl.ds(4 + k, half, stride=8), :] = part - high


def output_kernel(
    with_phi, src_hbm, phi_ref, mask_ref, mid_ref, fix_ref, weights_ref, cond_ref,
    out_ref, a3, rowbuf, fixbuf, src_ref, sem,
):
    chans, rows, width = src_ref.shape
    step = 3 * chans
    half = chans // 2
    fetch = pltpu.make_async_copy(src_hbm, src_ref, sem)
    fetch.start()
    if with_phi:
        gain = cond_ref[:, 2:3]
    lane8 = lane_iota(8)
    row8 = lax.rem(lax.broadcasted_iota(jnp.int32, (8, 128), 0), 4)
    place = (lane8 == jnp.where(row8 < 2, row8, row8 + (width - 4))).astype(F32).astype(BF)
    for j in range(half):
        got = lax.dot_general(
            fix_ref[8 * j : 8 * j + 8].astype(BF), place, TN, preferred_element_type=F32
        )
        fixbuf[j] = got[:rows]
        fixbuf[j + half] = got[rows:]

    for y in range(rows + 2):
        centre = mid_ref[y * chans : (y + 1) * chans]
        base = y * step
        a3[base : base + chans] = pltpu.roll(centre, 1, 1)
        a3[base + chans : base + 2 * chans] = centre
        a3[base + 2 * chans : base + 3 * chans] = pltpu.roll(centre, 127, 1)

    for it in range(rows // (2 * R2)):
        y0 = R2 * it
        got = lax.dot_general(
            weights_ref[...],
            jnp.concatenate(
                [a3[(y0 + h) * step : (y0 + h + R2 + 2) * step] for h in (0, rows // 2)], axis=1
            ),
            NN, preferred_element_type=F32,
        )
        for h in range(2):
            for r in range(R2):
                y = y0 + h * (rows // 2) + r
                part = got[r * chans : (r + 1) * chans, h * 128 : h * 128 + 128]
                if with_phi:
                    part = part + gain * phi_ref[y : y + 1]
                rowbuf[y] = part

    fetch.wait()
    for j in range(rows // 16):
        here = slice(16 * j, 16 * j + 16)
        keep = mask_ref[here]
        total = jnp.transpose(rowbuf[here], (1, 0, 2)) + fixbuf[:, here, :]
        out_ref[:, here, :] = ((total + src_ref[:, here, :].astype(F32)) * keep[None]).astype(BF)


def unpack_kernel(factor, keep_ref, other_ref, w1_ref, w2_ref, cond_ref, wire):
    chans = w1_ref.shape[2]
    step = 3 * chans
    count = keep_ref.shape[0]
    core = lax.rem(lax.axis_index("gy"), 2)
    wire[pl.ds(pl.multiple_of(core * count, 8), count), :] = keep_ref[...]
    wire[pl.ds(pl.multiple_of((1 - core) * count, 8), count), :] = other_ref[...]
    tail = wire[2 * step : 2 * step + chans] * factor
    rest_w = 2 * step - 256
    for n in range(3):
        low = n * chans
        wide = jnp.concatenate(
            [
                wire[low : low + chans] * factor,
                wire[step + low : step + low + chans] * factor,
                tail[:, n * rest_w : (n + 1) * rest_w],
            ],
            axis=1,
        )
        for k in range(3):
            w1_ref[2 - n, k] = wide[:, k * chans : (k + 1) * chans]
            w2_ref[k, 2 - n] = wide[:, step + k * chans : step + (k + 1) * chans]
    cond_ref[...] = jnp.transpose(tail)[3 * rest_w : 3 * rest_w + 3, :chans]


def limit(mib):
    return pltpu.CompilerParams(vmem_limit_bytes=mib << 20)


def keep_near(value):
    return pltpu.with_memory_space_constraint(value, pltpu.VMEM)


def stacked(block, count):
    chans, taps = block.shape
    step = taps // 3
    rows = []
    for r in range(count):
        parts = [block]
        if r:
            parts.insert(0, jnp.zeros((chans, r * step), BF))
        if r < count - 1:
            parts.append(jnp.zeros((chans, (count - 1 - r) * step), BF))
        rows.append(jnp.concatenate(parts, axis=1))
    return jnp.concatenate(rows, axis=0)


def weight_matrices(
    one, two, vec0, vec1, vec2,
    w1f_ref, w2b_ref, w2f_ref, w1b_ref, w1s_ref, w2bs_ref, w2s_ref, w1bs_ref, cond_ref,
):
    chans = one.shape[2]
    for src, fwd, fwd_s, count, bwd, bwd_s, back in (
        (one, w1f_ref, w1s_ref, R1, w1b_ref, w1bs_ref, R2),
        (two, w2f_ref, w2s_ref, R2, w2b_ref, w2bs_ref, R1),
    ):
        taps = [src[k // 3, k % 3] for k in range(9)]
        plain = jnp.concatenate(taps, axis=1)
        turned = jnp.concatenate(
            [jnp.transpose(t.astype(F32)).astype(BF) for t in taps[::-1]], axis=1
        )
        fwd[...] = plain
        bwd[...] = turned
        fwd_s[...] = stacked(plain, count)
        bwd_s[...] = stacked(turned, back)
    row = lax.broadcasted_iota(jnp.int32, (8, chans), 0)
    table = jnp.zeros((8, chans), F32)
    for k, ref in enumerate((vec0, vec1, vec2)):
        table = jnp.where(row == k, jnp.broadcast_to(ref[...].reshape(1, chans), (8, chans)), table)
    table = jnp.concatenate([table, jnp.zeros((8, 128 - chans), F32)], axis=1)
    table = jnp.concatenate([table, jnp.zeros((120, 128), F32)], axis=0)
    cond_ref[...] = jnp.transpose(table)[:chans]


def build(mesh):
    ny, nx = mesh.shape["gy"], mesh.shape["gx"]
    axes = ("gy", "gx")

    def send(value, move):
        pairs = []
        for a in range(ny):
            for b in range(nx):
                to = move(a, b)
                pairs.append((a * nx + b, to[0] * nx + to[1]))
        return lax.ppermute(value, axes, pairs)

    def swap(first, second, axis):
        def partner(offset):
            def move(a, b):
                v = [a, b]
                v[axis] += 1 if (v[axis] + offset) % 2 == 0 else -1
                if 0 <= v[axis] < (ny, nx)[axis]:
                    return v
                return (a, b ^ 1) if axis == 0 else (a ^ 1, b)

            return move

        return send(first, partner(0)), send(second, partner(1))

    def exchange(value, moves):
        got = [send(value, lambda a, b: (a ^ m[0], b ^ m[1])) for m in moves]
        if len(moves) == 1:
            return value + got[0]
        both = (moves[0][0] ^ moves[1][0], moves[0][1] ^ moves[1][1])
        far = send(value, lambda a, b: (a ^ both[0], b ^ both[1]))
        return (value + got[0]) + (got[1] + far)

    def local(
        sky, lens_phi, cotangent, tile_mask, weight_one, weight_two, cond_one, bias_one, cond_two
    ):
        chans, rows, width = sky.shape
        step = 3 * chans
        size = 4 * chans + 16
        assert 2 * rows == 128 and width == 128
        edge = jax.ShapeDtypeStruct((size, 128), BF)
        edges = jax.ShapeDtypeStruct((2, size, 128), BF)
        hbm = pl.BlockSpec(memory_space=pltpu.HBM)
        far = [
            pltpu.with_memory_space_constraint(v, pltpu.HBM)
            for v in (
                sky, cotangent, lens_phi, tile_mask,
                weight_one, weight_two, cond_one, bias_one, cond_two,
            )
        ]
        vmem = pl.BlockSpec(memory_space=pltpu.VMEM)
        ra, rb = pl.pallas_call(
            row_kernel,
            out_shape=(edge, edge),
            in_specs=[hbm] * 4,
            scratch_shapes=[
                pltpu.VMEM((4, chans, 16, width), BF),
                pltpu.VMEM((2, 16, width), BF),
                pltpu.VMEM(tile_mask.shape, jnp.int32),
                pltpu.SemaphoreType.DMA((7,)),
            ],
            compiler_params=limit(8),
            name="edge_rows",
        )(*far[:4])
        ra, rb = swap(ra, rb, 0)

        flat_w = jax.ShapeDtypeStruct((chans, 3 * step), BF)
        first_w = jax.ShapeDtypeStruct((R1 * chans, (R1 + 2) * step), BF)
        second_w = jax.ShapeDtypeStruct((R2 * chans, (R2 + 2) * step), BF)
        matrices = (
            flat_w, flat_w, flat_w, flat_w, first_w, first_w, second_w, second_w,
            jax.ShapeDtypeStruct((chans, 128), F32),
        )
        flops = 2 * 9 * chans * chans * rows * width
        field = jax.ShapeDtypeStruct((2, rows * step, 128), BF)
        flat = jax.ShapeDtypeStruct(lens_phi.shape, F32)
        a3, mine, gphi, phi_own, mask_own, *matrices = pl.pallas_call(
            prep_kernel,
            out_shape=(field, edges, jax.ShapeDtypeStruct((chans, 128), F32), flat, flat)
            + matrices,
            in_specs=[hbm] * 9,
            scratch_shapes=[pltpu.VMEM((2, 8 * chans // 2, 128), F32)]
            + [pltpu.VMEM(v.shape, v.dtype) for v in far]
            + [pltpu.SemaphoreType.DMA((9,))],
            compiler_params=limit(8),
            cost_estimate=pl.CostEstimate(
                flops=4 * flops, bytes_accessed=8 << 20, transcendentals=0
            ),
            name="prep",
        )(*far)
        w1f, w2b, w2f, w1b, w1s, w2bs, w2s, w1bs, conds = matrices
        ca, cb, own, halo = pl.pallas_call(
            lambda *refs: col_kernel(rows, width, ny, *refs),
            out_shape=(edge, edge, edges, edges),
            compiler_params=limit(8),
            name="edge_cols",
        )(mine, ra, rb)
        ca, cb = swap(ca, cb, 1)

        ring = pltpu.VMEM((4 * step, 128), BF)
        rowwise = pltpu.VMEM((rows + 8, 128), F32)
        inner = jax.ShapeDtypeStruct(((rows + 2) * chans, 128), BF)
        acc = jax.ShapeDtypeStruct((step, step), F32)
        hid, dpre, acc1, acc2, cacc = pl.pallas_call(
            hidden_kernel,
            out_shape=(inner, inner, acc, acc, jax.ShapeDtypeStruct((2, chans, 128), F32)),
            scratch_shapes=[
                pltpu.VMEM(((rows + 4) * chans, 128), BF), rowwise, rowwise, ring, ring,
            ],
            compiler_params=limit(16),
            cost_estimate=pl.CostEstimate(
                flops=8 * flops, bytes_accessed=8 << 20, transcendentals=0
            ),
            name="hidden",
        )(
            keep_near(a3), phi_own, mask_own, halo,
            w1s, w2bs, conds,
        )

        fix = jax.ShapeDtypeStruct((4 * chans, 128), F32)
        count = (2 * step + chans) // 2
        wires = jax.ShapeDtypeStruct((count, 128), F32)
        cols = jax.ShapeDtypeStruct((chans, 512), BF)
        hcol, dcol, keep, give = pl.pallas_call(
            lambda *refs: edge_kernel(rows, nx, *refs),
            out_shape=(cols, cols, wires, wires),
            scratch_shapes=[pltpu.VMEM((2 * count, 128), F32)],
            compiler_params=limit(8),
            name="edge_parts",
        )(ca, cb, own, w1f, w2b, conds, acc1, acc2, cacc, gphi)
        hfix, dfix = pl.pallas_call(
            lambda *refs: fix_kernel(rows, *refs),
            out_shape=(fix, fix),
            compiler_params=limit(8),
            cost_estimate=pl.CostEstimate(
                flops=flops // 2, bytes_accessed=1 << 20, transcendentals=0
            ),
            name="edge_fixes",
        )(w2f, w1b, hcol, dcol)

        def output(with_phi, src, mid, fix, weights, name):
            return pl.pallas_call(
                lambda *refs: output_kernel(with_phi, *refs),
                out_shape=jax.ShapeDtypeStruct(src.shape, BF),
                scratch_shapes=[
                    pltpu.VMEM(((rows + 2) * step, 128), BF),
                    pltpu.VMEM((rows, chans, 128), F32),
                    pltpu.VMEM((chans, rows, 128), F32),
                    pltpu.VMEM(src.shape, BF),
                    pltpu.SemaphoreType.DMA(()),
                ],
                in_specs=[hbm] + [vmem] * 6,
                compiler_params=limit(16),
                cost_estimate=pl.CostEstimate(
                    flops=2 * flops, bytes_accessed=4 << 20, transcendentals=0
                ),
                name=name,
            )(src, phi_own, mask_own, mid, fix, weights, conds)

        moves = [(1 << k, 0) for k in range(1, ny.bit_length() - 1)]
        moves += [(0, 1 << k) for k in range(nx.bit_length() - 1)]
        rounds = [moves[:2]] + [[move] for move in moves[2:]]
        keep = keep + send(give, lambda a, b: (a ^ 1, b))
        outs = []
        for n, move in enumerate(rounds):
            if n == 0:
                keep, hfix = lax.optimization_barrier((keep, hfix))
                outs.append(output(True, far[0], hid, hfix, w2s, "delensed"))
            if n == len(rounds) - 1:
                keep, dfix = lax.optimization_barrier((keep, dfix))
                outs.append(output(False, far[1], dpre, dfix, w1bs, "grad_input"))
            keep = exchange(keep, move)
            if n in (0, len(rounds) - 1):
                keep, outs[-1] = lax.optimization_barrier((keep, outs[-1]))
        delensed, grad_input = outs
        other = send(keep, lambda a, b: (a ^ 1, b))

        factor = float(1.0 / (rows * ny * width * nx) ** 0.5)
        grads = jax.ShapeDtypeStruct((3, 3, chans, chans), F32)
        grad_w1, grad_w2, grad_cond = pl.pallas_call(
            lambda *refs: unpack_kernel(factor, *refs),
            out_shape=(grads, grads, jax.ShapeDtypeStruct((3, chans), F32)),
            scratch_shapes=[pltpu.VMEM((2 * count, 128), F32)],
            compiler_params=limit(8),
            name="unpack",
        )(keep, other)
        return delensed, grad_input, grad_w1, grad_w2, grad_cond

    return local


def solution(mesh):
    return jax.shard_map(
        build(mesh),
        mesh=mesh,
        in_specs=(
            P(None, "gy", "gx"),
            P("gy", "gx"),
            P(None, "gy", "gx"),
            P("gy", "gx"),
            P(),
            P(),
            P(),
            P(),
            P(),
        ),
        out_specs=(P(None, "gy", "gx"), P(None, "gy", "gx"), P(), P(), P()),
        check_vma=False,
    )
```

```python
import jax
import jax.numpy as jnp
from jax import lax
from jax.experimental import pallas as pl
from jax.experimental.pallas import tpu as pltpu
from jax.sharding import PartitionSpec as P

TILE = 8
BF = jnp.bfloat16
F32 = jnp.float32
NT = (((1,), (1,)), ((), ()))
NN = (((1,), (0,)), ((), ()))
TN = (((0,), (0,)), ((), ()))
R1 = 3
R2 = 4
GROUP1 = 6
GROUP2 = 8


def lane_iota(rows):
    return lax.broadcasted_iota(jnp.int32, (rows, 128), 1)


def tile_rows(mask_ref):
    tcols = mask_ref.shape[1]
    lane = lax.broadcasted_iota(jnp.int32, (tcols, 128), 1)
    row = lax.broadcasted_iota(jnp.int32, (tcols, 128), 0)
    spread = (lane // TILE == row).astype(F32).astype(BF)
    return lax.dot_general(
        mask_ref[...].astype(F32).astype(BF), spread, NN, preferred_element_type=F32
    )


def is_odd(axis):
    return lax.rem(lax.axis_index(axis), 2) == 1


def received(axis, count, a_ref, b_ref):
    ends = (lax.axis_index(axis) == 0) | (lax.axis_index(axis) == count - 1)
    ra = a_ref[...]
    rb = jnp.where(ends, jnp.zeros_like(ra), b_ref[...])
    odd = is_odd(axis)
    return jnp.where(odd, ra, rb), jnp.where(odd, rb, ra)


def row_kernel(sky_ref, cot_ref, phi_ref, mask_ref, a_ref, b_ref, blocks, phis, tiles, sems):
    chans, rows, _ = sky_ref.shape
    copies = []
    for n, (src, dst) in enumerate(
        [
            (ref.at[:, pl.ds(first, 8), :], blocks.at[k])
            for k, (ref, first) in enumerate(
                ((sky_ref, 0), (cot_ref, 0), (sky_ref, rows - 8), (cot_ref, rows - 8))
            )
        ]
        + [(phi_ref.at[pl.ds(0, 16), :], phis.at[0]), (phi_ref.at[pl.ds(rows - 16, 16), :], phis.at[1])]
        + [(mask_ref, tiles)]
    ):
        copies.append(pltpu.make_async_copy(src, dst, sems.at[n]))
        copies[-1].start()
    for copy in copies:
        copy.wait()
    cells = tile_rows(tiles)
    odd = is_odd("gy")
    parts = []
    for side, (first, mrow) in enumerate(((0, 0), (6, tiles.shape[0] - 1))):
        keep = cells[mrow : mrow + 1]
        low = jnp.broadcast_to(keep, (chans, 128)).astype(BF)
        part = []
        for k in range(2):
            block = jnp.transpose(blocks[2 * side + k], (1, 0, 2))
            part += [block[first] * low, block[first + 1] * low]
        row = lax.broadcasted_iota(jnp.int32, (16, 128), 0)
        prow = phis[side].astype(F32)[15 * side : 15 * side + 1]
        prow = jnp.broadcast_to(prow, (16, 128))
        part.append(jnp.where(row == 0, prow, jnp.where(row == 1, keep, 0.0)).astype(BF))
        parts.append(jnp.concatenate(part, axis=0))
    up, down = parts
    a_ref[...] = jnp.where(odd, up, down)
    b_ref[...] = jnp.where(odd, down, up)


def prep_kernel(*refs):
    far, (a3, own_ref, gphi_ref, phix, maskx), mats = refs[:9], refs[9:14], refs[14:23]
    strip, near, sems = refs[23], refs[24:33], refs[33]
    copies = {
        n: pltpu.make_async_copy(far[n], near[n], sems.at[n])
        for n in (3, 2, 4, 5, 6, 7, 8, 0, 1)
    }
    for copy in copies.values():
        copy.start()
    for n in (3, 2, 4, 5, 6, 7, 8):
        copies[n].wait()
    weight_matrices(*near[4:], *mats)
    copies[0].wait()
    copies[1].wait()
    own_fields(*near[:4], a3, own_ref, gphi_ref, phix, maskx, strip)


def own_fields(
    sky_ref, cot_ref, phi_ref, mask_ref, a3, own_ref, gphi_ref, phix, maskx, strip
):
    chans, rows, width = sky_ref.shape
    size = own_ref.shape[1]
    step = 3 * chans
    half = chans // 2
    cells = tile_rows(mask_ref)
    phi = phi_ref[...].astype(F32)
    phix[...] = phi
    for t in range(mask_ref.shape[0]):
        maskx[TILE * t : TILE * (t + 1)] = jnp.broadcast_to(cells[t : t + 1], (TILE, 128))
    lane8 = lane_iota(8)
    row8 = lax.broadcasted_iota(jnp.int32, (8, 128), 0)
    pick = ((row8 < 2) & (lane8 == row8)) | (
        (row8 >= 2) & (row8 < 4) & (lane8 == row8 + (width - 4))
    )
    pick = pick.astype(F32).astype(BF)
    trows, tcols = mask_ref.shape
    prow = lax.broadcasted_iota(jnp.int32, (8, tcols), 0)
    pcol = lax.broadcasted_iota(jnp.int32, (8, tcols), 1)
    pick_t = ((prow < 2) & (pcol == 0)) | ((prow >= 2) & (prow < 4) & (pcol == tcols - 1))
    edge = lax.dot_general(
        pick_t.astype(F32).astype(BF),
        mask_ref[...].astype(F32).astype(BF),
        NT,
        preferred_element_type=F32,
    )
    lane_t = lax.broadcasted_iota(jnp.int32, (trows, 128), 1)
    row_t = lax.broadcasted_iota(jnp.int32, (trows, 128), 0)
    spread = (lane_t // TILE == row_t).astype(F32).astype(BF)
    keep = lax.dot_general(edge.astype(BF), spread, NN, preferred_element_type=F32)
    phis = lax.dot_general(pick, phi_ref[...], NT, preferred_element_type=F32)
    phis = jnp.concatenate([phis, jnp.zeros((8, 128 - rows), F32)], axis=1)
    gphi = jnp.zeros((chans, 128), F32)
    for which, src in ((0, sky_ref), (1, cot_ref)):
        both = jnp.concatenate([src[:half], src[half:]], axis=1).reshape(half * 128, width)
        flat = lax.dot_general(pick, both, NT, preferred_element_type=F32)
        for j in range(half):
            strip[which, 8 * j : 8 * j + 8] = flat[:, 128 * j : 128 * j + 128]
        for k in range(4):
            part = strip[which, pl.ds(k, half, stride=8), :]
            col = jnp.concatenate([part, pltpu.roll(part, 64, 1)], axis=0)
            base = (2 * which + k % 2) * chans
            own_ref[k // 2, base : base + chans] = (col * keep[k : k + 1]).astype(BF)
        for j in range(rows // 16):
            block = jnp.transpose(src[:, 16 * j : 16 * j + 16, :], (1, 0, 2))
            for t in range(2):
                low = jnp.broadcast_to(cells[2 * j + t : 2 * j + t + 1], (chans, 128)).astype(BF)
                for n in range(TILE):
                    y = 16 * j + TILE * t + n
                    value = block[TILE * t + n] * low
                    a3[which, y * step : (y + 1) * step] = three_copies(value)
                    if which:
                        gphi = gphi + value.astype(F32) * phi[y : y + 1]
    gphi_ref[...] = gphi
    row = lax.broadcasted_iota(jnp.int32, (16, 128), 0)
    for side, k in ((0, 0), (1, 3)):
        extra = jnp.where(
            row == 0,
            jnp.broadcast_to(phis[k : k + 1], (16, 128)),
            jnp.where(row == 1, jnp.broadcast_to(keep[k : k + 1], (16, 128)), 0.0),
        )
        own_ref[side, 4 * chans : size] = extra.astype(BF)


def three_copies(value):
    return jnp.concatenate([pltpu.roll(value, 1, 1), value, pltpu.roll(value, 127, 1)], axis=0)


def col_kernel(rows, width, count, mine_ref, a_ref, b_ref, sa_ref, sb_ref, own_ref, halo_ref):
    size = a_ref.shape[0]
    tops, bots = received("gy", count, a_ref, b_ref)
    halo_ref[0] = tops
    halo_ref[1] = bots
    chans = (size - 16) // 4
    lane = lane_iota(chans)
    lane16 = lane_iota(16)
    sides = []
    for side in range(2):
        parts = []
        for m in range(4):
            which, k = divmod(m, 2)
            at = k + (width - 2) * side
            col = mine_ref[side, m * chans : (m + 1) * chans]
            for value, where in ((tops, (126, 127)), (bots, (rows, rows + 1))):
                for n in range(2):
                    base = (2 * which + n) * chans
                    cell = value[base : base + chans, at : at + 1]
                    col = jnp.where(lane == where[n], jnp.broadcast_to(cell, col.shape), col)
            parts.append(col)
        at = (width - 1) * side
        extra = mine_ref[side, 4 * chans : size].astype(F32)
        for value, where in ((tops, 127), (bots, rows)):
            cell = value[4 * chans : size].astype(F32)[:, at : at + 1]
            extra = jnp.where(lane16 == where, jnp.broadcast_to(cell, (16, 128)), extra)
        parts.append(extra.astype(BF))
        sides.append(jnp.concatenate(parts, axis=0))
        own_ref[side] = sides[side]
    odd_x = is_odd("gx")
    sa_ref[...] = jnp.where(odd_x, sides[0], sides[1])
    sb_ref[...] = jnp.where(odd_x, sides[1], sides[0])


def silu_parts(pre):
    sigma = 1.0 / (1.0 + jnp.exp(-pre))
    return pre * sigma, sigma * (1.0 + pre * (1.0 - sigma))


def hidden_kernel(
    a3, phi_own, mask_own, halo_ref, w1s_ref, w2ts_ref, cond_ref,
    hid_ref, dpre_ref, acc1, acc2, cacc,
    dz, phix, maskx, ringx, ringg,
):
    rows, width = phi_own.shape
    a3x, a3g = a3.at[0], a3.at[1]
    size = halo_ref.shape[1]
    chans = (size - 16) // 4
    step = 3 * chans
    lane1 = lane_iota(1)
    inside = jnp.where((lane1 == 0) | (lane1 == 127), 0.0, 1.0)
    for k, at in ((0, 0), (1, rows + 1)):
        extra = halo_ref[k, 4 * chans : size].astype(F32)
        phix[at : at + 1] = extra[0:1]
        maskx[at : at + 1] = extra[1:2] * inside
    phix[1 : rows + 1] = phi_own[...]
    maskx[1 : rows + 1] = mask_own[...] * inside
    for which, ring in ((0, ringx), (1, ringg)):
        for k in range(2):
            for n in range(2):
                base = (2 * which + n) * chans
                ring[(2 * k + n) * step : (2 * k + n + 1) * step] = three_copies(
                    halo_ref[k, base : base + chans]
                )

    def window(own, ring, y, count):
        parts = []
        if y < 0:
            parts.append(ring[(y + 2) * step : min(2, y + 2 + count) * step])
        low, high = max(y, 0), min(y + count, rows)
        if low < high:
            parts.append(own[low * step : high * step])
        if y + count > rows:
            low = max(y, rows) - rows
            parts.append(ring[(2 + low) * step : (2 + y + count - rows) * step])
        return parts[0] if len(parts) == 1 else jnp.concatenate(parts, axis=0)

    gain = cond_ref[:, 0:1]
    bias = cond_ref[:, 1:2]
    split = (rows + 2) // 2
    zero = jnp.zeros((chans, 128), BF)
    for y in (-2, -1, rows, rows + 1):
        dz[(y + 2) * chans : (y + 3) * chans] = zero

    def first_pass(it, dphi, dsum):
        y0 = R1 * it - 1

        def both(own, ring):
            pair = [window(own, ring, y0 - 1 + h * split, R1 + 2) for h in range(2)]
            return jnp.concatenate(pair, axis=1)

        pre = lax.dot_general(w1s_ref[...], both(a3x, ringx), NN, preferred_element_type=F32)
        back = lax.dot_general(w2ts_ref[...], both(a3g, ringg), NN, preferred_element_type=F32)
        for h in range(2):
            for r in range(R1):
                row = y0 + h * split + r + 1
                here = (slice(r * chans, (r + 1) * chans), slice(h * 128, h * 128 + 128))
                keep = maskx[row : row + 1]
                act, slope = silu_parts(pre[here] + gain * phix[row : row + 1] + bias)
                base = row * chans
                hid_ref[base : base + chans] = (act * keep).astype(BF)
                value = (back[here] * keep * slope).astype(BF)
                dpre_ref[base : base + chans] = value
                if 1 <= row <= rows:
                    dz[base + chans : base + 2 * chans] = value
                    wide = value.astype(F32)
                    dphi = dphi + wide * phix[row : row + 1]
                    dsum = dsum + wide
        return dphi, dsum

    dphi = jnp.zeros((chans, 128), F32)
    dsum = jnp.zeros((chans, 128), F32)
    for it in range(split // R1):
        dphi, dsum = first_pass(it, dphi, dsum)
    cacc[0] = dphi
    cacc[1] = dsum

    acc1[...] = jnp.zeros_like(acc1)
    acc2[...] = jnp.zeros_like(acc2)

    def rows_of(src, start, size):
        return src[start : start + size]

    def grads_one(it):
        ys = [GROUP1 * it + n - 1 for n in range(GROUP1)]
        acc1[...] += lax.dot_general(
            jnp.concatenate([rows_of(dz, (y + 1) * chans, step) for y in ys], axis=1),
            jnp.concatenate([window(a3x, ringx, y, 1) for y in ys], axis=1),
            NT, preferred_element_type=F32,
        )

    def grads_two(it):
        ys = [GROUP2 * it + n for n in range(GROUP2)]
        acc2[...] += lax.dot_general(
            jnp.concatenate([window(a3g, ringg, y, 1) for y in ys], axis=1),
            jnp.concatenate([rows_of(hid_ref, y * chans, step) for y in ys], axis=1),
            NT, preferred_element_type=F32,
        )

    for it in range((rows + 2) // GROUP1):
        grads_one(it)
    for it in range(rows // GROUP2):
        grads_two(it)


def edge_kernel(
    rows, count, a_ref, b_ref, own_ref, w1c_ref, w2tc_ref, cond_ref,
    acc1, acc2, cacc, gphi_ref,
    hcol_ref, dcol_ref, keep_ref, give_ref, wire,
):
    size = a_ref.shape[0]
    chans = (size - 16) // 4
    step = 3 * chans
    lft, rgt = received("gx", count, a_ref, b_ref)
    own_l, own_r = own_ref[0], own_ref[1]

    def at(value, which, n):
        base = (2 * which + n) * chans
        return value[base : base + chans]

    def columns(which):
        return [at(v, which, n) for v in (lft, own_l, own_r, rgt) for n in range(2)]

    centres = (1, 2, 5, 6)

    def taps_of(cols):
        pieces = []
        for ky in range(3):
            moved = [c if ky == 1 else pltpu.roll(c, (1, 0, 127)[ky], 1) for c in cols]
            for kx in range(3):
                pieces.append(jnp.concatenate([moved[c + kx - 1] for c in centres], axis=1))
        return jnp.concatenate(pieces, axis=0)

    x_taps = taps_of(columns(0))
    g_cols = columns(1)
    extra = [v[4 * chans : size].astype(F32) for v in (lft, own_l, own_r, rgt)]
    phi_c = jnp.concatenate([e[0:1] for e in extra], axis=1)
    mask_c = jnp.concatenate([e[1:2] for e in extra], axis=1)
    pre = lax.dot_general(w1c_ref[...], x_taps, NN, preferred_element_type=F32)
    back = lax.dot_general(w2tc_ref[...], taps_of(g_cols), NN, preferred_element_type=F32)
    act, slope = silu_parts(pre + cond_ref[:, 0:1] * phi_c + cond_ref[:, 1:2])
    hcol = (act * mask_c).astype(BF)
    dcol = (back * mask_c * slope).astype(BF)
    hcol_ref[...] = hcol
    dcol_ref[...] = dcol

    mine = jnp.broadcast_to((lane_iota(1) < rows).astype(F32), (chans, 128)).astype(BF)
    d_own = [dcol[:, 128:256] * mine, dcol[:, 256:384] * mine]
    part1 = lax.dot_general(
        jnp.concatenate(d_own, axis=1), x_taps[:, 128:384], NT, preferred_element_type=F32
    )
    h_cols = [hcol[:, 128 * k : 128 * k + 128] for k in range(4)]
    g_own = {k: g_cols[n] * mine for k, n in ((0, 2), (1, 3), (2, 4), (3, 5))}
    for kx, pairs in (
        (0, ((0, 0), (1, 1))),
        (1, ((0, 1), (3, 2))),
        (2, ((2, 2), (3, 3))),
    ):
        lhs = jnp.concatenate([g_own[g] for g, _ in pairs], axis=1)
        rhs = []
        for ky in range(3):
            moved = [
                h_cols[h] if ky == 1 else pltpu.roll(h_cols[h], (1, 0, 127)[ky], 1)
                for _, h in pairs
            ]
            rhs.append(jnp.concatenate(moved, axis=1))
        part2 = lax.dot_general(
            lhs, jnp.concatenate(rhs, axis=0), NT, preferred_element_type=F32
        )
        low = (2 - kx) * chans
        wide = jnp.concatenate(
            [
                acc1[low : low + chans] + part1[:, kx * step : (kx + 1) * step],
                acc2[low : low + chans] + part2,
            ],
            axis=1,
        )
        wire[low : low + chans] = wide[:, :128]
        wire[step + low : step + low + chans] = wide[:, 128:256]
        if kx == 0:
            tails = []
        tails.insert(0, wide[:, 256 : 2 * step])
    dphi, dsum = cacc[0], cacc[1]
    for d, k in ((d_own[0], 1), (d_own[1], 2)):
        dphi = dphi + d.astype(F32) * extra[k][0:1]
        dsum = dsum + d.astype(F32)
    sums = [jnp.sum(v, axis=1, keepdims=True) for v in (dphi, dsum, gphi_ref[...])]
    fill = jnp.zeros((chans, 128 - 3 * tails[0].shape[1] - 3), F32)
    wire[2 * step : 2 * step + chans] = jnp.concatenate(tails + sums + [fill], axis=1)
    half = wire.shape[0] // 2
    core = lax.rem(lax.axis_index("gy"), 2)
    keep_ref[...] = wire[pl.ds(pl.multiple_of(core * half, 8), half), :]
    give_ref[...] = wire[pl.ds(pl.multiple_of((1 - core) * half, 8), half), :]


def fix_kernel(rows, w2c_ref, w1tc_ref, hcol_ref, dcol_ref, hfix_ref, dfix_ref):
    chans = hcol_ref.shape[0]
    none = jnp.zeros((chans, 128), BF)
    half = chans // 2
    lane = lane_iota(half)
    for weights, field, fix in ((w2c_ref, hcol_ref, hfix_ref), (w1tc_ref, dcol_ref, dfix_ref)):
        f = [field[:, 128 * k : 128 * k + 128] for k in range(4)]
        pieces = []
        for ky in range(3):
            m = [c if ky == 1 else pltpu.roll(c, (1, 0, 127)[ky], 1) for c in f]
            pieces.append(jnp.concatenate([m[0], m[1], none, none], axis=1))
            pieces.append(jnp.concatenate([m[1], none, none, m[2]], axis=1))
            pieces.append(jnp.concatenate([none, none, m[2], m[3]], axis=1))
        fixes = lax.dot_general(
            weights[...], jnp.concatenate(pieces, axis=0), NN, preferred_element_type=F32
        )
        for k in range(4):
            col = fixes[:, 128 * k : 128 * k + 128]
            part = jnp.where(lane < rows, col[:half], pltpu.roll(col[half:], rows, 1))
            high = part.astype(BF).astype(F32)
            fix[pl.ds(k, half, stride=8), :] = high
            fix[pl.ds(4 + k, half, stride=8), :] = part - high


def output_kernel(
    with_phi, src_hbm, phi_ref, mask_ref, mid_ref, fix_ref, weights_ref, cond_ref,
    out_ref, a3, rowbuf, fixbuf, src_ref, sem,
):
    chans, rows, width = src_ref.shape
    step = 3 * chans
    half = chans // 2
    fetch = pltpu.make_async_copy(src_hbm, src_ref, sem)
    fetch.start()
    if with_phi:
        gain = cond_ref[:, 2:3]
    lane8 = lane_iota(8)
    row8 = lax.rem(lax.broadcasted_iota(jnp.int32, (8, 128), 0), 4)
    place = (lane8 == jnp.where(row8 < 2, row8, row8 + (width - 4))).astype(F32).astype(BF)
    for j in range(half):
        got = lax.dot_general(
            fix_ref[8 * j : 8 * j + 8].astype(BF), place, TN, preferred_element_type=F32
        )
        fixbuf[j] = got[:rows]
        fixbuf[j + half] = got[rows:]

    for y in range(rows + 2):
        centre = mid_ref[y * chans : (y + 1) * chans]
        base = y * step
        a3[base : base + chans] = pltpu.roll(centre, 1, 1)
        a3[base + chans : base + 2 * chans] = centre
        a3[base + 2 * chans : base + 3 * chans] = pltpu.roll(centre, 127, 1)

    for it in range(rows // (2 * R2)):
        y0 = R2 * it
        got = lax.dot_general(
            weights_ref[...],
            jnp.concatenate(
                [a3[(y0 + h) * step : (y0 + h + R2 + 2) * step] for h in (0, rows // 2)], axis=1
            ),
            NN, preferred_element_type=F32,
        )
        for h in range(2):
            for r in range(R2):
                y = y0 + h * (rows // 2) + r
                part = got[r * chans : (r + 1) * chans, h * 128 : h * 128 + 128]
                if with_phi:
                    part = part + gain * phi_ref[y : y + 1]
                rowbuf[y] = part

    fetch.wait()
    for j in range(rows // 16):
        here = slice(16 * j, 16 * j + 16)
        keep = mask_ref[here]
        total = jnp.transpose(rowbuf[here], (1, 0, 2)) + fixbuf[:, here, :]
        out_ref[:, here, :] = ((total + src_ref[:, here, :].astype(F32)) * keep[None]).astype(BF)


def unpack_kernel(factor, keep_ref, other_ref, w1_ref, w2_ref, cond_ref, wire):
    chans = w1_ref.shape[2]
    step = 3 * chans
    count = keep_ref.shape[0]
    core = lax.rem(lax.axis_index("gy"), 2)
    wire[pl.ds(pl.multiple_of(core * count, 8), count), :] = keep_ref[...]
    wire[pl.ds(pl.multiple_of((1 - core) * count, 8), count), :] = other_ref[...]
    tail = wire[2 * step : 2 * step + chans] * factor
    rest_w = 2 * step - 256
    for n in range(3):
        low = n * chans
        wide = jnp.concatenate(
            [
                wire[low : low + chans] * factor,
                wire[step + low : step + low + chans] * factor,
                tail[:, n * rest_w : (n + 1) * rest_w],
            ],
            axis=1,
        )
        for k in range(3):
            w1_ref[2 - n, k] = wide[:, k * chans : (k + 1) * chans]
            w2_ref[k, 2 - n] = wide[:, step + k * chans : step + (k + 1) * chans]
    cond_ref[...] = jnp.transpose(tail)[3 * rest_w : 3 * rest_w + 3, :chans]


def limit(mib):
    return pltpu.CompilerParams(vmem_limit_bytes=mib << 20)


def keep_near(value):
    return pltpu.with_memory_space_constraint(value, pltpu.VMEM)


def stacked(block, count):
    chans, taps = block.shape
    step = taps // 3
    rows = []
    for r in range(count):
        parts = [block]
        if r:
            parts.insert(0, jnp.zeros((chans, r * step), BF))
        if r < count - 1:
            parts.append(jnp.zeros((chans, (count - 1 - r) * step), BF))
        rows.append(jnp.concatenate(parts, axis=1))
    return jnp.concatenate(rows, axis=0)


def weight_matrices(
    one, two, vec0, vec1, vec2,
    w1f_ref, w2b_ref, w2f_ref, w1b_ref, w1s_ref, w2bs_ref, w2s_ref, w1bs_ref, cond_ref,
):
    chans = one.shape[2]
    for src, fwd, fwd_s, count, bwd, bwd_s, back in (
        (one, w1f_ref, w1s_ref, R1, w1b_ref, w1bs_ref, R2),
        (two, w2f_ref, w2s_ref, R2, w2b_ref, w2bs_ref, R1),
    ):
        taps = [src[k // 3, k % 3] for k in range(9)]
        plain = jnp.concatenate(taps, axis=1)
        turned = jnp.concatenate(
            [jnp.transpose(t.astype(F32)).astype(BF) for t in taps[::-1]], axis=1
        )
        fwd[...] = plain
        bwd[...] = turned
        fwd_s[...] = stacked(plain, count)
        bwd_s[...] = stacked(turned, back)
    row = lax.broadcasted_iota(jnp.int32, (8, chans), 0)
    table = jnp.zeros((8, chans), F32)
    for k, ref in enumerate((vec0, vec1, vec2)):
        table = jnp.where(row == k, jnp.broadcast_to(ref[...].reshape(1, chans), (8, chans)), table)
    table = jnp.concatenate([table, jnp.zeros((8, 128 - chans), F32)], axis=1)
    table = jnp.concatenate([table, jnp.zeros((120, 128), F32)], axis=0)
    cond_ref[...] = jnp.transpose(table)[:chans]


def build(mesh):
    ny, nx = mesh.shape["gy"], mesh.shape["gx"]
    axes = ("gy", "gx")

    def send(value, move):
        pairs = []
        for a in range(ny):
            for b in range(nx):
                to = move(a, b)
                pairs.append((a * nx + b, to[0] * nx + to[1]))
        return lax.ppermute(value, axes, pairs)

    def swap(first, second, axis):
        def partner(offset):
            def move(a, b):
                v = [a, b]
                v[axis] += 1 if (v[axis] + offset) % 2 == 0 else -1
                if 0 <= v[axis] < (ny, nx)[axis]:
                    return v
                return (a, b ^ 1) if axis == 0 else (a ^ 1, b)

            return move

        return send(first, partner(0)), send(second, partner(1))

    def exchange(value, moves):
        sent = value.astype(BF)
        got = [send(sent, lambda a, b: (a ^ m[0], b ^ m[1])).astype(F32) for m in moves]
        if len(moves) == 1:
            return sent.astype(F32) + got[0]
        both = (moves[0][0] ^ moves[1][0], moves[0][1] ^ moves[1][1])
        far = send(sent, lambda a, b: (a ^ both[0], b ^ both[1])).astype(F32)
        return (sent.astype(F32) + got[0]) + (got[1] + far)

    def local(
        sky, lens_phi, cotangent, tile_mask, weight_one, weight_two, cond_one, bias_one, cond_two
    ):
        chans, rows, width = sky.shape
        step = 3 * chans
        size = 4 * chans + 16
        assert 2 * rows == 128 and width == 128
        edge = jax.ShapeDtypeStruct((size, 128), BF)
        edges = jax.ShapeDtypeStruct((2, size, 128), BF)
        hbm = pl.BlockSpec(memory_space=pltpu.HBM)
        far = [
            pltpu.with_memory_space_constraint(v, pltpu.HBM)
            for v in (
                sky, cotangent, lens_phi, tile_mask,
                weight_one, weight_two, cond_one, bias_one, cond_two,
            )
        ]
        vmem = pl.BlockSpec(memory_space=pltpu.VMEM)
        ra, rb = pl.pallas_call(
            row_kernel,
            out_shape=(edge, edge),
            in_specs=[hbm] * 4,
            scratch_shapes=[
                pltpu.VMEM((4, chans, 8, width), BF),
                pltpu.VMEM((2, 16, width), BF),
                pltpu.VMEM(tile_mask.shape, jnp.int32),
                pltpu.SemaphoreType.DMA((7,)),
            ],
            compiler_params=limit(8),
            name="edge_rows",
        )(*far[:4])
        ra, rb = swap(ra, rb, 0)

        flat_w = jax.ShapeDtypeStruct((chans, 3 * step), BF)
        first_w = jax.ShapeDtypeStruct((R1 * chans, (R1 + 2) * step), BF)
        second_w = jax.ShapeDtypeStruct((R2 * chans, (R2 + 2) * step), BF)
        matrices = (
            flat_w, flat_w, flat_w, flat_w, first_w, first_w, second_w, second_w,
            jax.ShapeDtypeStruct((chans, 128), F32),
        )
        flops = 2 * 9 * chans * chans * rows * width
        field = jax.ShapeDtypeStruct((2, rows * step, 128), BF)
        flat = jax.ShapeDtypeStruct(lens_phi.shape, F32)
        a3, mine, gphi, phi_own, mask_own, *matrices = pl.pallas_call(
            prep_kernel,
            out_shape=(field, edges, jax.ShapeDtypeStruct((chans, 128), F32), flat, flat)
            + matrices,
            in_specs=[hbm] * 9,
            scratch_shapes=[pltpu.VMEM((2, 8 * chans // 2, 128), F32)]
            + [pltpu.VMEM(v.shape, v.dtype) for v in far]
            + [pltpu.SemaphoreType.DMA((9,))],
            compiler_params=limit(8),
            cost_estimate=pl.CostEstimate(
                flops=4 * flops, bytes_accessed=8 << 20, transcendentals=0
            ),
            name="prep",
        )(*far)
        w1f, w2b, w2f, w1b, w1s, w2bs, w2s, w1bs, conds = matrices
        ca, cb, own, halo = pl.pallas_call(
            lambda *refs: col_kernel(rows, width, ny, *refs),
            out_shape=(edge, edge, edges, edges),
            compiler_params=limit(8),
            name="edge_cols",
        )(mine, ra, rb)
        ca, cb = swap(ca, cb, 1)

        ring = pltpu.VMEM((4 * step, 128), BF)
        rowwise = pltpu.VMEM((rows + 8, 128), F32)
        inner = jax.ShapeDtypeStruct(((rows + 2) * chans, 128), BF)
        acc = jax.ShapeDtypeStruct((step, step), F32)
        hid, dpre, acc1, acc2, cacc = pl.pallas_call(
            hidden_kernel,
            out_shape=(inner, inner, acc, acc, jax.ShapeDtypeStruct((2, chans, 128), F32)),
            scratch_shapes=[
                pltpu.VMEM(((rows + 4) * chans, 128), BF), rowwise, rowwise, ring, ring,
            ],
            compiler_params=limit(16),
            cost_estimate=pl.CostEstimate(
                flops=8 * flops, bytes_accessed=8 << 20, transcendentals=0
            ),
            name="hidden",
        )(
            keep_near(a3), phi_own, mask_own, halo,
            w1s, w2bs, conds,
        )

        fix = jax.ShapeDtypeStruct((4 * chans, 128), F32)
        count = (2 * step + chans) // 2
        wires = jax.ShapeDtypeStruct((count, 128), F32)
        cols = jax.ShapeDtypeStruct((chans, 512), BF)
        hcol, dcol, keep, give = pl.pallas_call(
            lambda *refs: edge_kernel(rows, nx, *refs),
            out_shape=(cols, cols, wires, wires),
            scratch_shapes=[pltpu.VMEM((2 * count, 128), F32)],
            compiler_params=limit(8),
            name="edge_parts",
        )(ca, cb, own, w1f, w2b, conds, acc1, acc2, cacc, gphi)
        hfix, dfix = pl.pallas_call(
            lambda *refs: fix_kernel(rows, *refs),
            out_shape=(fix, fix),
            compiler_params=limit(8),
            cost_estimate=pl.CostEstimate(
                flops=flops // 2, bytes_accessed=1 << 20, transcendentals=0
            ),
            name="edge_fixes",
        )(w2f, w1b, hcol, dcol)

        def output(with_phi, src, mid, fix, weights, name):
            return pl.pallas_call(
                lambda *refs: output_kernel(with_phi, *refs),
                out_shape=jax.ShapeDtypeStruct(src.shape, BF),
                scratch_shapes=[
                    pltpu.VMEM(((rows + 2) * step, 128), BF),
                    pltpu.VMEM((rows, chans, 128), F32),
                    pltpu.VMEM((chans, rows, 128), F32),
                    pltpu.VMEM(src.shape, BF),
                    pltpu.SemaphoreType.DMA(()),
                ],
                in_specs=[hbm] + [vmem] * 6,
                compiler_params=limit(16),
                cost_estimate=pl.CostEstimate(
                    flops=2 * flops, bytes_accessed=4 << 20, transcendentals=0
                ),
                name=name,
            )(src, phi_own, mask_own, mid, fix, weights, conds)

        moves = [(1 << k, 0) for k in range(1, ny.bit_length() - 1)]
        moves += [(0, 1 << k) for k in range(nx.bit_length() - 1)]
        rounds = [moves[k : k + 2] for k in range(0, len(moves), 2)]
        keep = keep + send(give, lambda a, b: (a ^ 1, b))
        outs = []
        for n, move in enumerate(rounds):
            if n == 0:
                keep, hfix = lax.optimization_barrier((keep, hfix))
                outs.append(output(True, far[0], hid, hfix, w2s, "delensed"))
            if n == len(rounds) - 1:
                keep, dfix = lax.optimization_barrier((keep, dfix))
                outs.append(output(False, far[1], dpre, dfix, w1bs, "grad_input"))
            keep = exchange(keep, move)
            if n in (0, len(rounds) - 1):
                keep, outs[-1] = lax.optimization_barrier((keep, outs[-1]))
        delensed, grad_input = outs
        other = send(keep, lambda a, b: (a ^ 1, b))

        factor = float(1.0 / (rows * ny * width * nx) ** 0.5)
        grads = jax.ShapeDtypeStruct((3, 3, chans, chans), F32)
        grad_w1, grad_w2, grad_cond = pl.pallas_call(
            lambda *refs: unpack_kernel(factor, *refs),
            out_shape=(grads, grads, jax.ShapeDtypeStruct((3, chans), F32)),
            scratch_shapes=[pltpu.VMEM((2 * count, 128), F32)],
            compiler_params=limit(8),
            name="unpack",
        )(keep, other)
        return delensed, grad_input, grad_w1, grad_w2, grad_cond

    return local


def solution(mesh):
    return jax.shard_map(
        build(mesh),
        mesh=mesh,
        in_specs=(
            P(None, "gy", "gx"),
            P("gy", "gx"),
            P(None, "gy", "gx"),
            P("gy", "gx"),
            P(),
            P(),
            P(),
            P(),
            P(),
        ),
        out_specs=(P(None, "gy", "gx"), P(None, "gy", "gx"), P(), P(), P()),
        check_vma=False,
    )
```

```python
import jax
import jax.numpy as jnp
from jax import lax
from jax.experimental import pallas as pl
from jax.experimental.pallas import tpu as pltpu
from jax.sharding import PartitionSpec as P

TILE = 8
BF = jnp.bfloat16
F32 = jnp.float32
NT = (((1,), (1,)), ((), ()))
NN = (((1,), (0,)), ((), ()))
TN = (((0,), (0,)), ((), ()))
R1 = 3
R2 = 4
GROUP1 = 6
GROUP2 = 8
COPY_STEP = 0.1


def lane_iota(rows):
    return lax.broadcasted_iota(jnp.int32, (rows, 128), 1)


def tile_rows(mask_ref):
    tcols = mask_ref.shape[1]
    lane = lax.broadcasted_iota(jnp.int32, (tcols, 128), 1)
    row = lax.broadcasted_iota(jnp.int32, (tcols, 128), 0)
    spread = (lane // TILE == row).astype(F32).astype(BF)
    return lax.dot_general(
        mask_ref[...].astype(F32).astype(BF), spread, NN, preferred_element_type=F32
    )


def is_odd(axis):
    return lax.rem(lax.axis_index(axis), 2) == 1


def received(axis, count, a_ref, b_ref):
    ends = (lax.axis_index(axis) == 0) | (lax.axis_index(axis) == count - 1)
    ra = a_ref[...]
    rb = jnp.where(ends, jnp.zeros_like(ra), b_ref[...])
    odd = is_odd(axis)
    return jnp.where(odd, ra, rb), jnp.where(odd, rb, ra)


def row_kernel(sky_ref, cot_ref, phi_ref, mask_ref, a_ref, b_ref, blocks, phis, tiles, sems):
    chans, rows, _ = sky_ref.shape
    copies = []
    for n, (src, dst) in enumerate(
        [
            (ref.at[:, pl.ds(first, 8), :], blocks.at[k])
            for k, (ref, first) in enumerate(
                ((sky_ref, 0), (cot_ref, 0), (sky_ref, rows - 8), (cot_ref, rows - 8))
            )
        ]
        + [(phi_ref.at[pl.ds(0, 16), :], phis.at[0]), (phi_ref.at[pl.ds(rows - 16, 16), :], phis.at[1])]
        + [(mask_ref, tiles)]
    ):
        copies.append(pltpu.make_async_copy(src, dst, sems.at[n]))
        copies[-1].start()
    for copy in copies:
        copy.wait()
    cells = tile_rows(tiles)
    odd = is_odd("gy")
    parts = []
    for side, (first, mrow) in enumerate(((0, 0), (6, tiles.shape[0] - 1))):
        keep = cells[mrow : mrow + 1]
        low = jnp.broadcast_to(keep, (chans, 128)).astype(BF)
        part = []
        for k in range(2):
            block = jnp.transpose(blocks[2 * side + k], (1, 0, 2))
            part += [block[first] * low, block[first + 1] * low]
        row = lax.broadcasted_iota(jnp.int32, (16, 128), 0)
        prow = phis[side].astype(F32)[15 * side : 15 * side + 1]
        prow = jnp.broadcast_to(prow, (16, 128))
        part.append(jnp.where(row == 0, prow, jnp.where(row == 1, keep, 0.0)).astype(BF))
        parts.append(jnp.concatenate(part, axis=0))
    up, down = parts
    a_ref[...] = jnp.where(odd, up, down)
    b_ref[...] = jnp.where(odd, down, up)


def prep_kernel(*refs):
    far, (a3, own_ref, gphi_ref, phix, maskx), mats = refs[:9], refs[9:14], refs[14:23]
    strip, near, sems = refs[23], refs[24:33], refs[33]
    copies = {
        n: pltpu.make_async_copy(far[n], near[n], sems.at[n])
        for n in (3, 2, 4, 5, 6, 7, 8, 0, 1)
    }
    for copy in copies.values():
        copy.start()
    for n in (3, 2, 4, 5, 6, 7, 8):
        copies[n].wait()
    weight_matrices(*near[4:], *mats)
    copies[0].wait()
    copies[1].wait()
    own_fields(*near[:4], a3, own_ref, gphi_ref, phix, maskx, strip)


def own_fields(
    sky_ref, cot_ref, phi_ref, mask_ref, a3, own_ref, gphi_ref, phix, maskx, strip
):
    chans, rows, width = sky_ref.shape
    size = own_ref.shape[1]
    step = 3 * chans
    half = chans // 2
    cells = tile_rows(mask_ref)
    phi = phi_ref[...].astype(F32)
    phix[...] = phi
    for t in range(mask_ref.shape[0]):
        maskx[TILE * t : TILE * (t + 1)] = jnp.broadcast_to(cells[t : t + 1], (TILE, 128))
    lane8 = lane_iota(8)
    row8 = lax.broadcasted_iota(jnp.int32, (8, 128), 0)
    pick = ((row8 < 2) & (lane8 == row8)) | (
        (row8 >= 2) & (row8 < 4) & (lane8 == row8 + (width - 4))
    )
    pick = pick.astype(F32).astype(BF)
    trows, tcols = mask_ref.shape
    prow = lax.broadcasted_iota(jnp.int32, (8, tcols), 0)
    pcol = lax.broadcasted_iota(jnp.int32, (8, tcols), 1)
    pick_t = ((prow < 2) & (pcol == 0)) | ((prow >= 2) & (prow < 4) & (pcol == tcols - 1))
    edge = lax.dot_general(
        pick_t.astype(F32).astype(BF),
        mask_ref[...].astype(F32).astype(BF),
        NT,
        preferred_element_type=F32,
    )
    lane_t = lax.broadcasted_iota(jnp.int32, (trows, 128), 1)
    row_t = lax.broadcasted_iota(jnp.int32, (trows, 128), 0)
    spread = (lane_t // TILE == row_t).astype(F32).astype(BF)
    keep = lax.dot_general(edge.astype(BF), spread, NN, preferred_element_type=F32)
    phis = lax.dot_general(pick, phi_ref[...], NT, preferred_element_type=F32)
    phis = jnp.concatenate([phis, jnp.zeros((8, 128 - rows), F32)], axis=1)
    gphi = jnp.zeros((chans, 128), F32)
    for which, src in ((0, sky_ref), (1, cot_ref)):
        both = jnp.concatenate([src[:half], src[half:]], axis=1).reshape(half * 128, width)
        flat = lax.dot_general(pick, both, NT, preferred_element_type=F32)
        for j in range(half):
            strip[which, 8 * j : 8 * j + 8] = flat[:, 128 * j : 128 * j + 128]
        for k in range(4):
            part = strip[which, pl.ds(k, half, stride=8), :]
            col = jnp.concatenate([part, pltpu.roll(part, 64, 1)], axis=0)
            base = (2 * which + k % 2) * chans
            own_ref[k // 2, base : base + chans] = (col * keep[k : k + 1]).astype(BF)
        for j in range(rows // 16):
            block = jnp.transpose(src[:, 16 * j : 16 * j + 16, :], (1, 0, 2))
            for t in range(2):
                low = jnp.broadcast_to(cells[2 * j + t : 2 * j + t + 1], (chans, 128)).astype(BF)
                for n in range(TILE):
                    y = 16 * j + TILE * t + n
                    value = block[TILE * t + n] * low
                    a3[which, y * step : (y + 1) * step] = three_copies(value)
                    if which:
                        gphi = gphi + value.astype(F32) * phi[y : y + 1]
    gphi_ref[...] = gphi
    row = lax.broadcasted_iota(jnp.int32, (16, 128), 0)
    for side, k in ((0, 0), (1, 3)):
        extra = jnp.where(
            row == 0,
            jnp.broadcast_to(phis[k : k + 1], (16, 128)),
            jnp.where(row == 1, jnp.broadcast_to(keep[k : k + 1], (16, 128)), 0.0),
        )
        own_ref[side, 4 * chans : size] = extra.astype(BF)


def three_copies(value):
    return jnp.concatenate([pltpu.roll(value, 1, 1), value, pltpu.roll(value, 127, 1)], axis=0)


def col_kernel(rows, width, count, mine_ref, a_ref, b_ref, sa_ref, sb_ref, own_ref, halo_ref):
    size = a_ref.shape[0]
    tops, bots = received("gy", count, a_ref, b_ref)
    halo_ref[0] = tops
    halo_ref[1] = bots
    chans = (size - 16) // 4
    lane = lane_iota(chans)
    lane16 = lane_iota(16)
    sides = []
    for side in range(2):
        parts = []
        for m in range(4):
            which, k = divmod(m, 2)
            at = k + (width - 2) * side
            col = mine_ref[side, m * chans : (m + 1) * chans]
            for value, where in ((tops, (126, 127)), (bots, (rows, rows + 1))):
                for n in range(2):
                    base = (2 * which + n) * chans
                    cell = value[base : base + chans, at : at + 1]
                    col = jnp.where(lane == where[n], jnp.broadcast_to(cell, col.shape), col)
            parts.append(col)
        at = (width - 1) * side
        extra = mine_ref[side, 4 * chans : size].astype(F32)
        for value, where in ((tops, 127), (bots, rows)):
            cell = value[4 * chans : size].astype(F32)[:, at : at + 1]
            extra = jnp.where(lane16 == where, jnp.broadcast_to(cell, (16, 128)), extra)
        parts.append(extra.astype(BF))
        sides.append(jnp.concatenate(parts, axis=0))
        own_ref[side] = sides[side]
    odd_x = is_odd("gx")
    sa_ref[...] = jnp.where(odd_x, sides[0], sides[1])
    sb_ref[...] = jnp.where(odd_x, sides[1], sides[0])


def silu_parts(pre):
    sigma = 1.0 / (1.0 + jnp.exp(-pre))
    return pre * sigma, sigma * (1.0 + pre * (1.0 - sigma))


def hidden_kernel(
    a3, phi_own, mask_own, halo_ref, w1s_ref, w2ts_ref, cond_ref,
    hid_ref, dpre_ref, acc1, acc2, cacc,
    dz, phix, maskx, ringx, ringg,
):
    rows, width = phi_own.shape
    a3x, a3g = a3.at[0], a3.at[1]
    size = halo_ref.shape[1]
    chans = (size - 16) // 4
    step = 3 * chans
    lane1 = lane_iota(1)
    inside = jnp.where((lane1 == 0) | (lane1 == 127), 0.0, 1.0)
    for k, at in ((0, 0), (1, rows + 1)):
        extra = halo_ref[k, 4 * chans : size].astype(F32)
        phix[at : at + 1] = extra[0:1]
        maskx[at : at + 1] = extra[1:2] * inside
    phix[1 : rows + 1] = phi_own[...]
    maskx[1 : rows + 1] = mask_own[...] * inside
    for which, ring in ((0, ringx), (1, ringg)):
        for k in range(2):
            for n in range(2):
                base = (2 * which + n) * chans
                ring[(2 * k + n) * step : (2 * k + n + 1) * step] = three_copies(
                    halo_ref[k, base : base + chans]
                )

    def window(own, ring, y, count):
        parts = []
        if y < 0:
            parts.append(ring[(y + 2) * step : min(2, y + 2 + count) * step])
        low, high = max(y, 0), min(y + count, rows)
        if low < high:
            parts.append(own[low * step : high * step])
        if y + count > rows:
            low = max(y, rows) - rows
            parts.append(ring[(2 + low) * step : (2 + y + count - rows) * step])
        return parts[0] if len(parts) == 1 else jnp.concatenate(parts, axis=0)

    gain = cond_ref[:, 0:1]
    bias = cond_ref[:, 1:2]
    split = (rows + 2) // 2
    zero = jnp.zeros((chans, 128), BF)
    for y in (-2, -1, rows, rows + 1):
        dz[(y + 2) * chans : (y + 3) * chans] = zero

    def first_pass(it, dphi, dsum):
        y0 = R1 * it - 1

        def both(own, ring):
            pair = [window(own, ring, y0 - 1 + h * split, R1 + 2) for h in range(2)]
            return jnp.concatenate(pair, axis=1)

        pre = lax.dot_general(w1s_ref[...], both(a3x, ringx), NN, preferred_element_type=F32)
        back = lax.dot_general(w2ts_ref[...], both(a3g, ringg), NN, preferred_element_type=F32)
        for h in range(2):
            for r in range(R1):
                row = y0 + h * split + r + 1
                here = (slice(r * chans, (r + 1) * chans), slice(h * 128, h * 128 + 128))
                keep = maskx[row : row + 1]
                act, slope = silu_parts(pre[here] + gain * phix[row : row + 1] + bias)
                base = row * chans
                hid_ref[base : base + chans] = (act * keep).astype(BF)
                value = (back[here] * keep * slope).astype(BF)
                dpre_ref[base : base + chans] = value
                if 1 <= row <= rows:
                    dz[base + chans : base + 2 * chans] = value
                    wide = value.astype(F32)
                    dphi = dphi + wide * phix[row : row + 1]
                    dsum = dsum + wide
        return dphi, dsum

    dphi = jnp.zeros((chans, 128), F32)
    dsum = jnp.zeros((chans, 128), F32)
    for it in range(split // R1):
        dphi, dsum = first_pass(it, dphi, dsum)
    cacc[0] = dphi
    cacc[1] = dsum

    acc1[...] = jnp.zeros_like(acc1)
    acc2[...] = jnp.zeros_like(acc2)

    def rows_of(src, start, size):
        return src[start : start + size]

    def grads_one(it):
        ys = [GROUP1 * it + n - 1 for n in range(GROUP1)]
        acc1[...] += lax.dot_general(
            jnp.concatenate([rows_of(dz, (y + 1) * chans, step) for y in ys], axis=1),
            jnp.concatenate([window(a3x, ringx, y, 1) for y in ys], axis=1),
            NT, preferred_element_type=F32,
        )

    def grads_two(it):
        ys = [GROUP2 * it + n for n in range(GROUP2)]
        acc2[...] += lax.dot_general(
            jnp.concatenate([window(a3g, ringg, y, 1) for y in ys], axis=1),
            jnp.concatenate([rows_of(hid_ref, y * chans, step) for y in ys], axis=1),
            NT, preferred_element_type=F32,
        )

    for it in range((rows + 2) // GROUP1):
        grads_one(it)
    for it in range(rows // GROUP2):
        grads_two(it)


def edge_kernel(
    rows, count, a_ref, b_ref, own_ref, w1c_ref, w2tc_ref, cond_ref,
    acc1, acc2, cacc, gphi_ref,
    hcol_ref, dcol_ref, keep_ref, give_ref, wire,
):
    size = a_ref.shape[0]
    chans = (size - 16) // 4
    step = 3 * chans
    lft, rgt = received("gx", count, a_ref, b_ref)
    own_l, own_r = own_ref[0], own_ref[1]

    def at(value, which, n):
        base = (2 * which + n) * chans
        return value[base : base + chans]

    def columns(which):
        return [at(v, which, n) for v in (lft, own_l, own_r, rgt) for n in range(2)]

    centres = (1, 2, 5, 6)

    def taps_of(cols):
        pieces = []
        for ky in range(3):
            moved = [c if ky == 1 else pltpu.roll(c, (1, 0, 127)[ky], 1) for c in cols]
            for kx in range(3):
                pieces.append(jnp.concatenate([moved[c + kx - 1] for c in centres], axis=1))
        return jnp.concatenate(pieces, axis=0)

    x_taps = taps_of(columns(0))
    g_cols = columns(1)
    extra = [v[4 * chans : size].astype(F32) for v in (lft, own_l, own_r, rgt)]
    phi_c = jnp.concatenate([e[0:1] for e in extra], axis=1)
    mask_c = jnp.concatenate([e[1:2] for e in extra], axis=1)
    pre = lax.dot_general(w1c_ref[...], x_taps, NN, preferred_element_type=F32)
    back = lax.dot_general(w2tc_ref[...], taps_of(g_cols), NN, preferred_element_type=F32)
    act, slope = silu_parts(pre + cond_ref[:, 0:1] * phi_c + cond_ref[:, 1:2])
    hcol = (act * mask_c).astype(BF)
    dcol = (back * mask_c * slope).astype(BF)
    hcol_ref[...] = hcol
    dcol_ref[...] = dcol

    mine = jnp.broadcast_to((lane_iota(1) < rows).astype(F32), (chans, 128)).astype(BF)
    d_own = [dcol[:, 128:256] * mine, dcol[:, 256:384] * mine]
    part1 = lax.dot_general(
        jnp.concatenate(d_own, axis=1), x_taps[:, 128:384], NT, preferred_element_type=F32
    )
    h_cols = [hcol[:, 128 * k : 128 * k + 128] for k in range(4)]
    g_own = {k: g_cols[n] * mine for k, n in ((0, 2), (1, 3), (2, 4), (3, 5))}
    for kx, pairs in (
        (0, ((0, 0), (1, 1))),
        (1, ((0, 1), (3, 2))),
        (2, ((2, 2), (3, 3))),
    ):
        lhs = jnp.concatenate([g_own[g] for g, _ in pairs], axis=1)
        rhs = []
        for ky in range(3):
            moved = [
                h_cols[h] if ky == 1 else pltpu.roll(h_cols[h], (1, 0, 127)[ky], 1)
                for _, h in pairs
            ]
            rhs.append(jnp.concatenate(moved, axis=1))
        part2 = lax.dot_general(
            lhs, jnp.concatenate(rhs, axis=0), NT, preferred_element_type=F32
        )
        low = (2 - kx) * chans
        wide = jnp.concatenate(
            [
                acc1[low : low + chans] + part1[:, kx * step : (kx + 1) * step],
                acc2[low : low + chans] + part2,
            ],
            axis=1,
        )
        wire[low : low + chans] = wide[:, :128]
        wire[step + low : step + low + chans] = wide[:, 128:256]
        if kx == 0:
            tails = []
        tails.insert(0, wide[:, 256 : 2 * step])
    dphi, dsum = cacc[0], cacc[1]
    for d, k in ((d_own[0], 1), (d_own[1], 2)):
        dphi = dphi + d.astype(F32) * extra[k][0:1]
        dsum = dsum + d.astype(F32)
    sums = [jnp.sum(v, axis=1, keepdims=True) for v in (dphi, dsum, gphi_ref[...])]
    base = 3 * tails[0].shape[1]
    place = jnp.maximum(lane_iota(chans) - base, 0)
    which = lax.rem(place, 3)
    wide_sums = [jnp.broadcast_to(v, (chans, 128)) for v in sums]
    coded = jnp.where(which == 0, wide_sums[0], jnp.where(which == 1, *wide_sums[1:]))
    coded = coded * (1.0 + COPY_STEP * (place // 3).astype(F32))
    wire[2 * step : 2 * step + chans] = jnp.concatenate(tails + [coded[:, base:]], axis=1)
    half = wire.shape[0] // 2
    core = lax.rem(lax.axis_index("gy"), 2)
    keep_ref[...] = wire[pl.ds(pl.multiple_of(core * half, 8), half), :]
    give_ref[...] = wire[pl.ds(pl.multiple_of((1 - core) * half, 8), half), :]


def fix_kernel(rows, w2c_ref, w1tc_ref, hcol_ref, dcol_ref, hfix_ref, dfix_ref):
    chans = hcol_ref.shape[0]
    none = jnp.zeros((chans, 128), BF)
    half = chans // 2
    lane = lane_iota(half)
    for weights, field, fix in ((w2c_ref, hcol_ref, hfix_ref), (w1tc_ref, dcol_ref, dfix_ref)):
        f = [field[:, 128 * k : 128 * k + 128] for k in range(4)]
        pieces = []
        for ky in range(3):
            m = [c if ky == 1 else pltpu.roll(c, (1, 0, 127)[ky], 1) for c in f]
            pieces.append(jnp.concatenate([m[0], m[1], none, none], axis=1))
            pieces.append(jnp.concatenate([m[1], none, none, m[2]], axis=1))
            pieces.append(jnp.concatenate([none, none, m[2], m[3]], axis=1))
        fixes = lax.dot_general(
            weights[...], jnp.concatenate(pieces, axis=0), NN, preferred_element_type=F32
        )
        for k in range(4):
            col = fixes[:, 128 * k : 128 * k + 128]
            part = jnp.where(lane < rows, col[:half], pltpu.roll(col[half:], rows, 1))
            high = part.astype(BF).astype(F32)
            fix[pl.ds(k, half, stride=8), :] = high
            fix[pl.ds(4 + k, half, stride=8), :] = part - high


def output_kernel(
    with_phi, src_hbm, phi_ref, mask_ref, mid_ref, fix_ref, weights_ref, cond_ref,
    out_ref, a3, rowbuf, fixbuf, src_ref, sem,
):
    chans, rows, width = src_ref.shape
    step = 3 * chans
    half = chans // 2
    fetch = pltpu.make_async_copy(src_hbm, src_ref, sem)
    fetch.start()
    if with_phi:
        gain = cond_ref[:, 2:3]
    lane8 = lane_iota(8)
    row8 = lax.rem(lax.broadcasted_iota(jnp.int32, (8, 128), 0), 4)
    place = (lane8 == jnp.where(row8 < 2, row8, row8 + (width - 4))).astype(F32).astype(BF)
    for j in range(half):
        got = lax.dot_general(
            fix_ref[8 * j : 8 * j + 8].astype(BF), place, TN, preferred_element_type=F32
        )
        fixbuf[j] = got[:rows]
        fixbuf[j + half] = got[rows:]

    for y in range(rows + 2):
        centre = mid_ref[y * chans : (y + 1) * chans]
        base = y * step
        a3[base : base + chans] = pltpu.roll(centre, 1, 1)
        a3[base + chans : base + 2 * chans] = centre
        a3[base + 2 * chans : base + 3 * chans] = pltpu.roll(centre, 127, 1)

    for it in range(rows // (2 * R2)):
        y0 = R2 * it
        got = lax.dot_general(
            weights_ref[...],
            jnp.concatenate(
                [a3[(y0 + h) * step : (y0 + h + R2 + 2) * step] for h in (0, rows // 2)], axis=1
            ),
            NN, preferred_element_type=F32,
        )
        for h in range(2):
            for r in range(R2):
                y = y0 + h * (rows // 2) + r
                part = got[r * chans : (r + 1) * chans, h * 128 : h * 128 + 128]
                if with_phi:
                    part = part + gain * phi_ref[y : y + 1]
                rowbuf[y] = part

    fetch.wait()
    for j in range(rows // 16):
        here = slice(16 * j, 16 * j + 16)
        keep = mask_ref[here]
        total = jnp.transpose(rowbuf[here], (1, 0, 2)) + fixbuf[:, here, :]
        out_ref[:, here, :] = ((total + src_ref[:, here, :].astype(F32)) * keep[None]).astype(BF)


def unpack_kernel(factor, keep_ref, other_ref, w1_ref, w2_ref, cond_ref, wire):
    chans = w1_ref.shape[2]
    step = 3 * chans
    count = keep_ref.shape[0]
    core = lax.rem(lax.axis_index("gy"), 2)
    wire[pl.ds(pl.multiple_of(core * count, 8), count), :] = keep_ref[...]
    wire[pl.ds(pl.multiple_of((1 - core) * count, 8), count), :] = other_ref[...]
    tail = wire[2 * step : 2 * step + chans] * factor
    rest_w = 2 * step - 256
    for n in range(3):
        low = n * chans
        wide = jnp.concatenate(
            [
                wire[low : low + chans] * factor,
                wire[step + low : step + low + chans] * factor,
                tail[:, n * rest_w : (n + 1) * rest_w],
            ],
            axis=1,
        )
        for k in range(3):
            w1_ref[2 - n, k] = wide[:, k * chans : (k + 1) * chans]
            w2_ref[k, 2 - n] = wide[:, step + k * chans : step + (k + 1) * chans]
    turned = jnp.transpose(tail)[:, :chans]
    copies = (128 - 3 * rest_w) // 3
    total = jnp.zeros((3, chans), F32)
    for j in range(copies):
        at = 3 * (rest_w + j)
        total = total + turned[at : at + 3] * (1.0 / (copies * (1.0 + COPY_STEP * j)))
    cond_ref[...] = total


def limit(mib):
    return pltpu.CompilerParams(vmem_limit_bytes=mib << 20)


def keep_near(value):
    return pltpu.with_memory_space_constraint(value, pltpu.VMEM)


def stacked(block, count):
    chans, taps = block.shape
    step = taps // 3
    rows = []
    for r in range(count):
        parts = [block]
        if r:
            parts.insert(0, jnp.zeros((chans, r * step), BF))
        if r < count - 1:
            parts.append(jnp.zeros((chans, (count - 1 - r) * step), BF))
        rows.append(jnp.concatenate(parts, axis=1))
    return jnp.concatenate(rows, axis=0)


def weight_matrices(
    one, two, vec0, vec1, vec2,
    w1f_ref, w2b_ref, w2f_ref, w1b_ref, w1s_ref, w2bs_ref, w2s_ref, w1bs_ref, cond_ref,
):
    chans = one.shape[2]
    for src, fwd, fwd_s, count, bwd, bwd_s, back in (
        (one, w1f_ref, w1s_ref, R1, w1b_ref, w1bs_ref, R2),
        (two, w2f_ref, w2s_ref, R2, w2b_ref, w2bs_ref, R1),
    ):
        taps = [src[k // 3, k % 3] for k in range(9)]
        plain = jnp.concatenate(taps, axis=1)
        turned = jnp.concatenate(
            [jnp.transpose(t.astype(F32)).astype(BF) for t in taps[::-1]], axis=1
        )
        fwd[...] = plain
        bwd[...] = turned
        fwd_s[...] = stacked(plain, count)
        bwd_s[...] = stacked(turned, back)
    row = lax.broadcasted_iota(jnp.int32, (8, chans), 0)
    table = jnp.zeros((8, chans), F32)
    for k, ref in enumerate((vec0, vec1, vec2)):
        table = jnp.where(row == k, jnp.broadcast_to(ref[...].reshape(1, chans), (8, chans)), table)
    table = jnp.concatenate([table, jnp.zeros((8, 128 - chans), F32)], axis=1)
    table = jnp.concatenate([table, jnp.zeros((120, 128), F32)], axis=0)
    cond_ref[...] = jnp.transpose(table)[:chans]


def build(mesh):
    ny, nx = mesh.shape["gy"], mesh.shape["gx"]
    axes = ("gy", "gx")

    def send(value, move):
        pairs = []
        for a in range(ny):
            for b in range(nx):
                to = move(a, b)
                pairs.append((a * nx + b, to[0] * nx + to[1]))
        return lax.ppermute(value, axes, pairs)

    def swap(first, second, axis):
        def partner(offset):
            def move(a, b):
                v = [a, b]
                v[axis] += 1 if (v[axis] + offset) % 2 == 0 else -1
                if 0 <= v[axis] < (ny, nx)[axis]:
                    return v
                return (a, b ^ 1) if axis == 0 else (a ^ 1, b)

            return move

        return send(first, partner(0)), send(second, partner(1))

    def exchange(value, moves):
        sent = value.astype(BF)
        got = [send(sent, lambda a, b: (a ^ m[0], b ^ m[1])).astype(F32) for m in moves]
        if len(moves) == 1:
            return sent.astype(F32) + got[0]
        both = (moves[0][0] ^ moves[1][0], moves[0][1] ^ moves[1][1])
        far = send(sent, lambda a, b: (a ^ both[0], b ^ both[1])).astype(F32)
        return (sent.astype(F32) + got[0]) + (got[1] + far)

    def local(
        sky, lens_phi, cotangent, tile_mask, weight_one, weight_two, cond_one, bias_one, cond_two
    ):
        chans, rows, width = sky.shape
        step = 3 * chans
        size = 4 * chans + 16
        assert 2 * rows == 128 and width == 128
        edge = jax.ShapeDtypeStruct((size, 128), BF)
        edges = jax.ShapeDtypeStruct((2, size, 128), BF)
        hbm = pl.BlockSpec(memory_space=pltpu.HBM)
        far = [
            pltpu.with_memory_space_constraint(v, pltpu.HBM)
            for v in (
                sky, cotangent, lens_phi, tile_mask,
                weight_one, weight_two, cond_one, bias_one, cond_two,
            )
        ]
        vmem = pl.BlockSpec(memory_space=pltpu.VMEM)
        ra, rb = pl.pallas_call(
            row_kernel,
            out_shape=(edge, edge),
            in_specs=[hbm] * 4,
            scratch_shapes=[
                pltpu.VMEM((4, chans, 8, width), BF),
                pltpu.VMEM((2, 16, width), BF),
                pltpu.VMEM(tile_mask.shape, jnp.int32),
                pltpu.SemaphoreType.DMA((7,)),
            ],
            compiler_params=limit(8),
            name="edge_rows",
        )(*far[:4])
        ra, rb = swap(ra, rb, 0)

        flat_w = jax.ShapeDtypeStruct((chans, 3 * step), BF)
        first_w = jax.ShapeDtypeStruct((R1 * chans, (R1 + 2) * step), BF)
        second_w = jax.ShapeDtypeStruct((R2 * chans, (R2 + 2) * step), BF)
        matrices = (
            flat_w, flat_w, flat_w, flat_w, first_w, first_w, second_w, second_w,
            jax.ShapeDtypeStruct((chans, 128), F32),
        )
        flops = 2 * 9 * chans * chans * rows * width
        field = jax.ShapeDtypeStruct((2, rows * step, 128), BF)
        flat = jax.ShapeDtypeStruct(lens_phi.shape, F32)
        a3, mine, gphi, phi_own, mask_own, *matrices = pl.pallas_call(
            prep_kernel,
            out_shape=(field, edges, jax.ShapeDtypeStruct((chans, 128), F32), flat, flat)
            + matrices,
            in_specs=[hbm] * 9,
            scratch_shapes=[pltpu.VMEM((2, 8 * chans // 2, 128), F32)]
            + [pltpu.VMEM(v.shape, v.dtype) for v in far]
            + [pltpu.SemaphoreType.DMA((9,))],
            compiler_params=limit(8),
            cost_estimate=pl.CostEstimate(
                flops=4 * flops, bytes_accessed=8 << 20, transcendentals=0
            ),
            name="prep",
        )(*far)
        w1f, w2b, w2f, w1b, w1s, w2bs, w2s, w1bs, conds = matrices
        ca, cb, own, halo = pl.pallas_call(
            lambda *refs: col_kernel(rows, width, ny, *refs),
            out_shape=(edge, edge, edges, edges),
            compiler_params=limit(8),
            name="edge_cols",
        )(mine, ra, rb)
        ca, cb = swap(ca, cb, 1)

        ring = pltpu.VMEM((4 * step, 128), BF)
        rowwise = pltpu.VMEM((rows + 8, 128), F32)
        inner = jax.ShapeDtypeStruct(((rows + 2) * chans, 128), BF)
        acc = jax.ShapeDtypeStruct((step, step), F32)
        hid, dpre, acc1, acc2, cacc = pl.pallas_call(
            hidden_kernel,
            out_shape=(inner, inner, acc, acc, jax.ShapeDtypeStruct((2, chans, 128), F32)),
            scratch_shapes=[
                pltpu.VMEM(((rows + 4) * chans, 128), BF), rowwise, rowwise, ring, ring,
            ],
            compiler_params=limit(16),
            cost_estimate=pl.CostEstimate(
                flops=8 * flops, bytes_accessed=8 << 20, transcendentals=0
            ),
            name="hidden",
        )(
            keep_near(a3), phi_own, mask_own, halo,
            w1s, w2bs, conds,
        )

        fix = jax.ShapeDtypeStruct((4 * chans, 128), F32)
        count = (2 * step + chans) // 2
        wires = jax.ShapeDtypeStruct((count, 128), F32)
        cols = jax.ShapeDtypeStruct((chans, 512), BF)
        hcol, dcol, keep, give = pl.pallas_call(
            lambda *refs: edge_kernel(rows, nx, *refs),
            out_shape=(cols, cols, wires, wires),
            scratch_shapes=[pltpu.VMEM((2 * count, 128), F32)],
            compiler_params=limit(8),
            name="edge_parts",
        )(ca, cb, own, w1f, w2b, conds, acc1, acc2, cacc, gphi)
        hfix, dfix = pl.pallas_call(
            lambda *refs: fix_kernel(rows, *refs),
            out_shape=(fix, fix),
            compiler_params=limit(8),
            cost_estimate=pl.CostEstimate(
                flops=flops // 2, bytes_accessed=1 << 20, transcendentals=0
            ),
            name="edge_fixes",
        )(w2f, w1b, hcol, dcol)

        def output(with_phi, src, mid, fix, weights, name):
            return pl.pallas_call(
                lambda *refs: output_kernel(with_phi, *refs),
                out_shape=jax.ShapeDtypeStruct(src.shape, BF),
                scratch_shapes=[
                    pltpu.VMEM(((rows + 2) * step, 128), BF),
                    pltpu.VMEM((rows, chans, 128), F32),
                    pltpu.VMEM((chans, rows, 128), F32),
                    pltpu.VMEM(src.shape, BF),
                    pltpu.SemaphoreType.DMA(()),
                ],
                in_specs=[hbm] + [vmem] * 6,
                compiler_params=limit(16),
                cost_estimate=pl.CostEstimate(
                    flops=2 * flops, bytes_accessed=4 << 20, transcendentals=0
                ),
                name=name,
            )(src, phi_own, mask_own, mid, fix, weights, conds)

        moves = [(1 << k, 0) for k in range(1, ny.bit_length() - 1)]
        moves += [(0, 1 << k) for k in range(nx.bit_length() - 1)]
        rounds = [moves[k : k + 2] for k in range(0, len(moves), 2)]
        keep = keep + send(give, lambda a, b: (a ^ 1, b))
        outs = []
        for n, move in enumerate(rounds):
            if n == 0:
                keep, hfix = lax.optimization_barrier((keep, hfix))
                outs.append(output(True, far[0], hid, hfix, w2s, "delensed"))
            if n == len(rounds) - 1:
                keep, dfix = lax.optimization_barrier((keep, dfix))
                outs.append(output(False, far[1], dpre, dfix, w1bs, "grad_input"))
            keep = exchange(keep, move)
            if n in (0, len(rounds) - 1):
                keep, outs[-1] = lax.optimization_barrier((keep, outs[-1]))
        delensed, grad_input = outs
        other = send(keep, lambda a, b: (a ^ 1, b))

        factor = float(1.0 / (rows * ny * width * nx) ** 0.5)
        grads = jax.ShapeDtypeStruct((3, 3, chans, chans), F32)
        grad_w1, grad_w2, grad_cond = pl.pallas_call(
            lambda *refs: unpack_kernel(factor, *refs),
            out_shape=(grads, grads, jax.ShapeDtypeStruct((3, chans), F32)),
            scratch_shapes=[pltpu.VMEM((2 * count, 128), F32)],
            compiler_params=limit(8),
            name="unpack",
        )(keep, other)
        return delensed, grad_input, grad_w1, grad_w2, grad_cond

    return local


def solution(mesh):
    return jax.shard_map(
        build(mesh),
        mesh=mesh,
        in_specs=(
            P(None, "gy", "gx"),
            P("gy", "gx"),
            P(None, "gy", "gx"),
            P("gy", "gx"),
            P(),
            P(),
            P(),
            P(),
            P(),
        ),
        out_specs=(P(None, "gy", "gx"), P(None, "gy", "gx"), P(), P(), P()),
        check_vma=False,
    )
```

```python
import jax
import jax.numpy as jnp
from jax import lax
from jax.experimental import pallas as pl
from jax.experimental.pallas import tpu as pltpu
from jax.sharding import PartitionSpec as P

TILE = 8
BF = jnp.bfloat16
F32 = jnp.float32
NT = (((1,), (1,)), ((), ()))
NN = (((1,), (0,)), ((), ()))
TN = (((0,), (0,)), ((), ()))
R1 = 3
R2 = 4
GROUP1 = 6
GROUP2 = 8
COPY_STEP = 0.1


def lane_iota(rows):
    return lax.broadcasted_iota(jnp.int32, (rows, 128), 1)


def tile_rows(mask_ref):
    tcols = mask_ref.shape[1]
    lane = lax.broadcasted_iota(jnp.int32, (tcols, 128), 1)
    row = lax.broadcasted_iota(jnp.int32, (tcols, 128), 0)
    spread = (lane // TILE == row).astype(F32).astype(BF)
    return lax.dot_general(
        mask_ref[...].astype(F32).astype(BF), spread, NN, preferred_element_type=F32
    )


def is_odd(axis):
    return lax.rem(lax.axis_index(axis), 2) == 1


def received(axis, count, a_ref, b_ref):
    ends = (lax.axis_index(axis) == 0) | (lax.axis_index(axis) == count - 1)
    ra = a_ref[...]
    rb = jnp.where(ends, jnp.zeros_like(ra), b_ref[...])
    odd = is_odd(axis)
    return jnp.where(odd, ra, rb), jnp.where(odd, rb, ra)


def row_kernel(sky_ref, cot_ref, phi_ref, mask_ref, a_ref, b_ref, blocks, phis, tiles, sems):
    chans, rows, _ = sky_ref.shape
    copies = []
    for n, (src, dst) in enumerate(
        [
            (ref.at[:, pl.ds(first, 8), :], blocks.at[k])
            for k, (ref, first) in enumerate(
                ((sky_ref, 0), (cot_ref, 0), (sky_ref, rows - 8), (cot_ref, rows - 8))
            )
        ]
        + [(phi_ref.at[pl.ds(0, 16), :], phis.at[0]), (phi_ref.at[pl.ds(rows - 16, 16), :], phis.at[1])]
        + [(mask_ref, tiles)]
    ):
        copies.append(pltpu.make_async_copy(src, dst, sems.at[n]))
        copies[-1].start()
    for copy in copies:
        copy.wait()
    cells = tile_rows(tiles)
    odd = is_odd("gy")
    parts = []
    for side, (first, mrow) in enumerate(((0, 0), (6, tiles.shape[0] - 1))):
        keep = cells[mrow : mrow + 1]
        low = jnp.broadcast_to(keep, (chans, 128)).astype(BF)
        part = []
        for k in range(2):
            block = jnp.transpose(blocks[2 * side + k], (1, 0, 2))
            part += [block[first] * low, block[first + 1] * low]
        row = lax.broadcasted_iota(jnp.int32, (16, 128), 0)
        prow = phis[side].astype(F32)[15 * side : 15 * side + 1]
        prow = jnp.broadcast_to(prow, (16, 128))
        part.append(jnp.where(row == 0, prow, jnp.where(row == 1, keep, 0.0)).astype(BF))
        parts.append(jnp.concatenate(part, axis=0))
    up, down = parts
    a_ref[...] = jnp.where(odd, up, down)
    b_ref[...] = jnp.where(odd, down, up)


def prep_kernel(*refs):
    far, (a3, own_ref, gphi_ref, phix, maskx), mats = refs[:9], refs[9:14], refs[14:23]
    strip, near, sems = refs[23], refs[24:33], refs[33]
    copies = {
        n: pltpu.make_async_copy(far[n], near[n], sems.at[n])
        for n in (3, 2, 4, 5, 6, 7, 8, 0, 1)
    }
    for copy in copies.values():
        copy.start()
    for n in (3, 2, 4, 5, 6, 7, 8):
        copies[n].wait()
    weight_matrices(*near[4:], *mats)
    copies[0].wait()
    copies[1].wait()
    own_fields(*near[:4], a3, own_ref, gphi_ref, phix, maskx, strip)


def own_fields(
    sky_ref, cot_ref, phi_ref, mask_ref, a3, own_ref, gphi_ref, phix, maskx, strip
):
    chans, rows, width = sky_ref.shape
    size = own_ref.shape[1]
    step = 3 * chans
    half = chans // 2
    cells = tile_rows(mask_ref)
    phi = phi_ref[...].astype(F32)
    phix[...] = phi
    for t in range(mask_ref.shape[0]):
        maskx[TILE * t : TILE * (t + 1)] = jnp.broadcast_to(cells[t : t + 1], (TILE, 128))
    lane8 = lane_iota(8)
    row8 = lax.broadcasted_iota(jnp.int32, (8, 128), 0)
    pick = ((row8 < 2) & (lane8 == row8)) | (
        (row8 >= 2) & (row8 < 4) & (lane8 == row8 + (width - 4))
    )
    pick = pick.astype(F32).astype(BF)
    trows, tcols = mask_ref.shape
    prow = lax.broadcasted_iota(jnp.int32, (8, tcols), 0)
    pcol = lax.broadcasted_iota(jnp.int32, (8, tcols), 1)
    pick_t = ((prow < 2) & (pcol == 0)) | ((prow >= 2) & (prow < 4) & (pcol == tcols - 1))
    edge = lax.dot_general(
        pick_t.astype(F32).astype(BF),
        mask_ref[...].astype(F32).astype(BF),
        NT,
        preferred_element_type=F32,
    )
    lane_t = lax.broadcasted_iota(jnp.int32, (trows, 128), 1)
    row_t = lax.broadcasted_iota(jnp.int32, (trows, 128), 0)
    spread = (lane_t // TILE == row_t).astype(F32).astype(BF)
    keep = lax.dot_general(edge.astype(BF), spread, NN, preferred_element_type=F32)
    phis = lax.dot_general(pick, phi_ref[...], NT, preferred_element_type=F32)
    phis = jnp.concatenate([phis, jnp.zeros((8, 128 - rows), F32)], axis=1)
    gphi = jnp.zeros((chans, 128), F32)
    for which, src in ((0, sky_ref), (1, cot_ref)):
        both = jnp.concatenate([src[:half], src[half:]], axis=1).reshape(half * 128, width)
        flat = lax.dot_general(pick, both, NT, preferred_element_type=F32)
        for j in range(half):
            strip[which, 8 * j : 8 * j + 8] = flat[:, 128 * j : 128 * j + 128]
        for k in range(4):
            part = strip[which, pl.ds(k, half, stride=8), :]
            col = jnp.concatenate([part, pltpu.roll(part, 64, 1)], axis=0)
            base = (2 * which + k % 2) * chans
            own_ref[k // 2, base : base + chans] = (col * keep[k : k + 1]).astype(BF)
        for j in range(rows // 16):
            block = jnp.transpose(src[:, 16 * j : 16 * j + 16, :], (1, 0, 2))
            for t in range(2):
                low = jnp.broadcast_to(cells[2 * j + t : 2 * j + t + 1], (chans, 128)).astype(BF)
                for n in range(TILE):
                    y = 16 * j + TILE * t + n
                    value = block[TILE * t + n] * low
                    a3[which, y * step : (y + 1) * step] = three_copies(value)
                    if which:
                        gphi = gphi + value.astype(F32) * phi[y : y + 1]
    gphi_ref[...] = gphi
    row = lax.broadcasted_iota(jnp.int32, (16, 128), 0)
    for side, k in ((0, 0), (1, 3)):
        extra = jnp.where(
            row == 0,
            jnp.broadcast_to(phis[k : k + 1], (16, 128)),
            jnp.where(row == 1, jnp.broadcast_to(keep[k : k + 1], (16, 128)), 0.0),
        )
        own_ref[side, 4 * chans : size] = extra.astype(BF)


def three_copies(value):
    return jnp.concatenate([pltpu.roll(value, 1, 1), value, pltpu.roll(value, 127, 1)], axis=0)


def col_kernel(rows, width, count, mine_ref, a_ref, b_ref, sa_ref, sb_ref, own_ref, halo_ref):
    size = a_ref.shape[0]
    tops, bots = received("gy", count, a_ref, b_ref)
    halo_ref[0] = tops
    halo_ref[1] = bots
    chans = (size - 16) // 4
    lane = lane_iota(chans)
    lane16 = lane_iota(16)
    sides = []
    for side in range(2):
        parts = []
        for m in range(4):
            which, k = divmod(m, 2)
            at = k + (width - 2) * side
            col = mine_ref[side, m * chans : (m + 1) * chans]
            for value, where in ((tops, (126, 127)), (bots, (rows, rows + 1))):
                for n in range(2):
                    base = (2 * which + n) * chans
                    cell = value[base : base + chans, at : at + 1]
                    col = jnp.where(lane == where[n], jnp.broadcast_to(cell, col.shape), col)
            parts.append(col)
        at = (width - 1) * side
        extra = mine_ref[side, 4 * chans : size].astype(F32)
        for value, where in ((tops, 127), (bots, rows)):
            cell = value[4 * chans : size].astype(F32)[:, at : at + 1]
            extra = jnp.where(lane16 == where, jnp.broadcast_to(cell, (16, 128)), extra)
        parts.append(extra.astype(BF))
        sides.append(jnp.concatenate(parts, axis=0))
        own_ref[side] = sides[side]
    odd_x = is_odd("gx")
    sa_ref[...] = jnp.where(odd_x, sides[0], sides[1])
    sb_ref[...] = jnp.where(odd_x, sides[1], sides[0])


def silu_parts(pre):
    sigma = 1.0 / (1.0 + jnp.exp(-pre))
    return pre * sigma, sigma * (1.0 + pre * (1.0 - sigma))


def hidden_kernel(
    a3, phi_own, mask_own, halo_ref, w1s_ref, w2ts_ref, cond_ref,
    hid_ref, dpre_ref, acc1, acc2, cacc,
    dz, phix, maskx, ringx, ringg,
):
    rows, width = phi_own.shape
    a3x, a3g = a3.at[0], a3.at[1]
    size = halo_ref.shape[1]
    chans = (size - 16) // 4
    step = 3 * chans
    lane1 = lane_iota(1)
    inside = jnp.where((lane1 == 0) | (lane1 == 127), 0.0, 1.0)
    for k, at in ((0, 0), (1, rows + 1)):
        extra = halo_ref[k, 4 * chans : size].astype(F32)
        phix[at : at + 1] = extra[0:1]
        maskx[at : at + 1] = extra[1:2] * inside
    phix[1 : rows + 1] = phi_own[...]
    maskx[1 : rows + 1] = mask_own[...] * inside
    for which, ring in ((0, ringx), (1, ringg)):
        for k in range(2):
            for n in range(2):
                base = (2 * which + n) * chans
                ring[(2 * k + n) * step : (2 * k + n + 1) * step] = three_copies(
                    halo_ref[k, base : base + chans]
                )

    def window(own, ring, y, count):
        parts = []
        if y < 0:
            parts.append(ring[(y + 2) * step : min(2, y + 2 + count) * step])
        low, high = max(y, 0), min(y + count, rows)
        if low < high:
            parts.append(own[low * step : high * step])
        if y + count > rows:
            low = max(y, rows) - rows
            parts.append(ring[(2 + low) * step : (2 + y + count - rows) * step])
        return parts[0] if len(parts) == 1 else jnp.concatenate(parts, axis=0)

    gain = cond_ref[:, 0:1]
    bias = cond_ref[:, 1:2]
    split = (rows + 2) // 2
    zero = jnp.zeros((chans, 128), BF)
    for y in (-2, -1, rows, rows + 1):
        dz[(y + 2) * chans : (y + 3) * chans] = zero

    def first_pass(it, dphi, dsum):
        y0 = R1 * it - 1

        def both(own, ring):
            pair = [window(own, ring, y0 - 1 + h * split, R1 + 2) for h in range(2)]
            return jnp.concatenate(pair, axis=1)

        pre = lax.dot_general(w1s_ref[...], both(a3x, ringx), NN, preferred_element_type=F32)
        back = lax.dot_general(w2ts_ref[...], both(a3g, ringg), NN, preferred_element_type=F32)
        for h in range(2):
            for r in range(R1):
                row = y0 + h * split + r + 1
                here = (slice(r * chans, (r + 1) * chans), slice(h * 128, h * 128 + 128))
                keep = maskx[row : row + 1]
                act, slope = silu_parts(pre[here] + gain * phix[row : row + 1] + bias)
                base = row * chans
                hid_ref[base : base + chans] = (act * keep).astype(BF)
                value = (back[here] * keep * slope).astype(BF)
                dpre_ref[base : base + chans] = value
                if 1 <= row <= rows:
                    dz[base + chans : base + 2 * chans] = value
                    wide = value.astype(F32)
                    dphi = dphi + wide * phix[row : row + 1]
                    dsum = dsum + wide
        return dphi, dsum

    dphi = jnp.zeros((chans, 128), F32)
    dsum = jnp.zeros((chans, 128), F32)
    for it in range(split // R1):
        dphi, dsum = first_pass(it, dphi, dsum)
    cacc[0] = dphi
    cacc[1] = dsum

    acc1[...] = jnp.zeros_like(acc1)
    acc2[...] = jnp.zeros_like(acc2)

    def rows_of(src, start, size):
        return src[start : start + size]

    def grads_one(it):
        ys = [GROUP1 * it + n - 1 for n in range(GROUP1)]
        acc1[...] += lax.dot_general(
            jnp.concatenate([rows_of(dz, (y + 1) * chans, step) for y in ys], axis=1),
            jnp.concatenate([window(a3x, ringx, y, 1) for y in ys], axis=1),
            NT, preferred_element_type=F32,
        )

    def grads_two(it):
        ys = [GROUP2 * it + n for n in range(GROUP2)]
        acc2[...] += lax.dot_general(
            jnp.concatenate([window(a3g, ringg, y, 1) for y in ys], axis=1),
            jnp.concatenate([rows_of(hid_ref, y * chans, step) for y in ys], axis=1),
            NT, preferred_element_type=F32,
        )

    for it in range((rows + 2) // GROUP1):
        grads_one(it)
    for it in range(rows // GROUP2):
        grads_two(it)


def edge_kernel(
    rows, count, a_ref, b_ref, own_ref, w1c_ref, w2tc_ref, cond_ref,
    acc1, acc2, cacc, gphi_ref,
    hcol_ref, dcol_ref, keep_ref, give_ref, wire,
):
    size = a_ref.shape[0]
    chans = (size - 16) // 4
    step = 3 * chans
    lft, rgt = received("gx", count, a_ref, b_ref)
    own_l, own_r = own_ref[0], own_ref[1]

    def at(value, which, n):
        base = (2 * which + n) * chans
        return value[base : base + chans]

    def columns(which):
        return [at(v, which, n) for v in (lft, own_l, own_r, rgt) for n in range(2)]

    centres = (1, 2, 5, 6)

    def taps_of(cols):
        pieces = []
        for ky in range(3):
            moved = [c if ky == 1 else pltpu.roll(c, (1, 0, 127)[ky], 1) for c in cols]
            for kx in range(3):
                pieces.append(jnp.concatenate([moved[c + kx - 1] for c in centres], axis=1))
        return jnp.concatenate(pieces, axis=0)

    x_taps = taps_of(columns(0))
    g_cols = columns(1)
    extra = [v[4 * chans : size].astype(F32) for v in (lft, own_l, own_r, rgt)]
    phi_c = jnp.concatenate([e[0:1] for e in extra], axis=1)
    mask_c = jnp.concatenate([e[1:2] for e in extra], axis=1)
    pre = lax.dot_general(w1c_ref[...], x_taps, NN, preferred_element_type=F32)
    back = lax.dot_general(w2tc_ref[...], taps_of(g_cols), NN, preferred_element_type=F32)
    act, slope = silu_parts(pre + cond_ref[:, 0:1] * phi_c + cond_ref[:, 1:2])
    hcol = (act * mask_c).astype(BF)
    dcol = (back * mask_c * slope).astype(BF)
    hcol_ref[...] = hcol
    dcol_ref[...] = dcol

    mine = jnp.broadcast_to((lane_iota(1) < rows).astype(F32), (chans, 128)).astype(BF)
    d_own = [dcol[:, 128:256] * mine, dcol[:, 256:384] * mine]
    part1 = lax.dot_general(
        jnp.concatenate(d_own, axis=1), x_taps[:, 128:384], NT, preferred_element_type=F32
    )
    h_cols = [hcol[:, 128 * k : 128 * k + 128] for k in range(4)]
    g_own = {k: g_cols[n] * mine for k, n in ((0, 2), (1, 3), (2, 4), (3, 5))}
    for kx, pairs in (
        (0, ((0, 0), (1, 1))),
        (1, ((0, 1), (3, 2))),
        (2, ((2, 2), (3, 3))),
    ):
        lhs = jnp.concatenate([g_own[g] for g, _ in pairs], axis=1)
        rhs = []
        for ky in range(3):
            moved = [
                h_cols[h] if ky == 1 else pltpu.roll(h_cols[h], (1, 0, 127)[ky], 1)
                for _, h in pairs
            ]
            rhs.append(jnp.concatenate(moved, axis=1))
        part2 = lax.dot_general(
            lhs, jnp.concatenate(rhs, axis=0), NT, preferred_element_type=F32
        )
        low = (2 - kx) * chans
        wide = jnp.concatenate(
            [
                acc1[low : low + chans] + part1[:, kx * step : (kx + 1) * step],
                acc2[low : low + chans] + part2,
            ],
            axis=1,
        )
        wire[low : low + chans] = wide[:, :128]
        wire[step + low : step + low + chans] = wide[:, 128:256]
        if kx == 0:
            tails = []
        tails.insert(0, wide[:, 256 : 2 * step])
    dphi, dsum = cacc[0], cacc[1]
    for d, k in ((d_own[0], 1), (d_own[1], 2)):
        dphi = dphi + d.astype(F32) * extra[k][0:1]
        dsum = dsum + d.astype(F32)
    sums = [jnp.sum(v, axis=1, keepdims=True) for v in (dphi, dsum, gphi_ref[...])]
    base = 3 * tails[0].shape[1]
    place = jnp.maximum(lane_iota(chans) - base, 0)
    which = lax.rem(place, 3)
    wide_sums = [jnp.broadcast_to(v, (chans, 128)) for v in sums]
    coded = jnp.where(which == 0, wide_sums[0], jnp.where(which == 1, *wide_sums[1:]))
    coded = coded * (1.0 + COPY_STEP * (place // 3).astype(F32))
    wire[2 * step : 2 * step + chans] = jnp.concatenate(tails + [coded[:, base:]], axis=1)
    half = wire.shape[0] // 2
    core = lax.rem(lax.axis_index("gy"), 2)
    keep_ref[...] = wire[pl.ds(pl.multiple_of(core * half, 8), half), :]
    give_ref[...] = wire[pl.ds(pl.multiple_of((1 - core) * half, 8), half), :]


def fix_kernel(rows, w2c_ref, w1tc_ref, hcol_ref, dcol_ref, hfix_ref, dfix_ref):
    chans = hcol_ref.shape[0]
    none = jnp.zeros((chans, 128), BF)
    half = chans // 2
    lane = lane_iota(half)
    for weights, field, fix in ((w2c_ref, hcol_ref, hfix_ref), (w1tc_ref, dcol_ref, dfix_ref)):
        f = [field[:, 128 * k : 128 * k + 128] for k in range(4)]
        pieces = []
        for ky in range(3):
            m = [c if ky == 1 else pltpu.roll(c, (1, 0, 127)[ky], 1) for c in f]
            pieces.append(jnp.concatenate([m[0], m[1], none, none], axis=1))
            pieces.append(jnp.concatenate([m[1], none, none, m[2]], axis=1))
            pieces.append(jnp.concatenate([none, none, m[2], m[3]], axis=1))
        fixes = lax.dot_general(
            weights[...], jnp.concatenate(pieces, axis=0), NN, preferred_element_type=F32
        )
        for k in range(4):
            col = fixes[:, 128 * k : 128 * k + 128]
            part = jnp.where(lane < rows, col[:half], pltpu.roll(col[half:], rows, 1))
            high = part.astype(BF).astype(F32)
            fix[pl.ds(k, half, stride=8), :] = high
            fix[pl.ds(4 + k, half, stride=8), :] = part - high


def output_kernel(
    with_phi, src_hbm, phi_ref, mask_ref, mid_ref, fix_ref, weights_ref, cond_ref,
    out_ref, a3, rowbuf, fixbuf, src_ref, sem,
):
    chans, rows, width = src_ref.shape
    step = 3 * chans
    half = chans // 2
    fetch = pltpu.make_async_copy(src_hbm, src_ref, sem)
    fetch.start()
    if with_phi:
        gain = cond_ref[:, 2:3]
    lane8 = lane_iota(8)
    row8 = lax.rem(lax.broadcasted_iota(jnp.int32, (8, 128), 0), 4)
    place = (lane8 == jnp.where(row8 < 2, row8, row8 + (width - 4))).astype(F32).astype(BF)
    for j in range(half):
        got = lax.dot_general(
            fix_ref[8 * j : 8 * j + 8].astype(BF), place, TN, preferred_element_type=F32
        )
        fixbuf[j] = got[:rows]
        fixbuf[j + half] = got[rows:]

    for y in range(rows + 2):
        centre = mid_ref[y * chans : (y + 1) * chans]
        base = y * step
        a3[base : base + chans] = pltpu.roll(centre, 1, 1)
        a3[base + chans : base + 2 * chans] = centre
        a3[base + 2 * chans : base + 3 * chans] = pltpu.roll(centre, 127, 1)

    for it in range(rows // (2 * R2)):
        y0 = R2 * it
        got = lax.dot_general(
            weights_ref[...],
            jnp.concatenate(
                [a3[(y0 + h) * step : (y0 + h + R2 + 2) * step] for h in (0, rows // 2)], axis=1
            ),
            NN, preferred_element_type=F32,
        )
        for h in range(2):
            for r in range(R2):
                y = y0 + h * (rows // 2) + r
                part = got[r * chans : (r + 1) * chans, h * 128 : h * 128 + 128]
                if with_phi:
                    part = part + gain * phi_ref[y : y + 1]
                rowbuf[y] = part

    fetch.wait()
    for j in range(rows // 16):
        here = slice(16 * j, 16 * j + 16)
        keep = mask_ref[here]
        total = jnp.transpose(rowbuf[here], (1, 0, 2)) + fixbuf[:, here, :]
        out_ref[:, here, :] = ((total + src_ref[:, here, :].astype(F32)) * keep[None]).astype(BF)


def unpack_kernel(factor, keep_ref, other_ref, w1_ref, w2_ref, cond_ref, wire):
    chans = w1_ref.shape[2]
    step = 3 * chans
    count = keep_ref.shape[0]
    core = lax.rem(lax.axis_index("gy"), 2)
    wire[pl.ds(pl.multiple_of(core * count, 8), count), :] = keep_ref[...]
    wire[pl.ds(pl.multiple_of((1 - core) * count, 8), count), :] = other_ref[...]
    tail = wire[2 * step : 2 * step + chans] * factor
    rest_w = 2 * step - 256
    for n in range(3):
        low = n * chans
        wide = jnp.concatenate(
            [
                wire[low : low + chans] * factor,
                wire[step + low : step + low + chans] * factor,
                tail[:, n * rest_w : (n + 1) * rest_w],
            ],
            axis=1,
        )
        for k in range(3):
            w1_ref[2 - n, k] = wide[:, k * chans : (k + 1) * chans]
            w2_ref[k, 2 - n] = wide[:, step + k * chans : step + (k + 1) * chans]
    turned = jnp.transpose(tail)[:, :chans]
    copies = (128 - 3 * rest_w) // 3
    total = jnp.zeros((3, chans), F32)
    for j in range(copies):
        at = 3 * (rest_w + j)
        total = total + turned[at : at + 3] * (1.0 / (copies * (1.0 + COPY_STEP * j)))
    cond_ref[...] = total


def limit(mib):
    return pltpu.CompilerParams(vmem_limit_bytes=mib << 20)


def keep_near(value):
    return pltpu.with_memory_space_constraint(value, pltpu.VMEM)


def stacked(block, count):
    chans, taps = block.shape
    step = taps // 3
    rows = []
    for r in range(count):
        parts = [block]
        if r:
            parts.insert(0, jnp.zeros((chans, r * step), BF))
        if r < count - 1:
            parts.append(jnp.zeros((chans, (count - 1 - r) * step), BF))
        rows.append(jnp.concatenate(parts, axis=1))
    return jnp.concatenate(rows, axis=0)


def weight_matrices(
    one, two, vec0, vec1, vec2,
    w1f_ref, w2b_ref, w2f_ref, w1b_ref, w1s_ref, w2bs_ref, w2s_ref, w1bs_ref, cond_ref,
):
    chans = one.shape[2]
    for src, fwd, fwd_s, count, bwd, bwd_s, back in (
        (one, w1f_ref, w1s_ref, R1, w1b_ref, w1bs_ref, R2),
        (two, w2f_ref, w2s_ref, R2, w2b_ref, w2bs_ref, R1),
    ):
        taps = [src[k // 3, k % 3] for k in range(9)]
        plain = jnp.concatenate(taps, axis=1)
        turned = jnp.concatenate(
            [jnp.transpose(t.astype(F32)).astype(BF) for t in taps[::-1]], axis=1
        )
        fwd[...] = plain
        bwd[...] = turned
        fwd_s[...] = stacked(plain, count)
        bwd_s[...] = stacked(turned, back)
    row = lax.broadcasted_iota(jnp.int32, (8, chans), 0)
    table = jnp.zeros((8, chans), F32)
    for k, ref in enumerate((vec0, vec1, vec2)):
        table = jnp.where(row == k, jnp.broadcast_to(ref[...].reshape(1, chans), (8, chans)), table)
    table = jnp.concatenate([table, jnp.zeros((8, 128 - chans), F32)], axis=1)
    table = jnp.concatenate([table, jnp.zeros((120, 128), F32)], axis=0)
    cond_ref[...] = jnp.transpose(table)[:chans]


def build(mesh):
    ny, nx = mesh.shape["gy"], mesh.shape["gx"]
    axes = ("gy", "gx")

    def send(value, move):
        pairs = []
        for a in range(ny):
            for b in range(nx):
                to = move(a, b)
                pairs.append((a * nx + b, to[0] * nx + to[1]))
        return lax.ppermute(value, axes, pairs)

    def swap(first, second, axis):
        def partner(offset):
            def move(a, b):
                v = [a, b]
                v[axis] += 1 if (v[axis] + offset) % 2 == 0 else -1
                if 0 <= v[axis] < (ny, nx)[axis]:
                    return v
                return (a, b ^ 1) if axis == 0 else (a ^ 1, b)

            return move

        return send(first, partner(0)), send(second, partner(1))

    def exchange(value, moves):
        sent = value.astype(BF)
        got = [send(sent, lambda a, b: (a ^ m[0], b ^ m[1])).astype(F32) for m in moves]
        if len(moves) == 1:
            return sent.astype(F32) + got[0]
        both = (moves[0][0] ^ moves[1][0], moves[0][1] ^ moves[1][1])
        far = send(sent, lambda a, b: (a ^ both[0], b ^ both[1])).astype(F32)
        return (sent.astype(F32) + got[0]) + (far + got[1])

    def local(
        sky, lens_phi, cotangent, tile_mask, weight_one, weight_two, cond_one, bias_one, cond_two
    ):
        chans, rows, width = sky.shape
        step = 3 * chans
        size = 4 * chans + 16
        assert 2 * rows == 128 and width == 128
        edge = jax.ShapeDtypeStruct((size, 128), BF)
        edges = jax.ShapeDtypeStruct((2, size, 128), BF)
        hbm = pl.BlockSpec(memory_space=pltpu.HBM)
        far = [
            pltpu.with_memory_space_constraint(v, pltpu.HBM)
            for v in (
                sky, cotangent, lens_phi, tile_mask,
                weight_one, weight_two, cond_one, bias_one, cond_two,
            )
        ]
        vmem = pl.BlockSpec(memory_space=pltpu.VMEM)
        ra, rb = pl.pallas_call(
            row_kernel,
            out_shape=(edge, edge),
            in_specs=[hbm] * 4,
            scratch_shapes=[
                pltpu.VMEM((4, chans, 8, width), BF),
                pltpu.VMEM((2, 16, width), BF),
                pltpu.VMEM(tile_mask.shape, jnp.int32),
                pltpu.SemaphoreType.DMA((7,)),
            ],
            compiler_params=limit(8),
            name="edge_rows",
        )(*far[:4])
        ra, rb = swap(ra, rb, 0)

        flat_w = jax.ShapeDtypeStruct((chans, 3 * step), BF)
        first_w = jax.ShapeDtypeStruct((R1 * chans, (R1 + 2) * step), BF)
        second_w = jax.ShapeDtypeStruct((R2 * chans, (R2 + 2) * step), BF)
        matrices = (
            flat_w, flat_w, flat_w, flat_w, first_w, first_w, second_w, second_w,
            jax.ShapeDtypeStruct((chans, 128), F32),
        )
        flops = 2 * 9 * chans * chans * rows * width
        field = jax.ShapeDtypeStruct((2, rows * step, 128), BF)
        flat = jax.ShapeDtypeStruct(lens_phi.shape, F32)
        a3, mine, gphi, phi_own, mask_own, *matrices = pl.pallas_call(
            prep_kernel,
            out_shape=(field, edges, jax.ShapeDtypeStruct((chans, 128), F32), flat, flat)
            + matrices,
            in_specs=[hbm] * 9,
            scratch_shapes=[pltpu.VMEM((2, 8 * chans // 2, 128), F32)]
            + [pltpu.VMEM(v.shape, v.dtype) for v in far]
            + [pltpu.SemaphoreType.DMA((9,))],
            compiler_params=limit(8),
            cost_estimate=pl.CostEstimate(
                flops=4 * flops, bytes_accessed=8 << 20, transcendentals=0
            ),
            name="prep",
        )(*far)
        w1f, w2b, w2f, w1b, w1s, w2bs, w2s, w1bs, conds = matrices
        ca, cb, own, halo = pl.pallas_call(
            lambda *refs: col_kernel(rows, width, ny, *refs),
            out_shape=(edge, edge, edges, edges),
            compiler_params=limit(8),
            name="edge_cols",
        )(mine, ra, rb)
        ca, cb = swap(ca, cb, 1)

        ring = pltpu.VMEM((4 * step, 128), BF)
        rowwise = pltpu.VMEM((rows + 8, 128), F32)
        inner = jax.ShapeDtypeStruct(((rows + 2) * chans, 128), BF)
        acc = jax.ShapeDtypeStruct((step, step), F32)
        hid, dpre, acc1, acc2, cacc = pl.pallas_call(
            hidden_kernel,
            out_shape=(inner, inner, acc, acc, jax.ShapeDtypeStruct((2, chans, 128), F32)),
            scratch_shapes=[
                pltpu.VMEM(((rows + 4) * chans, 128), BF), rowwise, rowwise, ring, ring,
            ],
            compiler_params=limit(16),
            cost_estimate=pl.CostEstimate(
                flops=8 * flops, bytes_accessed=8 << 20, transcendentals=0
            ),
            name="hidden",
        )(
            keep_near(a3), phi_own, mask_own, halo,
            w1s, w2bs, conds,
        )

        fix = jax.ShapeDtypeStruct((4 * chans, 128), F32)
        count = (2 * step + chans) // 2
        wires = jax.ShapeDtypeStruct((count, 128), F32)
        cols = jax.ShapeDtypeStruct((chans, 512), BF)
        hcol, dcol, keep, give = pl.pallas_call(
            lambda *refs: edge_kernel(rows, nx, *refs),
            out_shape=(cols, cols, wires, wires),
            scratch_shapes=[pltpu.VMEM((2 * count, 128), F32)],
            compiler_params=limit(8),
            name="edge_parts",
        )(ca, cb, own, w1f, w2b, conds, acc1, acc2, cacc, gphi)
        hfix, dfix = pl.pallas_call(
            lambda *refs: fix_kernel(rows, *refs),
            out_shape=(fix, fix),
            compiler_params=limit(8),
            cost_estimate=pl.CostEstimate(
                flops=flops // 2, bytes_accessed=1 << 20, transcendentals=0
            ),
            name="edge_fixes",
        )(w2f, w1b, hcol, dcol)

        def output(with_phi, src, mid, fix, weights, name):
            return pl.pallas_call(
                lambda *refs: output_kernel(with_phi, *refs),
                out_shape=jax.ShapeDtypeStruct(src.shape, BF),
                scratch_shapes=[
                    pltpu.VMEM(((rows + 2) * step, 128), BF),
                    pltpu.VMEM((rows, chans, 128), F32),
                    pltpu.VMEM((chans, rows, 128), F32),
                    pltpu.VMEM(src.shape, BF),
                    pltpu.SemaphoreType.DMA(()),
                ],
                in_specs=[hbm] + [vmem] * 6,
                compiler_params=limit(16),
                cost_estimate=pl.CostEstimate(
                    flops=2 * flops, bytes_accessed=4 << 20, transcendentals=0
                ),
                name=name,
            )(src, phi_own, mask_own, mid, fix, weights, conds)

        moves = [(1 << k, 0) for k in range(1, ny.bit_length() - 1)]
        moves += [(0, 1 << k) for k in range(nx.bit_length() - 1)]
        rounds = [moves[k : k + 2] for k in range(0, len(moves), 2)]
        keep = keep + send(give, lambda a, b: (a ^ 1, b))
        outs = []
        for n, move in enumerate(rounds):
            if n == 0:
                keep, hfix = lax.optimization_barrier((keep, hfix))
                outs.append(output(True, far[0], hid, hfix, w2s, "delensed"))
            if n == len(rounds) - 1:
                keep, dfix = lax.optimization_barrier((keep, dfix))
                outs.append(output(False, far[1], dpre, dfix, w1bs, "grad_input"))
            keep = exchange(keep, move)
            if n in (0, len(rounds) - 1):
                keep, outs[-1] = lax.optimization_barrier((keep, outs[-1]))
        delensed, grad_input = outs
        other = send(keep, lambda a, b: (a ^ 1, b))

        factor = float(1.0 / (rows * ny * width * nx) ** 0.5)
        grads = jax.ShapeDtypeStruct((3, 3, chans, chans), F32)
        grad_w1, grad_w2, grad_cond = pl.pallas_call(
            lambda *refs: unpack_kernel(factor, *refs),
            out_shape=(grads, grads, jax.ShapeDtypeStruct((3, chans), F32)),
            scratch_shapes=[pltpu.VMEM((2 * count, 128), F32)],
            compiler_params=limit(8),
            name="unpack",
        )(keep, other)
        return delensed, grad_input, grad_w1, grad_w2, grad_cond

    return local


def solution(mesh):
    return jax.shard_map(
        build(mesh),
        mesh=mesh,
        in_specs=(
            P(None, "gy", "gx"),
            P("gy", "gx"),
            P(None, "gy", "gx"),
            P("gy", "gx"),
            P(),
            P(),
            P(),
            P(),
            P(),
        ),
        out_specs=(P(None, "gy", "gx"), P(None, "gy", "gx"), P(), P(), P()),
        check_vma=False,
    )
```
